128 devices in a mesh: kv: 16 (over x, y), tp: 8 (over z, core).
Axes of the slice: x: 4, y: 4, z: 4, core: 2. Of those that a mesh axis runs over, the one named last changes fastest.
Arguments:
- activations: bfloat16 [256, 5120], P(('kv', 'tp')), may hold values from -27 to 27
- queries: bfloat16 [256, 5120], P('kv', 'tp'), may hold values from -16 to 16
- tree_cache_keys: bfloat16 [16384, 1024], P('kv', 'tp'), may hold values from -16 to 16
- tree_cache_values: bfloat16 [16384, 1024], P('kv', 'tp'), may hold values from -8 to 8
- parents: int32 [13], replicated, may hold values from 0 to 4, as said below
- node_lengths: int32 [13], replicated, may hold values from 1 to 4096, as said below
- token_leaf: int32 [256], replicated, may hold values from 5 to 12
- out_weight: bfloat16 [5120, 5120], P('tp'), may hold values from -0.078125 to 0.078125
- norm_gain: float32 [5120], replicated, may hold values from 0.5 to 1.5
- gate_weight: bfloat16 [5120, 27648], P(None, ('kv', 'tp')), may hold values from -0.078125 to 0.078125
- up_weight: bfloat16 [5120, 27648], P(None, ('kv', 'tp')), may hold values from -0.078125 to 0.078125
- down_weight: bfloat16 [27648, 5120], P(('kv', 'tp')), may hold values from -0.0390625 to 0.0390625
Outputs:
- output: bfloat16 [256, 5120], P(('kv', 'tp'))
The draws below stay inside these ranges and needn't reach their ends.
Inputs may be any that keep to these rules, and one draw needn't show every extreme that they name: Node 0 is the root, nodes 1 to 4 are tenants, the rest are leaves. parents[0] = 0, every tenant's parent is 0, every leaf's parent is a tenant, and every tenant is the parent of some leaf. `node_lengths`: the root holds exactly 4096 slots, every tenant at most 2048 and one tenant exactly that many, every leaf at most 512 and one leaf exactly that many. The nodes' slots follow one another in node order from slot 0.
All inputs are finite; a program needn't handle non-finite values.
Results may differ from the reference program's by a relative error of at most 0.017.
Values may be sent and summed in bfloat16 or wider, within the bound.
No kernel may reach another device: no remote copies, remote signals or barrier semaphores. Data moves between devices by JAX's collectives and lax.ppermute only.
A program may use at most 128 MiB of HBM per device.

```python
import math
import jax
import jax.numpy as jnp
from jax import lax

D = 5120
QUERY_HEADS = 40
KEY_VALUE_HEADS = 8
HEAD_WIDTH = 128
FF = 27648
TENANTS = 4
TOKENS = 256
KEY_SLOTS = 16384
NODES = 13
NODE_MOST = 4096
LEAF_MOST = 512


def aligned_layout(key):
    sign_vector = jnp.sign(jax.random.normal(jax.random.fold_in(key, 4242), (HEAD_WIDTH,), jnp.float32))
    sign_vector = jnp.where(sign_vector == 0, 1.0, sign_vector)
    amplitude = math.sqrt(230.0 / math.sqrt(HEAD_WIDTH))
    return amplitude * sign_vector


def base_entry(key, shape):
    return jnp.clip(1.5 * jax.random.normal(key, shape, jnp.float32), -6.0, 6.0)


def draw_queries(key, part):
    values_entry = base_entry(jax.random.fold_in(key, 11), (TOKENS, QUERY_HEADS * HEAD_WIDTH))
    row_ids = jnp.arange(TOKENS)
    strength = 0.8 + 0.1 * (row_ids % 3).astype(jnp.float32)
    chosen = row_ids % 97 == 3
    layout = jnp.tile(aligned_layout(key), QUERY_HEADS)
    values_entry = jnp.where(chosen[:, None], strength[:, None] * layout[None, :], values_entry)
    return values_entry.astype(jnp.bfloat16)


def draw_tree_cache_keys(key, part):
    values_entry = base_entry(jax.random.fold_in(key, 12), (KEY_SLOTS, KEY_VALUE_HEADS * HEAD_WIDTH))
    row_ids = jnp.arange(KEY_SLOTS)
    layout = jnp.tile(aligned_layout(key), KEY_VALUE_HEADS)
    factor = jnp.where(row_ids == 0, 1.0, 0.99)
    values_entry = jnp.where((row_ids < 2)[:, None], factor[:, None] * layout[None, :], values_entry)
    return values_entry.astype(jnp.bfloat16)


def draw_activations(key, part):
    row_scale = jnp.exp(jax.random.uniform(jax.random.fold_in(key, 21), (TOKENS, 1), jnp.float32, math.log(0.3), math.log(3.0)))
    column_scale = jnp.exp(jax.random.uniform(jax.random.fold_in(key, 22), (1, D), jnp.float32, math.log(0.3), math.log(3.0)))
    values_entry = jnp.clip(jax.random.normal(jax.random.fold_in(key, 23), (TOKENS, D), jnp.float32), -3.0, 3.0)
    return (values_entry * row_scale * column_scale).astype(jnp.bfloat16)


def draw_parents(key, part):
    node_ids = jnp.arange(NODES, dtype=jnp.int32)
    picked = jax.random.randint(jax.random.fold_in(key, 31), (NODES,), 1, TENANTS + 1).astype(jnp.int32)
    leaf_rank = node_ids - 1 - TENANTS
    leaf_parent = jnp.where(leaf_rank < TENANTS, 1 + leaf_rank, picked)
    return jnp.where(node_ids <= TENANTS, 0, leaf_parent).astype(jnp.int32)


def draw_node_lengths(key, part):
    node_ids = jnp.arange(NODES, dtype=jnp.int32)
    tenant_sizes = jax.random.randint(jax.random.fold_in(key, 41), (NODES,), NODE_MOST // 8, NODE_MOST // 2 + 1).astype(jnp.int32)
    leaf_sizes = jax.random.randint(jax.random.fold_in(key, 42), (NODES,), 1, LEAF_MOST + 1).astype(jnp.int32)
    tenant_full = jax.random.randint(jax.random.fold_in(key, 43), (), 1, TENANTS + 1)
    leaf_full = jax.random.randint(jax.random.fold_in(key, 44), (), TENANTS + 1, NODES)
    tenant_sizes = jnp.where(node_ids == tenant_full, NODE_MOST // 2, tenant_sizes)
    leaf_sizes = jnp.where(node_ids == leaf_full, LEAF_MOST, leaf_sizes)
    return jnp.where(node_ids == 0, NODE_MOST, jnp.where(node_ids <= TENANTS, tenant_sizes, leaf_sizes)).astype(jnp.int32)


def place_ends(entries, own_key, smallest, largest):
    dims = entries.shape
    place = [jax.random.randint(jax.random.fold_in(own_key, axis), (), 0, dims[axis]) for axis in range(len(dims))]
    entries = entries.at[tuple(place)].set(smallest)
    longest = dims.index(max(dims))
    place[longest] = (place[longest] + 1) % dims[longest]
    return entries.at[tuple(place)].set(largest)


def level_of(rng, extent, split, least, high):
    gain, own = 1.0, jax.random.fold_in(rng, 6)
    for dim, blocks in split:
        draws = jnp.exp(jax.random.uniform(jax.random.fold_in(own, dim), (blocks,), jnp.float32, least / len(split), high / len(split)))
        gain = gain * jnp.repeat(draws, extent[dim] // blocks).reshape([-1 if axis == dim else 1 for axis in range(len(extent))])
    return gain


def centred(own_key, extent, spread, bound, pieces=(), held_as=jnp.bfloat16):
    array = jax.random.normal(own_key, extent, jnp.float32) * spread
    if len(pieces) > 0:
        array = level_of(own_key, extent, pieces, -0.22, 0.18) * array
    return jnp.clip(array, min=-bound, max=bound).astype(held_as)


def setup_inputs(seed: int = 0) -> dict:
    splits = jax.random.split(jax.random.key(seed), 13)
    activations = draw_activations(jax.random.fold_in(splits[12], 71), 0)
    queries = draw_queries(jax.random.fold_in(splits[12], 71), 0)
    tree_cache_keys = draw_tree_cache_keys(jax.random.fold_in(splits[12], 71), 0)
    tree_cache_values = centred(splits[3], (KEY_SLOTS, KEY_VALUE_HEADS * HEAD_WIDTH), 2.0, 8.0, ((0, 16), (1, 8)))
    parents = draw_parents(jax.random.fold_in(splits[12], 71), 0)
    node_lengths = draw_node_lengths(jax.random.fold_in(splits[12], 71), 0)
    token_leaf = place_ends(jax.random.randint(splits[6], (TOKENS,), TENANTS + 1, NODES), jax.random.fold_in(splits[6], 1), TENANTS + 1, NODES - 1).astype(jnp.int32)
    out_weight = centred(splits[7], (QUERY_HEADS * HEAD_WIDTH, D), (QUERY_HEADS * HEAD_WIDTH) ** -0.5, 0.078125, ((0, 8),))
    norm_gain = jnp.clip(1.0 + 0.1 * jax.random.normal(splits[8], (D,), jnp.float32), 0.5, 1.5)
    gate_weight = centred(splits[9], (D, FF), D ** -0.5, 0.078125, ((1, 128),))
    up_weight = centred(splits[10], (D, FF), D ** -0.5, 0.078125, ((1, 128),))
    down_weight = centred(splits[11], (FF, D), FF ** -0.5, 0.0390625, ((0, 128),))
    return {"activations": activations, "queries": queries, "tree_cache_keys": tree_cache_keys, "tree_cache_values": tree_cache_values, "parents": parents, "node_lengths": node_lengths, "token_leaf": token_leaf, "out_weight": out_weight, "norm_gain": norm_gain, "gate_weight": gate_weight, "up_weight": up_weight, "down_weight": down_weight}


LOWEST = -1e+30
EPSILON = 1e-06

def slot_owner(node_lengths, slot_total):
    node_ends = jnp.cumsum(node_lengths).astype(jnp.int32)
    node_starts = (node_ends - node_lengths).astype(jnp.int32)
    slot_ids = jnp.arange(slot_total, dtype=jnp.int32)
    inside = (slot_ids[:, None] >= node_starts[None, :]) & (slot_ids[:, None] < node_ends[None, :])
    labels = jnp.arange(node_lengths.shape[0], dtype=jnp.int32)
    holder = lax.optimization_barrier(jnp.sum(jnp.where(inside, labels[None, :], 0), axis=1)).astype(jnp.int32)
    return jnp.where(jnp.any(inside, axis=1), holder, -1).astype(jnp.int32)

def parent_of(node_ids, parents):
    labels = jnp.arange(parents.shape[0], dtype=jnp.int32)
    return lax.optimization_barrier(jnp.sum(jnp.where(node_ids[:, None] == labels[None, :], parents[None, :], 0), axis=1)).astype(jnp.int32)

def reference(activations, queries, tree_cache_keys, tree_cache_values, parents, node_lengths, token_leaf, out_weight, norm_gain, gate_weight, up_weight, down_weight):
    heads_per_group = QUERY_HEADS // KEY_VALUE_HEADS
    slot_node = slot_owner(node_lengths, KEY_SLOTS)
    tenant = parent_of(token_leaf, parents)
    block_length = math.gcd(TOKENS, 128)
    count_of_blocks = TOKENS // block_length
    score_scale = 1.0 / math.sqrt(HEAD_WIDTH)
    query_head_rows = queries.reshape(count_of_blocks, block_length, KEY_VALUE_HEADS, heads_per_group, HEAD_WIDTH).transpose(2, 0, 1, 3, 4)
    key_head_rows = tree_cache_keys.reshape(KEY_SLOTS, KEY_VALUE_HEADS, HEAD_WIDTH).transpose(1, 0, 2)
    value_head_rows = tree_cache_values.reshape(KEY_SLOTS, KEY_VALUE_HEADS, HEAD_WIDTH).transpose(1, 0, 2)
    leaf_blocks = token_leaf.reshape(count_of_blocks, block_length)
    tenant_blocks = tenant.reshape(count_of_blocks, block_length)

    def one_head(packed):
        query_head, key_rows, value_rows = packed
        keys_wide = key_rows.astype(jnp.float32)
        values_wide = value_rows.astype(jnp.float32)

        def one_block(blocked):
            query_block, leaf_ids, tenant_ids = blocked
            scores = jnp.einsum('tgd,sd->tgs', query_block.astype(jnp.float32), keys_wide) * score_scale
            allowed = (slot_node[None, :] == 0) | (slot_node[None, :] == tenant_ids[:, None]) | (slot_node[None, :] == leaf_ids[:, None])
            allowed = allowed[:, None, :]
            highest = lax.optimization_barrier(jnp.max(jnp.where(allowed, scores, LOWEST), axis=2, keepdims=True))
            weights = jnp.exp(jnp.where(allowed, scores - highest, -jnp.inf))
            denominator = lax.optimization_barrier(jnp.sum(weights, axis=2))
            rounded = lax.optimization_barrier(weights.astype(jnp.bfloat16)).astype(jnp.float32)
            weighted = jnp.einsum('tgs,sd->tgd', rounded, values_wide)
            return (weighted / denominator[..., None]).astype(jnp.bfloat16)
        return lax.map(one_block, (query_head, leaf_blocks, tenant_blocks))
    context = lax.map(one_head, (query_head_rows, key_head_rows, value_head_rows))
    context = context.transpose(1, 2, 0, 3, 4).reshape(TOKENS, QUERY_HEADS * HEAD_WIDTH)
    attended = jnp.dot(context, out_weight, preferred_element_type=jnp.float32)
    residual = (activations.astype(jnp.float32) + attended).astype(jnp.bfloat16)
    widened = residual.astype(jnp.float32)
    normed = (widened * lax.rsqrt(lax.optimization_barrier(jnp.mean(widened * widened, axis=1, keepdims=True)) + EPSILON) * norm_gain).astype(jnp.bfloat16)
    gate_proj = jnp.dot(normed, gate_weight, preferred_element_type=jnp.float32)
    up_proj = jnp.dot(normed, up_weight, preferred_element_type=jnp.float32)
    hidden = (jax.nn.silu(gate_proj) * up_proj).astype(jnp.bfloat16)
    down_proj = jnp.dot(hidden, down_weight, preferred_element_type=jnp.float32)
    return (widened + down_proj).astype(jnp.bfloat16)
```

```python
import math

import jax
import jax.numpy as jnp
from jax import lax
from jax.sharding import PartitionSpec as P

QUERY_HEADS = 40
KEY_VALUE_HEADS = 8
HEAD_WIDTH = 128
GROUP = QUERY_HEADS // KEY_VALUE_HEADS
LOWEST = -1e30
EPSILON = 1e-06
BF = jnp.bfloat16
F32 = jnp.float32


def move_x(value, k):
    pairs = [(x * 4 + y, (x + k) % 4 * 4 + y) for x in range(4) for y in range(4)]
    return lax.ppermute(value, "kv", pairs)


def move_y(value, k):
    pairs = [(x * 4 + y, x * 4 + (y + k) % 4) for x in range(4) for y in range(4)]
    return lax.ppermute(value, "kv", pairs)


def move_z(value, k):
    pairs = [(z * 2 + c, (z + k) % 4 * 2 + c) for z in range(4) for c in range(2)]
    return lax.ppermute(value, "tp", pairs)


def move_core(value):
    return lax.ppermute(value, "tp", [(i, i ^ 1) for i in range(8)])


def spread(value, move):
    return jnp.concatenate([value] + [move(value, k) for k in (1, 2, 3)], axis=0)


def collect(value, move):
    rows = value.shape[0] // 4
    sent = [move(value[k * rows : (k + 1) * rows].astype(BF), -k) for k in (1, 2, 3)]
    total = value[:rows].astype(F32)
    for part in sent:
        total = total + part.astype(F32)
    return total


def slot_owner(node_lengths, first_slot, slot_total):
    node_ends = jnp.cumsum(node_lengths)
    node_starts = node_ends - node_lengths
    slot_ids = first_slot + jnp.arange(slot_total, dtype=jnp.int32)
    inside = (slot_ids[:, None] >= node_starts[None, :]) & (slot_ids[:, None] < node_ends[None, :])
    labels = jnp.arange(node_lengths.shape[0], dtype=jnp.int32)
    holder = jnp.sum(jnp.where(inside, labels[None, :], 0), axis=1)
    return jnp.where(jnp.any(inside, axis=1), holder, -1)


def parent_of(node_ids, parents):
    labels = jnp.arange(parents.shape[0], dtype=jnp.int32)
    return jnp.sum(jnp.where(node_ids[:, None] == labels[None, :], parents[None, :], 0), axis=1)


def pack(o, m, l):
    n = o.shape[0]
    high = l.astype(BF)
    low = (l - high.astype(F32)).astype(BF)
    stats = jnp.concatenate(
        [m.astype(BF), high, low, jnp.zeros((n, 128 - 3 * GROUP), BF)], axis=1
    )
    return jnp.concatenate([o.astype(BF).reshape(n, GROUP * HEAD_WIDTH), stats], axis=1)


def unpack(packed):
    n = packed.shape[0]
    o = packed[:, : GROUP * HEAD_WIDTH].astype(F32).reshape(n, GROUP, HEAD_WIDTH)
    s = packed[:, GROUP * HEAD_WIDTH :].astype(F32)
    return o, s[:, :GROUP], s[:, GROUP : 2 * GROUP] + s[:, 2 * GROUP : 3 * GROUP]


def merge(parts):
    parts = [unpack(p) for p in parts]
    top = parts[0][1]
    for p in parts[1:]:
        top = jnp.maximum(top, p[1])
    o, l = 0.0, 0.0
    for p in parts:
        scale = jnp.exp(p[1] - top)
        o = o + p[0] * scale[..., None]
        l = l + p[2] * scale
    return o, top, l


def collect_softmax(packed, move):
    rows = packed.shape[0] // 4
    blocks = [packed[k * rows : (k + 1) * rows] for k in range(4)]
    return merge([blocks[0]] + [move(blocks[k], -k) for k in (1, 2, 3)])


def local(
    activations,
    queries,
    keys,
    values,
    parents,
    node_lengths,
    token_leaf,
    out_weight,
    norm_gain,
    gate_weight,
    up_weight,
    down_weight,
):
    scale = 1.0 / math.sqrt(HEAD_WIDTH)
    kv = lax.axis_index("kv")
    tp = lax.axis_index("tp")
    x, y, z, c = kv // 4, kv % 4, tp // 2, tp % 2
    slot_total = keys.shape[0]

    i16 = jnp.arange(16, dtype=jnp.int32)
    row_order = (z + 4 - i16 // 2 % 4) % 4 * 4 + (c ^ (i16 // 8)) * 2 + i16 % 2
    pick = (row_order[:, None] == i16[None, :])
    block_order = (x + 4 - i16 // 4) % 4 * 4 + (y + 4 - i16 % 4) % 4
    tokens = (block_order[:, None] * 16 + row_order[None, :]).reshape(256)
    leaf = jnp.sum(
        jnp.where(tokens[:, None] == jnp.arange(256, dtype=jnp.int32)[None, :], token_leaf[None, :], 0), axis=1
    )
    tenant = parent_of(leaf, parents)
    slot_node = slot_owner(node_lengths, kv * slot_total, slot_total)

    q = jnp.dot(pick.astype(BF), queries, preferred_element_type=F32).astype(BF)
    q = spread(spread(q, move_y), move_x)
    q = q.reshape(256, GROUP, HEAD_WIDTH)
    scores = jnp.einsum("tgd,sd->tgs", q, keys, preferred_element_type=F32) * scale
    allowed = (
        (slot_node[None, :] == 0)
        | (slot_node[None, :] == tenant[:, None])
        | (slot_node[None, :] == leaf[:, None])
    )[:, None, :]
    top = jnp.max(jnp.where(allowed, scores, LOWEST), axis=2)
    top = lax.reduce_precision(top, 8, 7)
    weights = jnp.exp(jnp.where(allowed, scores - top[..., None], -jnp.inf))
    mass = jnp.sum(weights, axis=2)
    weighted = jnp.einsum("tgs,sd->tgd", weights.astype(BF), values, preferred_element_type=F32)

    packed = pack(weighted, top, mass)
    packed = pack(*collect_softmax(packed, move_x))
    o, top, mass = collect_softmax(packed, move_y)
    context = (o / mass[..., None]).astype(BF).reshape(16, GROUP * HEAD_WIDTH)

    attended = jnp.dot(context, out_weight, preferred_element_type=F32)
    attended = attended[:8] + move_core(attended[8:].astype(BF)).astype(F32)
    attended = collect(attended, move_z)
    residual = (activations.astype(F32) + attended).astype(BF)
    widened = residual.astype(F32)
    normed = (
        widened
        * lax.rsqrt(jnp.mean(widened * widened, axis=1, keepdims=True) + EPSILON)
        * norm_gain
    ).astype(BF)

    rows = spread(spread(spread(normed, move_z), move_y), move_x)
    rows = jnp.concatenate([rows, move_core(rows)], axis=0)
    gate = jnp.dot(rows, gate_weight, preferred_element_type=F32)
    up = jnp.dot(rows, up_weight, preferred_element_type=F32)
    hidden = (jax.nn.silu(gate) * up).astype(BF)
    mixed = jnp.dot(hidden, down_weight, preferred_element_type=F32)
    mixed = mixed[:128] + move_core(mixed[128:].astype(BF)).astype(F32)
    mixed = collect(collect(collect(mixed, move_x), move_y), move_z)
    return (widened + mixed).astype(BF)


def solution(mesh):
    return jax.shard_map(
        local,
        mesh=mesh,
        in_specs=(
            P(("kv", "tp"), None),
            P("kv", "tp"),
            P("kv", "tp"),
            P("kv", "tp"),
            P(),
            P(),
            P(),
            P("tp", None),
            P(),
            P(None, ("kv", "tp")),
            P(None, ("kv", "tp")),
            P(("kv", "tp"), None),
        ),
        out_specs=P(("kv", "tp"), None),
        check_vma=False,
    )
```

```python
import functools
import math

import jax
import jax.numpy as jnp
from jax import lax
from jax.experimental import pallas as pl
from jax.experimental.pallas import tpu as pltpu
from jax.sharding import PartitionSpec as P

QUERY_HEADS = 40
KEY_VALUE_HEADS = 8
HEAD_WIDTH = 128
GROUP = QUERY_HEADS // KEY_VALUE_HEADS
LOWEST = -(2.0**100)
SCALE = 1.0 / math.sqrt(HEAD_WIDTH)
EPSILON = 1e-06
BF = jnp.bfloat16
F32 = jnp.float32
D = 5120
VM = pltpu.VMEM
SM = pltpu.SMEM


def call(kernel, out_shape, in_spaces, scratch=(), limit=48 << 20, **kw):
    outs = out_shape if isinstance(out_shape, (list, tuple)) else [out_shape]
    specs = [pl.BlockSpec(memory_space=VM) for _ in outs]
    return pl.pallas_call(
        kernel,
        out_shape=out_shape,
        in_specs=[pl.BlockSpec(memory_space=s) for s in in_spaces],
        out_specs=specs if isinstance(out_shape, (list, tuple)) else specs[0],
        scratch_shapes=list(scratch),
        compiler_params=pltpu.CompilerParams(vmem_limit_bytes=limit),
        **kw,
    )


def nt(a, b):
    return lax.dot_general(a, b, (((1,), (1,)), ((), ())), preferred_element_type=F32)


def mm(a, b):
    return lax.dot_general(a, b, (((1,), (0,)), ((), ())), preferred_element_type=F32)


def attend_kernel(lengths, parents, first, leaf, q, keys, values, out, starts):
    nodes = lengths.shape[0]
    slots = keys.shape[0]
    tokens = q.shape[0]
    running = jnp.int32(0)
    for n in range(nodes):
        starts[n] = running
        running = running + lengths[n]
    lane = lax.broadcasted_iota(jnp.int32, (1, 128), 1)
    zero = jnp.zeros((1, 128), jnp.int32)
    own_lo, own_hi, up_lo, up_hi = zero, zero, zero, zero
    for n in range(nodes):
        lo = starts[n]
        up = parents[n]
        here = lane == n
        own_lo = jnp.where(here, lo, own_lo)
        own_hi = jnp.where(here, lo + lengths[n], own_hi)
        up_lo = jnp.where(here, starts[up], up_lo)
        up_hi = jnp.where(here, starts[up] + lengths[up], up_hi)
    slot = first[0] + lax.broadcasted_iota(jnp.int32, (slots, 128), 0)
    seen = (
        (slot < lengths[0])
        | ((slot >= own_lo) & (slot < own_hi))
        | ((slot >= up_lo) & (slot < up_hi))
    )
    bias = jnp.where(seen, 0.0, LOWEST).astype(BF)
    node = lax.broadcasted_iota(jnp.int32, (128, tokens), 0)
    onehot = jnp.where(node == leaf[...], 1.0, 0.0).astype(F32).T.astype(BF)
    keys_wide = jnp.concatenate([keys[...], bias], axis=1)

    lane_t = lax.broadcasted_iota(jnp.int32, (tokens, 128), 1)
    stats = jnp.zeros((tokens, 128), F32)
    for g in range(GROUP):
        cols = pl.ds(g * HEAD_WIDTH, HEAD_WIDTH)
        q_wide = jnp.concatenate([q[:, cols], onehot], axis=1)
        scores = nt(q_wide, keys_wide)
        top = jnp.max(scores, axis=1, keepdims=True).astype(BF).astype(F32)
        weights = jnp.exp((scores - top) * SCALE)
        mass = jnp.sum(weights, axis=1, keepdims=True)
        out[:, cols] = mm(weights.astype(BF), values[...]).astype(BF)
        high = mass.astype(BF).astype(F32)
        stats = jnp.where(lane_t == g, top, stats)
        stats = jnp.where(lane_t == GROUP + g, high, stats)
        stats = jnp.where(lane_t == 2 * GROUP + g, mass - high, stats)
    out[:, GROUP * HEAD_WIDTH :] = stats.astype(BF)


def project_kernel(core, parts, weight, own, other):
    sources = parts.shape[0]
    width = GROUP * HEAD_WIDTH
    stats = [parts[s, :, width:].astype(F32) for s in range(sources)]
    top = stats[0]
    for s in stats[1:]:
        top = jnp.maximum(top, s)
    scales = [jnp.exp((s - top) * SCALE) for s in stats]
    heads = []
    for g in range(GROUP):
        total = jnp.zeros((16, HEAD_WIDTH), F32)
        mass = jnp.zeros((16, 1), F32)
        for s in range(sources):
            scale = scales[s][:, g : g + 1]
            part = parts[s, :, g * HEAD_WIDTH : (g + 1) * HEAD_WIDTH].astype(F32)
            total = total + part * scale
            low = stats[s][:, GROUP + g : GROUP + g + 1] + stats[s][:, 2 * GROUP + g : 2 * GROUP + g + 1]
            mass = mass + low * scale
        heads.append((total / mass).astype(BF))
    context = jnp.concatenate(heads, axis=1)
    row = lax.broadcasted_iota(jnp.int32, (16, 16), 0)
    col = lax.broadcasted_iota(jnp.int32, (16, 16), 1)
    half = jnp.where(row < 8, core[0], 1 - core[0])
    source = (row % 8) // 2 * 4 + half * 2 + row % 2
    pick = jnp.where(col == source, 1.0, 0.0).astype(BF)
    context = mm(pick, context).astype(BF)
    result = mm(context, weight[...])
    own[...] = result[:8]
    other[...] = result[8:].astype(BF)


def hidden_of(rows, gate, up):
    g = nt(rows, gate)
    u = nt(rows, up)
    return (g / (1.0 + jnp.exp(-g)) * u).astype(BF)


def hidden_kernel(rows, gate, up, out):
    out[...] = hidden_of(rows[...], gate[...], up[...])


def mlp_kernel(rows, gate, up, down, out):
    out[...] = mm(hidden_of(rows[...], gate[...], up[...]), down[...]).astype(out.dtype)


def down_kernel(hidden, down, out):
    out[...] = mm(hidden[...], down[...]).astype(out.dtype)


def move_z(value, k):
    pairs = [(z * 2 + c, (z + k) % 4 * 2 + c) for z in range(4) for c in range(2)]
    return lax.ppermute(value, "tp", pairs)


def move_core(value):
    return lax.ppermute(value, "tp", [(i, i ^ 1) for i in range(8)])


def local(
    activations,
    queries,
    keys,
    values,
    parents,
    node_lengths,
    token_leaf,
    out_weight,
    norm_gain,
    gate_weight,
    up_weight,
    down_weight,
):
    kv = lax.axis_index("kv")
    tp = lax.axis_index("tp")
    z, c = tp // 2, tp % 2
    slots = keys.shape[0]
    gate_t, up_t = gate_weight.T, up_weight.T
    shape = jax.ShapeDtypeStruct

    q = lax.all_to_all(jnp.broadcast_to(queries[None], (16, 16, 640)), "kv", 0, 0)
    packed = call(
        attend_kernel,
        shape((256, 768), BF),
        [SM, SM, SM, VM, VM, VM, VM],
        [pltpu.SMEM((16,), jnp.int32)],
    )(node_lengths, parents, (kv * slots)[None], token_leaf[None, :], q.reshape(256, 640), keys, values)
    parts = lax.all_to_all(packed.reshape(16, 16, 768), "kv", 0, 0)
    own, other = call(project_kernel, [shape((8, D), F32), shape((8, D), BF)], [SM, VM, VM])(
        c[None], parts, out_weight
    )

    mine = (jnp.arange(8) // 2 == z)[:, None]
    act = jnp.where(mine, jnp.tile(activations, (4, 1)), 0).astype(F32)
    attended = own + move_core(other).astype(F32) + act
    sent = attended.astype(BF)
    for part in [move_z(sent, k) for k in (1, 3, 2)]:
        attended = attended + part.astype(F32)
    residual = attended.astype(BF)
    widened = residual.astype(F32)
    normed = (
        widened
        * lax.rsqrt(jnp.mean(widened * widened, axis=1, keepdims=True) + EPSILON)
        * norm_gain
    ).astype(BF)

    rows = lax.all_to_all(jnp.broadcast_to(normed[None], (16, 8, D)), "kv", 0, 0).reshape(128, D)
    rows_other = move_core(rows)
    hidden = call(hidden_kernel, shape((128, 216), BF), [VM, VM, VM])(rows, gate_t, up_t)
    y_other = call(mlp_kernel, shape((128, D), BF), [VM, VM, VM, VM])(rows_other, gate_t, up_t, down_weight)
    back = move_core(y_other)
    y_own = call(down_kernel, shape((128, D), F32), [VM, VM])(hidden, down_weight)
    mixed = (y_own + back.astype(F32)).astype(BF).reshape(64, 2, D)
    groups = [[i for i in range(128) if i % 2 == k] for k in range(2)]
    mixed = lax.all_to_all(mixed, ("kv", "tp"), 0, 0, axis_index_groups=groups)
    final = lax.dynamic_slice_in_dim(widened, z * 2, 2, 0) + jnp.sum(mixed.astype(F32), axis=0)
    return final.astype(BF)


def solution(mesh):
    return jax.shard_map(
        local,
        mesh=mesh,
        in_specs=(
            P(("kv", "tp"), None),
            P("kv", "tp"),
            P("kv", "tp"),
            P("kv", "tp"),
            P(),
            P(),
            P(),
            P("tp", None),
            P(),
            P(None, ("kv", "tp")),
            P(None, ("kv", "tp")),
            P(("kv", "tp"), None),
        ),
        out_specs=P(("kv", "tp"), None),
        check_vma=False,
    )
```

```python
import functools
import math

import jax
import jax.numpy as jnp
from jax import lax
from jax.experimental import pallas as pl
from jax.experimental.pallas import tpu as pltpu
from jax.sharding import PartitionSpec as P

QUERY_HEADS = 40
KEY_VALUE_HEADS = 8
HEAD_WIDTH = 128
GROUP = QUERY_HEADS // KEY_VALUE_HEADS
LOWEST = -(2.0**100)
SCALE = 1.0 / math.sqrt(HEAD_WIDTH)
EPSILON = 1e-06
BF = jnp.bfloat16
F32 = jnp.float32
D = 5120
VM = pltpu.VMEM
SM = pltpu.SMEM


def call(kernel, out_shape, in_spaces, scratch=(), limit=12 << 20, **kw):
    outs = out_shape if isinstance(out_shape, (list, tuple)) else [out_shape]
    specs = [pl.BlockSpec(memory_space=VM) for _ in outs]
    return pl.pallas_call(
        kernel,
        out_shape=out_shape,
        in_specs=[pl.BlockSpec(memory_space=s) for s in in_spaces],
        out_specs=specs if isinstance(out_shape, (list, tuple)) else specs[0],
        scratch_shapes=list(scratch),
        compiler_params=pltpu.CompilerParams(vmem_limit_bytes=limit),
        **kw,
    )


def nt(a, b):
    return lax.dot_general(a, b, (((1,), (1,)), ((), ())), preferred_element_type=F32)


def mm(a, b):
    return lax.dot_general(a, b, (((1,), (0,)), ((), ())), preferred_element_type=F32)


def prepare_kernel(lengths, parents, first, leaf, keys, values, keys_wide, values_out, onehot, starts):
    nodes = lengths.shape[0]
    slots = keys.shape[0]
    tokens = leaf.shape[1]
    running = jnp.int32(0)
    for n in range(nodes):
        starts[n] = running
        running = running + lengths[n]
    lane = lax.broadcasted_iota(jnp.int32, (1, 128), 1)
    zero = jnp.zeros((1, 128), jnp.int32)
    own_lo, own_hi, up_lo, up_hi = zero, zero, zero, zero
    for n in range(nodes):
        lo = starts[n]
        up = parents[n]
        here = lane == n
        own_lo = jnp.where(here, lo, own_lo)
        own_hi = jnp.where(here, lo + lengths[n], own_hi)
        up_lo = jnp.where(here, starts[up], up_lo)
        up_hi = jnp.where(here, starts[up] + lengths[up], up_hi)
    slot = first[0] + lax.broadcasted_iota(jnp.int32, (slots, 128), 0)
    seen = (
        (slot < lengths[0])
        | ((slot >= own_lo) & (slot < own_hi))
        | ((slot >= up_lo) & (slot < up_hi))
    )
    keys_wide[:, :HEAD_WIDTH] = keys[...]
    keys_wide[:, HEAD_WIDTH:] = jnp.where(seen, 0.0, LOWEST).astype(BF)
    values_out[...] = values[...]
    node = lax.broadcasted_iota(jnp.int32, (128, tokens), 0)
    onehot[...] = jnp.where(node == leaf[...], 1.0, 0.0).astype(F32).T.astype(BF)


def attend_kernel(q, keys_wide, values, onehot, out):
    tokens = q.shape[0]
    lane_t = lax.broadcasted_iota(jnp.int32, (tokens, 128), 1)
    stats = jnp.zeros((tokens, 128), F32)
    for g in range(GROUP):
        cols = pl.ds(g * HEAD_WIDTH, HEAD_WIDTH)
        q_wide = jnp.concatenate([q[:, cols], onehot[...]], axis=1)
        scores = nt(q_wide, keys_wide[...])
        top = jnp.max(scores, axis=1, keepdims=True).astype(BF).astype(F32)
        weights = jnp.exp((scores - top) * SCALE)
        mass = jnp.sum(weights, axis=1, keepdims=True)
        out[:, cols] = mm(weights.astype(BF), values[...]).astype(BF)
        high = mass.astype(BF).astype(F32)
        stats = jnp.where(lane_t == g, top, stats)
        stats = jnp.where(lane_t == GROUP + g, high, stats)
        stats = jnp.where(lane_t == 2 * GROUP + g, mass - high, stats)
    out[:, GROUP * HEAD_WIDTH :] = stats.astype(BF)


def project_kernel(core, parts, weight_far, own, other, weight, sem):
    copy = pltpu.make_async_copy(weight_far, weight, sem)
    copy.start()
    sources = parts.shape[0]
    width = GROUP * HEAD_WIDTH
    stats = [parts[s, :, width:].astype(F32) for s in range(sources)]
    top = stats[0]
    for s in stats[1:]:
        top = jnp.maximum(top, s)
    scales = [jnp.exp((s - top) * SCALE) for s in stats]
    heads = []
    for g in range(GROUP):
        total = jnp.zeros((16, HEAD_WIDTH), F32)
        mass = jnp.zeros((16, 1), F32)
        for s in range(sources):
            scale = scales[s][:, g : g + 1]
            part = parts[s, :, g * HEAD_WIDTH : (g + 1) * HEAD_WIDTH].astype(F32)
            total = total + part * scale
            low = stats[s][:, GROUP + g : GROUP + g + 1] + stats[s][:, 2 * GROUP + g : 2 * GROUP + g + 1]
            mass = mass + low * scale
        heads.append((total / mass).astype(BF))
    context = jnp.concatenate(heads, axis=1)
    row = lax.broadcasted_iota(jnp.int32, (16, 16), 0)
    col = lax.broadcasted_iota(jnp.int32, (16, 16), 1)
    half = jnp.where(row < 8, core[0], 1 - core[0])
    source = (row % 8) // 2 * 4 + half * 2 + row % 2
    pick = jnp.where(col == source, 1.0, 0.0).astype(BF)
    context = mm(pick, context).astype(BF)
    copy.wait()
    result = mm(context, weight[...])
    own[...] = result[:8]
    other[...] = result[8:].astype(BF)


def hidden_of(rows, gate, up):
    g = nt(rows, gate)
    u = nt(rows, up)
    return (g / (1.0 + jnp.exp(-g)) * u).astype(BF)


def mlp_kernel(rows, gate, up, down, out):
    out[...] = mm(hidden_of(rows[...], gate[...], up[...]), down[...]).astype(out.dtype)


def mlp_after_kernel(rows, gate, up, down, earlier, out):
    mlp_kernel(rows, gate, up, down, out)


def move_z(value, k):
    pairs = [(z * 2 + c, (z + k) % 4 * 2 + c) for z in range(4) for c in range(2)]
    return lax.ppermute(value, "tp", pairs)


def move_core(value):
    return lax.ppermute(value, "tp", [(i, i ^ 1) for i in range(8)])


def local(
    activations,
    queries,
    keys,
    values,
    parents,
    node_lengths,
    token_leaf,
    out_weight,
    norm_gain,
    gate_weight,
    up_weight,
    down_weight,
):
    kv = lax.axis_index("kv")
    tp = lax.axis_index("tp")
    z, c = tp // 2, tp % 2
    slots = keys.shape[0]
    gate_t, up_t = gate_weight.T, up_weight.T
    shape = jax.ShapeDtypeStruct

    q = lax.all_to_all(jnp.broadcast_to(queries[None], (16, 16, 640)), "kv", 0, 0)
    keys_wide, values_in, onehot = call(
        prepare_kernel,
        [shape((slots, 256), BF), shape((slots, 128), BF), shape((256, 128), BF)],
        [SM, SM, SM, VM, VM, VM],
        [pltpu.SMEM((16,), jnp.int32)],
    )(node_lengths, parents, (kv * slots)[None], token_leaf[None, :], keys, values)
    packed = call(attend_kernel, shape((256, 768), BF), [VM] * 4, limit=12 << 20)(
        q.reshape(256, 640), keys_wide, values_in, onehot
    )
    parts = lax.all_to_all(packed.reshape(16, 16, 768), "kv", 0, 0)
    own, other = call(
        project_kernel,
        [shape((8, D), F32), shape((8, D), BF)],
        [SM, VM, pltpu.HBM],
        [pltpu.VMEM(out_weight.shape, BF), pltpu.SemaphoreType.DMA],
    )(c[None], parts, out_weight)

    mine = (jnp.arange(8) // 2 == z)[:, None]
    act = jnp.where(mine, jnp.tile(activations, (4, 1)), 0).astype(F32)
    attended = own + move_core(other).astype(F32) + act
    sent = attended.astype(BF)
    for part in [move_z(sent, k) for k in (1, 3, 2)]:
        attended = attended + part.astype(F32)
    residual = attended.astype(BF)
    widened = residual.astype(F32)
    normed = (
        widened
        * lax.rsqrt(jnp.mean(widened * widened, axis=1, keepdims=True) + EPSILON)
        * norm_gain
    ).astype(BF)

    rows = lax.all_to_all(jnp.broadcast_to(normed[None], (16, 8, D)), "kv", 0, 0).reshape(128, D)
    rows_other = move_core(rows)
    y_own = call(mlp_kernel, shape((128, D), F32), [VM] * 4, limit=12 << 20)(rows, gate_t, up_t, down_weight)
    y_other = call(mlp_after_kernel, shape((128, D), BF), [VM] * 4 + [pl.ANY], limit=12 << 20)(
        rows_other, gate_t, up_t, down_weight, y_own
    )
    mixed = (y_own + move_core(y_other).astype(F32)).astype(BF).reshape(64, 2, D)
    keep = lax.dynamic_slice_in_dim(widened, z * 2, 2, 0)
    mixed, keep = lax.optimization_barrier((mixed, keep))
    groups = [[i for i in range(128) if i % 2 == k] for k in range(2)]
    mixed = lax.all_to_all(mixed, ("kv", "tp"), 0, 0, axis_index_groups=groups)
    return (keep + jnp.sum(mixed.astype(F32), axis=0)).astype(BF)


def solution(mesh):
    return jax.shard_map(
        local,
        mesh=mesh,
        in_specs=(
            P(("kv", "tp"), None),
            P("kv", "tp"),
            P("kv", "tp"),
            P("kv", "tp"),
            P(),
            P(),
            P(),
            P("tp", None),
            P(),
            P(None, ("kv", "tp")),
            P(None, ("kv", "tp")),
            P(("kv", "tp"), None),
        ),
        out_specs=P(("kv", "tp"), None),
        check_vma=False,
    )
```

```python
import functools
import math

import jax
import jax.numpy as jnp
from jax import lax
from jax.experimental import pallas as pl
from jax.experimental.pallas import tpu as pltpu
from jax.sharding import PartitionSpec as P

QUERY_HEADS = 40
KEY_VALUE_HEADS = 8
HEAD_WIDTH = 128
GROUP = QUERY_HEADS // KEY_VALUE_HEADS
LOWEST = -(2.0**100)
SCALE = 1.0 / math.sqrt(HEAD_WIDTH)
EPSILON = 1e-06
BF = jnp.bfloat16
F32 = jnp.float32
D = 5120
VM = pltpu.VMEM
SM = pltpu.SMEM


def call(kernel, out_shape, in_spaces, scratch=(), limit=12 << 20, **kw):
    outs = out_shape if isinstance(out_shape, (list, tuple)) else [out_shape]
    specs = [pl.BlockSpec(memory_space=VM) for _ in outs]
    return pl.pallas_call(
        kernel,
        out_shape=out_shape,
        in_specs=[pl.BlockSpec(memory_space=s) for s in in_spaces],
        out_specs=specs if isinstance(out_shape, (list, tuple)) else specs[0],
        scratch_shapes=list(scratch),
        compiler_params=pltpu.CompilerParams(vmem_limit_bytes=limit),
        **kw,
    )


def nt(a, b):
    return lax.dot_general(a, b, (((1,), (1,)), ((), ())), preferred_element_type=F32)


def mm(a, b):
    return lax.dot_general(a, b, (((1,), (0,)), ((), ())), preferred_element_type=F32)


def prepare_kernel(lengths, parents, kv, leaf, keys, values, keys_wide, values_out, onehot, starts):
    nodes = lengths.shape[0]
    slots = keys.shape[0]
    tokens = leaf.shape[1]
    running = jnp.int32(0)
    for n in range(nodes):
        starts[n] = running
        running = running + lengths[n]
    lane = lax.broadcasted_iota(jnp.int32, (1, 128), 1)
    zero = jnp.zeros((1, 128), jnp.int32)
    own_lo, own_hi, up_lo, up_hi = zero, zero, zero, zero
    for n in range(nodes):
        lo = starts[n]
        up = parents[n]
        here = lane == n
        own_lo = jnp.where(here, lo, own_lo)
        own_hi = jnp.where(here, lo + lengths[n], own_hi)
        up_lo = jnp.where(here, starts[up], up_lo)
        up_hi = jnp.where(here, starts[up] + lengths[up], up_hi)
    slot = kv[0] * slots + lax.broadcasted_iota(jnp.int32, (slots, 128), 0)
    seen = (
        (slot < lengths[0])
        | ((slot >= own_lo) & (slot < own_hi))
        | ((slot >= up_lo) & (slot < up_hi))
    )
    keys_wide[:, :HEAD_WIDTH] = keys[...]
    keys_wide[:, HEAD_WIDTH:] = jnp.where(seen, 0.0, LOWEST).astype(BF)
    values_out[...] = values[...]
    node = lax.broadcasted_iota(jnp.int32, (128, tokens), 0)
    onehot[...] = jnp.where(node == leaf[...], 1.0, 0.0).astype(F32).T.astype(BF)


def attend_kernel(q, keys_wide, values, onehot, out):
    tokens = q.shape[0]
    lane_t = lax.broadcasted_iota(jnp.int32, (tokens, 128), 1)
    stats = jnp.zeros((tokens, 128), F32)
    for g in range(GROUP):
        cols = pl.ds(g * HEAD_WIDTH, HEAD_WIDTH)
        q_wide = jnp.concatenate([q[:, cols], onehot[...]], axis=1)
        scores = nt(q_wide, keys_wide[...])
        top = jnp.max(scores, axis=1, keepdims=True).astype(BF).astype(F32)
        weights = jnp.exp((scores - top) * SCALE)
        mass = jnp.sum(weights, axis=1, keepdims=True)
        out[:, cols] = mm(weights.astype(BF), values[...]).astype(BF)
        high = mass.astype(BF).astype(F32)
        stats = jnp.where(lane_t == g, top, stats)
        stats = jnp.where(lane_t == GROUP + g, high, stats)
        stats = jnp.where(lane_t == 2 * GROUP + g, mass - high, stats)
    out[:, GROUP * HEAD_WIDTH :] = stats.astype(BF)


def project_kernel(tp, parts, weight_far, activations, own, other, weight, sem):
    copy = pltpu.make_async_copy(weight_far, weight, sem)
    copy.start()
    z, core = tp[0] >> 1, tp[0] & 1
    sources = parts.shape[0]
    width = GROUP * HEAD_WIDTH
    stats = [parts[s, :, width:].astype(F32) for s in range(sources)]
    top = stats[0]
    for s in stats[1:]:
        top = jnp.maximum(top, s)
    scales = [jnp.exp((s - top) * SCALE) for s in stats]
    heads = []
    for g in range(GROUP):
        total = jnp.zeros((16, HEAD_WIDTH), F32)
        mass = jnp.zeros((16, 1), F32)
        for s in range(sources):
            scale = scales[s][:, g : g + 1]
            part = parts[s, :, g * HEAD_WIDTH : (g + 1) * HEAD_WIDTH].astype(F32)
            total = total + part * scale
            low = stats[s][:, GROUP + g : GROUP + g + 1] + stats[s][:, 2 * GROUP + g : 2 * GROUP + g + 1]
            mass = mass + low * scale
        heads.append((total / mass).astype(BF))
    context = jnp.concatenate(heads, axis=1)
    row = lax.broadcasted_iota(jnp.int32, (16, 16), 0)
    col = lax.broadcasted_iota(jnp.int32, (16, 16), 1)
    half = jnp.where(row < 8, core, 1 - core)
    source = (row % 8) // 2 * 4 + half * 2 + row % 2
    pick = jnp.where(col == source, 1.0, 0.0).astype(BF)
    context = mm(pick, context).astype(BF)
    copy.wait()
    result = mm(context, weight[...])
    row = lax.broadcasted_iota(jnp.int32, (8, 2), 0)
    col = lax.broadcasted_iota(jnp.int32, (8, 2), 1)
    place = jnp.where(row == z * 2 + col, 1.0, 0.0).astype(BF)
    own[...] = result[:8] + mm(place, activations[...])
    other[...] = result[8:].astype(BF)


def hidden_of(rows, gate, up):
    g = nt(rows, gate)
    u = nt(rows, up)
    return (g / (1.0 + jnp.exp(-g)) * u).astype(BF)


def ordered(hidden, tp):
    n = hidden.shape[0]
    row = lax.broadcasted_iota(jnp.int32, (n, n), 0)
    col = lax.broadcasted_iota(jnp.int32, (n, n), 1)
    z = tp[0] >> 1
    source = (row % 32) // 2 * 8 + (z + 4 - row // 32) % 4 * 2 + row % 2
    return mm(jnp.where(col == source, 1.0, 0.0).astype(BF), hidden).astype(BF)


def hidden_kernel(tp, rows, gate, up, out):
    out[...] = ordered(hidden_of(rows[...], gate[...], up[...]), tp)


def mlp_kernel(tp, rows, gate, up, down, earlier, out):
    hidden = ordered(hidden_of(rows[...], gate[...], up[...]), tp)
    out[...] = mm(hidden, down[...]).astype(BF)


def down_kernel(hidden, down, back, own, *sent):
    result = mm(hidden[...], down[...]) + back[...].astype(F32)
    own[...] = result[:32]
    for k, ref in enumerate(sent):
        ref[...] = result[32 * (k + 1) : 32 * (k + 2)].astype(BF)


def move_z(value, k):
    pairs = [(z * 2 + c, (z + k) % 4 * 2 + c) for z in range(4) for c in range(2)]
    return lax.ppermute(value, "tp", pairs)


def move_core(value):
    return lax.ppermute(value, "tp", [(i, i ^ 1) for i in range(8)])


def local(
    activations,
    queries,
    keys,
    values,
    parents,
    node_lengths,
    token_leaf,
    out_weight,
    norm_gain,
    gate_weight,
    up_weight,
    down_weight,
):
    kv = lax.axis_index("kv")[None]
    tp = lax.axis_index("tp")[None]
    gate_t, up_t = gate_weight.T, up_weight.T
    shape = jax.ShapeDtypeStruct
    queries, kv, tp = lax.optimization_barrier((queries, kv, tp))

    q = lax.all_to_all(jnp.broadcast_to(queries[None], (16, 16, 640)), "kv", 0, 0)
    keys_wide, values_in, onehot = call(
        prepare_kernel,
        [shape((keys.shape[0], 256), BF), shape(values.shape, BF), shape((256, 128), BF)],
        [SM, SM, SM, VM, VM, VM],
        [pltpu.SMEM((16,), jnp.int32)],
    )(node_lengths, parents, kv, token_leaf[None, :], keys, values)
    packed = call(attend_kernel, shape((256, 768), BF), [VM] * 4, limit=12 << 20)(
        q.reshape(256, 640), keys_wide, values_in, onehot
    )
    parts = lax.all_to_all(packed.reshape(16, 16, 768), "kv", 0, 0)
    own, other = call(
        project_kernel,
        [shape((8, D), F32), shape((8, D), BF)],
        [SM, VM, pl.ANY, VM],
        [pltpu.VMEM(out_weight.shape, BF), pltpu.SemaphoreType.DMA],
        limit=56 << 20,
    )(tp, parts, out_weight, activations)
    attended = own + move_core(other).astype(F32)
    sent = attended.astype(BF)
    for part in [move_z(sent, k) for k in (1, 3, 2)]:
        attended = attended + part.astype(F32)
    residual = attended.astype(BF)
    widened = residual.astype(F32)
    normed = (
        widened
        * lax.rsqrt(jnp.mean(widened * widened, axis=1, keepdims=True) + EPSILON)
        * norm_gain
    ).astype(BF)

    rows = lax.all_to_all(jnp.broadcast_to(normed[None], (16, 8, D)), "kv", 0, 0).reshape(128, D)
    rows_other = move_core(rows)
    hidden = call(hidden_kernel, shape((128, 216), BF), [SM] + [VM] * 3)(tp, rows, gate_t, up_t)
    y_other = call(mlp_kernel, shape((128, D), BF), [SM] + [VM] * 4 + [pl.ANY])(
        tp, rows_other, gate_t, up_t, down_weight, hidden
    )
    block = shape((32, D), BF)
    mixed, *sent = call(down_kernel, [shape((32, D), F32), block, block, block], [VM] * 3)(
        hidden, down_weight, move_core(y_other)
    )
    for part in [move_z(sent[k - 1], -k) for k in (1, 3, 2)]:
        mixed = mixed + part.astype(F32)
    keep = lax.dynamic_slice_in_dim(widened, (tp[0] >> 1) * 2, 2, 0)
    mixed, keep = lax.optimization_barrier((mixed.astype(BF).reshape(16, 2, D), keep))
    mixed = lax.all_to_all(mixed, "kv", 0, 0)
    return (keep + jnp.sum(mixed.astype(F32), axis=0)).astype(BF)


def solution(mesh):
    return jax.shard_map(
        local,
        mesh=mesh,
        in_specs=(
            P(("kv", "tp"), None),
            P("kv", "tp"),
            P("kv", "tp"),
            P("kv", "tp"),
            P(),
            P(),
            P(),
            P("tp", None),
            P(),
            P(None, ("kv", "tp")),
            P(None, ("kv", "tp")),
            P(("kv", "tp"), None),
        ),
        out_specs=P(("kv", "tp"), None),
        check_vma=False,
    )
```

```python
import functools
import math

import jax
import jax.numpy as jnp
from jax import lax
from jax.experimental import pallas as pl
from jax.experimental.pallas import tpu as pltpu
from jax.sharding import PartitionSpec as P

QUERY_HEADS = 40
KEY_VALUE_HEADS = 8
HEAD_WIDTH = 128
GROUP = QUERY_HEADS // KEY_VALUE_HEADS
LOWEST = -(2.0**100)
SCALE = 1.0 / math.sqrt(HEAD_WIDTH)
EPSILON = 1e-06
BF = jnp.bfloat16
F32 = jnp.float32
D = 5120
VM = pltpu.VMEM
SM = pltpu.SMEM


def call(kernel, out_shape, in_spaces, scratch=(), limit=12 << 20, **kw):
    outs = out_shape if isinstance(out_shape, (list, tuple)) else [out_shape]
    specs = [pl.BlockSpec(memory_space=VM) for _ in outs]
    return pl.pallas_call(
        kernel,
        out_shape=out_shape,
        in_specs=[pl.BlockSpec(memory_space=s) for s in in_spaces],
        out_specs=specs if isinstance(out_shape, (list, tuple)) else specs[0],
        scratch_shapes=list(scratch),
        compiler_params=pltpu.CompilerParams(vmem_limit_bytes=limit),
        **kw,
    )


def nt(a, b):
    return lax.dot_general(a, b, (((1,), (1,)), ((), ())), preferred_element_type=F32)


def mm(a, b):
    return lax.dot_general(a, b, (((1,), (0,)), ((), ())), preferred_element_type=F32)


def prepare_kernel(lengths, parents, kv, leaf, keys, values, keys_wide, values_out, onehot, starts):
    nodes = lengths.shape[0]
    slots = keys.shape[0]
    tokens = leaf.shape[1]
    running = jnp.int32(0)
    for n in range(nodes):
        starts[n] = running
        running = running + lengths[n]
    lane = lax.broadcasted_iota(jnp.int32, (1, 128), 1)
    zero = jnp.zeros((1, 128), jnp.int32)
    own_lo, own_hi, up_lo, up_hi = zero, zero, zero, zero
    for n in range(nodes):
        lo = starts[n]
        up = parents[n]
        here = lane == n
        own_lo = jnp.where(here, lo, own_lo)
        own_hi = jnp.where(here, lo + lengths[n], own_hi)
        up_lo = jnp.where(here, starts[up], up_lo)
        up_hi = jnp.where(here, starts[up] + lengths[up], up_hi)
    slot = kv[0] * slots + lax.broadcasted_iota(jnp.int32, (slots, 128), 0)
    seen = (
        (slot < lengths[0])
        | ((slot >= own_lo) & (slot < own_hi))
        | ((slot >= up_lo) & (slot < up_hi))
    )
    keys_wide[:, :HEAD_WIDTH] = keys[...]
    keys_wide[:, HEAD_WIDTH:] = jnp.where(seen, 0.0, LOWEST).astype(BF)
    values_out[...] = values[...]
    node = lax.broadcasted_iota(jnp.int32, (128, tokens), 0)
    onehot[...] = jnp.where(node == leaf[...], 1.0, 0.0).astype(F32).T.astype(BF)


def attend_kernel(q, keys_wide, values, onehot, out):
    tokens = q.shape[0]
    lane_t = lax.broadcasted_iota(jnp.int32, (tokens, 128), 1)
    stats = jnp.zeros((tokens, 128), F32)
    for g in range(GROUP):
        cols = pl.ds(g * HEAD_WIDTH, HEAD_WIDTH)
        q_wide = jnp.concatenate([q[:, cols], onehot[...]], axis=1)
        scores = nt(q_wide, keys_wide[...])
        top = jnp.max(scores, axis=1, keepdims=True).astype(BF).astype(F32)
        weights = jnp.exp((scores - top) * SCALE)
        mass = jnp.sum(weights, axis=1, keepdims=True)
        out[:, cols] = mm(weights.astype(BF), values[...]).astype(BF)
        high = mass.astype(BF).astype(F32)
        stats = jnp.where(lane_t == g, top, stats)
        stats = jnp.where(lane_t == GROUP + g, high, stats)
        stats = jnp.where(lane_t == 2 * GROUP + g, mass - high, stats)
    out[:, GROUP * HEAD_WIDTH :] = stats.astype(BF)


def project_kernel(tp, parts, weight, activations, own, other):
    z, core = tp[0] >> 1, tp[0] & 1
    sources = parts.shape[0]
    width = GROUP * HEAD_WIDTH
    stats = [parts[s, :, width:].astype(F32) for s in range(sources)]
    top = stats[0]
    for s in stats[1:]:
        top = jnp.maximum(top, s)
    scales = [jnp.exp((s - top) * SCALE) for s in stats]
    heads = []
    for g in range(GROUP):
        total = jnp.zeros((16, HEAD_WIDTH), F32)
        mass = jnp.zeros((16, 1), F32)
        for s in range(sources):
            scale = scales[s][:, g : g + 1]
            part = parts[s, :, g * HEAD_WIDTH : (g + 1) * HEAD_WIDTH].astype(F32)
            total = total + part * scale
            low = stats[s][:, GROUP + g : GROUP + g + 1] + stats[s][:, 2 * GROUP + g : 2 * GROUP + g + 1]
            mass = mass + low * scale
        heads.append((total / mass).astype(BF))
    context = jnp.concatenate(heads, axis=1)
    row = lax.broadcasted_iota(jnp.int32, (16, 16), 0)
    col = lax.broadcasted_iota(jnp.int32, (16, 16), 1)
    half = jnp.where(row < 8, core, 1 - core)
    source = (row % 8) // 2 * 4 + half * 2 + row % 2
    pick = jnp.where(col == source, 1.0, 0.0).astype(BF)
    context = mm(pick, context).astype(BF)
    result = mm(context, weight[...])
    row = lax.broadcasted_iota(jnp.int32, (8, 2), 0)
    col = lax.broadcasted_iota(jnp.int32, (8, 2), 1)
    place = jnp.where(row == z * 2 + col, 1.0, 0.0).astype(BF)
    own[...] = result[:8] + mm(place, activations[...])
    other[...] = result[8:].astype(BF)


def hidden_of(rows, gate, up):
    g = nt(rows, gate)
    u = nt(rows, up)
    return (g / (1.0 + jnp.exp(-g)) * u).astype(BF)


def ordered(hidden, kv, tp, other):
    n = hidden.shape[0]
    row = lax.broadcasted_iota(jnp.int32, (n, n), 0)
    col = lax.broadcasted_iota(jnp.int32, (n, n), 1)
    x, z, core = kv[0] >> 2, tp[0] >> 1, tp[0] & 1
    core = 1 - core if other else core
    run = row // 16
    q = (run & 1) * 8 + (row & 15) // 2
    places = jnp.where(run < 2, 0, jnp.where((run == 2) | (run == 5), 2, jnp.where((run == 3) | (run == 6), 1, 3)))
    along_z = q * 8 + ((z + places) & 3) * 2
    along_x = (((x + places) & 3) * 4 + q // 4) * 8 + (q & 3) * 2
    source = jnp.where(core == 0, along_z, along_x) + (row & 1)
    return mm(jnp.where(col == source, 1.0, 0.0).astype(BF), hidden).astype(BF)


def hidden_kernel(kv, tp, rows, gate, up, out):
    out[...] = ordered(hidden_of(rows[...], gate[...], up[...]), kv, tp, False)


def mlp_kernel(kv, tp, rows, gate, up, down, out):
    hidden = ordered(hidden_of(rows[...], gate[...], up[...]), kv, tp, True)
    out[...] = mm(hidden, down[...]).astype(BF)


def down_kernel(hidden, down, back, own, ahead, behind, rest_ahead, rest_behind):
    result = mm(hidden[...], down[...]) + back[...].astype(F32)
    own[...] = result[:32]
    ahead[...] = result[32:64].astype(BF)
    behind[...] = result[64:96].astype(BF)
    rest_ahead[...] = result[96:112]
    rest_behind[...] = result[112:]


def device(x, y, z, c):
    return (x * 4 + y) * 8 + z * 2 + c


def move_ring(value, k):
    pairs = [
        (device(x, y, z, c), device(x, y, (z + k) % 4, c) if c == 0 else device((x + k) % 4, y, z, c))
        for x in range(4)
        for y in range(4)
        for z in range(4)
        for c in range(2)
    ]
    return lax.ppermute(value, ("kv", "tp"), pairs)


PLANES = [[device(x, y, z, 0) for x in range(4) for y in range(4)] for z in range(4)] + [
    [device(x, y, z, 1) for y in range(4) for z in range(4)] for x in range(4)
]


def move_z(value, k):
    pairs = [(z * 2 + c, (z + k) % 4 * 2 + c) for z in range(4) for c in range(2)]
    return lax.ppermute(value, "tp", pairs)


def move_core(value):
    return lax.ppermute(value, "tp", [(i, i ^ 1) for i in range(8)])


def local(
    activations,
    queries,
    keys,
    values,
    parents,
    node_lengths,
    token_leaf,
    out_weight,
    norm_gain,
    gate_weight,
    up_weight,
    down_weight,
):
    kv = lax.axis_index("kv")[None]
    tp = lax.axis_index("tp")[None]
    gate_t, up_t = gate_weight.T, up_weight.T
    shape = jax.ShapeDtypeStruct
    queries, kv, tp = lax.optimization_barrier((queries, kv, tp))

    q = lax.all_to_all(jnp.broadcast_to(queries[None], (16, 16, 640)), "kv", 0, 0)
    keys_wide, values_in, onehot = call(
        prepare_kernel,
        [shape((keys.shape[0], 256), BF), shape(values.shape, BF), shape((256, 128), BF)],
        [SM, SM, SM, VM, VM, VM],
        [pltpu.SMEM((16,), jnp.int32)],
    )(node_lengths, parents, kv, token_leaf[None, :], keys, values)
    packed = call(attend_kernel, shape((256, 768), BF), [VM] * 4, limit=12 << 20)(
        q.reshape(256, 640), keys_wide, values_in, onehot
    )
    parts = lax.all_to_all(packed.reshape(16, 16, 768), "kv", 0, 0)
    own, other = call(project_kernel, [shape((8, D), F32), shape((8, D), BF)], [SM, VM, VM, VM])(
        tp, parts, out_weight, activations
    )
    attended = own + move_core(other).astype(F32)
    sent = attended.astype(BF)
    for part in [move_z(sent, k) for k in (1, 3, 2)]:
        attended = attended + part.astype(F32)
    residual = attended.astype(BF)
    widened = residual.astype(F32)
    normed = (
        widened
        * lax.rsqrt(jnp.mean(widened * widened, axis=1, keepdims=True) + EPSILON)
        * norm_gain
    ).astype(BF)

    rows = lax.all_to_all(jnp.broadcast_to(normed[None], (16, 8, D)), "kv", 0, 0).reshape(128, D)
    rows_other = move_core(rows)
    hidden = call(hidden_kernel, shape((128, 216), BF), [SM, SM] + [VM] * 3)(kv, tp, rows, gate_t, up_t)
    rows_other, hidden = lax.optimization_barrier((rows_other, hidden))
    y_other = call(mlp_kernel, shape((128, D), BF), [SM, SM] + [VM] * 4)(
        kv, tp, rows_other, gate_t, up_t, down_weight
    )
    wide, narrow = shape((32, D), BF), shape((16, D), F32)
    mixed, ahead, behind, rest_ahead, rest_behind = call(
        down_kernel, [shape((32, D), F32), wide, wide, narrow, narrow], [VM] * 3
    )(hidden, down_weight, move_core(y_other))
    from_behind = move_ring(ahead, 1)
    from_ahead = move_ring(behind, -1)
    rest_ahead = move_ring((rest_ahead + from_behind[:16].astype(F32)).astype(BF), 1)
    rest_behind = move_ring((rest_behind + from_ahead[16:].astype(F32)).astype(BF), -1)
    first = mixed[:16] + from_ahead[:16].astype(F32) + rest_ahead.astype(F32)
    second = mixed[16:] + from_behind[16:].astype(F32) + rest_behind.astype(F32)
    mixed = jnp.concatenate([first.astype(BF).reshape(8, 2, D), second.astype(BF).reshape(8, 2, D)], axis=0)
    keep = lax.dynamic_slice_in_dim(widened, (tp[0] >> 1) * 2, 2, 0)
    mixed, keep = lax.optimization_barrier((mixed, keep))
    mixed = lax.all_to_all(mixed, ("kv", "tp"), 0, 0, axis_index_groups=PLANES)
    return (keep + jnp.sum(mixed.astype(F32), axis=0)).astype(BF)


def solution(mesh):
    return jax.shard_map(
        local,
        mesh=mesh,
        in_specs=(
            P(("kv", "tp"), None),
            P("kv", "tp"),
            P("kv", "tp"),
            P("kv", "tp"),
            P(),
            P(),
            P(),
            P("tp", None),
            P(),
            P(None, ("kv", "tp")),
            P(None, ("kv", "tp")),
            P(("kv", "tp"), None),
        ),
        out_specs=P(("kv", "tp"), None),
        check_vma=False,
    )
```

```python
import functools
import math

import jax
import jax.numpy as jnp
from jax import lax
from jax.experimental import pallas as pl
from jax.experimental.pallas import tpu as pltpu
from jax.sharding import PartitionSpec as P

QUERY_HEADS = 40
KEY_VALUE_HEADS = 8
HEAD_WIDTH = 128
GROUP = QUERY_HEADS // KEY_VALUE_HEADS
LOWEST = -(2.0**100)
SCALE = 1.0 / math.sqrt(HEAD_WIDTH)
EPSILON = 1e-06
BF = jnp.bfloat16
F32 = jnp.float32
D = 5120
VM = pltpu.VMEM
SM = pltpu.SMEM


def call(kernel, out_shape, in_spaces, scratch=(), limit=12 << 20, **kw):
    outs = out_shape if isinstance(out_shape, (list, tuple)) else [out_shape]
    specs = [pl.BlockSpec(memory_space=VM) for _ in outs]
    return pl.pallas_call(
        kernel,
        out_shape=out_shape,
        in_specs=[pl.BlockSpec(memory_space=s) for s in in_spaces],
        out_specs=specs if isinstance(out_shape, (list, tuple)) else specs[0],
        scratch_shapes=list(scratch),
        compiler_params=pltpu.CompilerParams(vmem_limit_bytes=limit),
        **kw,
    )


def nt(a, b):
    return lax.dot_general(a, b, (((1,), (1,)), ((), ())), preferred_element_type=F32)


def mm(a, b):
    return lax.dot_general(a, b, (((1,), (0,)), ((), ())), preferred_element_type=F32)


def prepare_kernel(lengths, parents, kv, leaf, keys, values, keys_wide, values_out, onehot, starts):
    nodes = lengths.shape[0]
    slots = keys.shape[0]
    tokens = leaf.shape[1]
    running = jnp.int32(0)
    for n in range(nodes):
        starts[n] = running
        running = running + lengths[n]
    lane = lax.broadcasted_iota(jnp.int32, (1, 128), 1)
    zero = jnp.zeros((1, 128), jnp.int32)
    own_lo, own_hi, up_lo, up_hi = zero, zero, zero, zero
    for n in range(nodes):
        lo = starts[n]
        up = parents[n]
        here = lane == n
        own_lo = jnp.where(here, lo, own_lo)
        own_hi = jnp.where(here, lo + lengths[n], own_hi)
        up_lo = jnp.where(here, starts[up], up_lo)
        up_hi = jnp.where(here, starts[up] + lengths[up], up_hi)
    slot = kv[0] * slots + lax.broadcasted_iota(jnp.int32, (slots, 128), 0)
    seen = (
        (slot < lengths[0])
        | ((slot >= own_lo) & (slot < own_hi))
        | ((slot >= up_lo) & (slot < up_hi))
    )
    keys_wide[:, :HEAD_WIDTH] = keys[...]
    keys_wide[:, HEAD_WIDTH:] = jnp.where(seen, 0.0, LOWEST).astype(BF)
    values_out[...] = values[...]
    node = lax.broadcasted_iota(jnp.int32, (128, tokens), 0)
    onehot[...] = jnp.where(node == leaf[...], 1.0, 0.0).astype(F32).T.astype(BF)


def attend_kernel(q, keys_wide, values, onehot, out):
    tokens = q.shape[0]
    lane_t = lax.broadcasted_iota(jnp.int32, (tokens, 128), 1)
    stats = jnp.zeros((tokens, 128), F32)
    for g in range(GROUP):
        cols = pl.ds(g * HEAD_WIDTH, HEAD_WIDTH)
        q_wide = jnp.concatenate([q[:, cols], onehot[...]], axis=1)
        scores = nt(q_wide, keys_wide[...])
        top = jnp.max(scores, axis=1, keepdims=True).astype(BF).astype(F32)
        weights = jnp.exp((scores - top) * SCALE)
        mass = jnp.sum(weights, axis=1, keepdims=True)
        out[:, cols] = mm(weights.astype(BF), values[...]).astype(BF)
        high = mass.astype(BF).astype(F32)
        stats = jnp.where(lane_t == g, top, stats)
        stats = jnp.where(lane_t == GROUP + g, high, stats)
        stats = jnp.where(lane_t == 2 * GROUP + g, mass - high, stats)
    out[:, GROUP * HEAD_WIDTH :] = stats.astype(BF)


def project_kernel(tp, parts, weight_far, activations, own, other, weight, sem):
    copy = pltpu.make_async_copy(weight_far, weight, sem)
    copy.start()
    z, core = tp[0] >> 1, tp[0] & 1
    sources = parts.shape[0]
    width = GROUP * HEAD_WIDTH
    stats = [parts[s, :, width:].astype(F32) for s in range(sources)]
    top = stats[0]
    for s in stats[1:]:
        top = jnp.maximum(top, s)
    scales = [jnp.exp((s - top) * SCALE) for s in stats]
    heads = []
    for g in range(GROUP):
        total = jnp.zeros((16, HEAD_WIDTH), F32)
        mass = jnp.zeros((16, 1), F32)
        for s in range(sources):
            scale = scales[s][:, g : g + 1]
            part = parts[s, :, g * HEAD_WIDTH : (g + 1) * HEAD_WIDTH].astype(F32)
            total = total + part * scale
            low = stats[s][:, GROUP + g : GROUP + g + 1] + stats[s][:, 2 * GROUP + g : 2 * GROUP + g + 1]
            mass = mass + low * scale
        heads.append((total / mass).astype(BF))
    context = jnp.concatenate(heads, axis=1)
    row = lax.broadcasted_iota(jnp.int32, (16, 16), 0)
    col = lax.broadcasted_iota(jnp.int32, (16, 16), 1)
    half = jnp.where(row < 8, core, 1 - core)
    source = (row % 8) // 2 * 4 + half * 2 + row % 2
    pick = jnp.where(col == source, 1.0, 0.0).astype(BF)
    context = mm(pick, context).astype(BF)
    copy.wait()
    result = mm(context, weight[...])
    row = lax.broadcasted_iota(jnp.int32, (8, 2), 0)
    col = lax.broadcasted_iota(jnp.int32, (8, 2), 1)
    place = jnp.where(row == z * 2 + col, 1.0, 0.0).astype(BF)
    own[...] = result[:8] + mm(place, activations[...])
    other[...] = result[8:].astype(BF)


def hidden_of(rows, gate, up):
    g = nt(rows, gate)
    u = nt(rows, up)
    return (g / (1.0 + jnp.exp(-g)) * u).astype(BF)


def ordered(hidden, kv, tp):
    n = hidden.shape[0]
    row = lax.broadcasted_iota(jnp.int32, (n, n), 0)
    col = lax.broadcasted_iota(jnp.int32, (n, n), 1)
    x, z, core = kv[0] >> 2, tp[0] >> 1, tp[0] & 1
    run = row // 16
    q = (run & 1) * 8 + (row & 15) // 2
    places = jnp.where(run < 2, 0, jnp.where((run == 2) | (run == 5), 2, jnp.where((run == 3) | (run == 6), 1, 3)))
    along_z = q * 8 + ((z + places) & 3) * 2
    along_x = (((x + places) & 3) * 4 + q // 4) * 8 + (q & 3) * 2
    source = jnp.where(core == 0, along_z, along_x) + (row & 1)
    return mm(jnp.where(col == source, 1.0, 0.0).astype(BF), hidden).astype(BF)


def mlp_kernel(
    kv, tp, rows, gate, up, down, gate_far, up_far, down_far, own, ahead, behind, rest_ahead, rest_behind
):
    near = ordered(hidden_of(rows[...], gate[...], up[...]), kv, tp)
    far = ordered(hidden_of(rows[...], gate_far[...], up_far[...]), kv, tp)
    result = mm(near, down[...]) + mm(far, down_far[...])
    own[...] = result[:32]
    ahead[...] = result[32:64].astype(BF)
    behind[...] = result[64:96].astype(BF)
    rest_ahead[...] = result[96:112]
    rest_behind[...] = result[112:]


def device(x, y, z, c):
    return (x * 4 + y) * 8 + z * 2 + c


def move_ring(value, k):
    pairs = [
        (device(x, y, z, c), device(x, y, (z + k) % 4, c) if c == 0 else device((x + k) % 4, y, z, c))
        for x in range(4)
        for y in range(4)
        for z in range(4)
        for c in range(2)
    ]
    return lax.ppermute(value, ("kv", "tp"), pairs)


PLANES = [[device(x, y, z, 0) for x in range(4) for y in range(4)] for z in range(4)] + [
    [device(x, y, z, 1) for y in range(4) for z in range(4)] for x in range(4)
]


def move_z(value, k):
    pairs = [(z * 2 + c, (z + k) % 4 * 2 + c) for z in range(4) for c in range(2)]
    return lax.ppermute(value, "tp", pairs)


def move_core(value):
    return lax.ppermute(value, "tp", [(i, i ^ 1) for i in range(8)])


def local(
    activations,
    queries,
    keys,
    values,
    parents,
    node_lengths,
    token_leaf,
    out_weight,
    norm_gain,
    gate_weight,
    up_weight,
    down_weight,
):
    kv = lax.axis_index("kv")[None]
    tp = lax.axis_index("tp")[None]
    gate_t, up_t = gate_weight.T, up_weight.T
    shape = jax.ShapeDtypeStruct
    far = [move_core(w) for w in (gate_t, up_t, down_weight)]
    queries, kv, tp = lax.optimization_barrier((queries, kv, tp))

    q = lax.all_to_all(jnp.broadcast_to(queries[None], (16, 16, 640)), "kv", 0, 0)
    keys_wide, values_in, onehot = call(
        prepare_kernel,
        [shape((keys.shape[0], 256), BF), shape(values.shape, BF), shape((256, 128), BF)],
        [SM, SM, SM, VM, VM, VM],
        [pltpu.SMEM((16,), jnp.int32)],
    )(node_lengths, parents, kv, token_leaf[None, :], keys, values)
    packed = call(attend_kernel, shape((256, 768), BF), [VM] * 4, limit=12 << 20)(
        q.reshape(256, 640), keys_wide, values_in, onehot
    )
    parts = lax.all_to_all(packed.reshape(16, 16, 768), "kv", 0, 0)
    own, other = call(
        project_kernel,
        [shape((8, D), F32), shape((8, D), BF)],
        [SM, VM, pl.ANY, VM],
        [pltpu.VMEM(out_weight.shape, BF), pltpu.SemaphoreType.DMA],
        limit=48 << 20,
    )(tp, parts, out_weight, activations)
    attended = own + move_core(other).astype(F32)
    sent = attended.astype(BF)
    for part in [move_z(sent, k) for k in (1, 3, 2)]:
        attended = attended + part.astype(F32)
    residual = attended.astype(BF)
    widened = residual.astype(F32)
    normed = (
        widened
        * lax.rsqrt(jnp.mean(widened * widened, axis=1, keepdims=True) + EPSILON)
        * norm_gain
    ).astype(BF)

    rows = lax.all_to_all(jnp.broadcast_to(normed[None], (16, 8, D)), "kv", 0, 0).reshape(128, D)
    wide, narrow = shape((32, D), BF), shape((16, D), F32)
    mixed, ahead, behind, rest_ahead, rest_behind = call(
        mlp_kernel, [shape((32, D), F32), wide, wide, narrow, narrow], [SM, SM] + [VM] * 7, limit=28 << 20
    )(kv, tp, rows, gate_t, up_t, down_weight, *far)
    from_behind = move_ring(ahead, 1)
    from_ahead = move_ring(behind, -1)
    rest_ahead = move_ring((rest_ahead + from_behind[:16].astype(F32)).astype(BF), 1)
    rest_behind = move_ring((rest_behind + from_ahead[16:].astype(F32)).astype(BF), -1)
    first = mixed[:16] + from_ahead[:16].astype(F32) + rest_ahead.astype(F32)
    second = mixed[16:] + from_behind[16:].astype(F32) + rest_behind.astype(F32)
    mixed = jnp.concatenate([first.astype(BF).reshape(8, 2, D), second.astype(BF).reshape(8, 2, D)], axis=0)
    keep = lax.dynamic_slice_in_dim(widened, (tp[0] >> 1) * 2, 2, 0)
    mixed, keep = lax.optimization_barrier((mixed, keep))
    mixed = lax.all_to_all(mixed, ("kv", "tp"), 0, 0, axis_index_groups=PLANES)
    return (keep + jnp.sum(mixed.astype(F32), axis=0)).astype(BF)


def solution(mesh):
    return jax.shard_map(
        local,
        mesh=mesh,
        in_specs=(
            P(("kv", "tp"), None),
            P("kv", "tp"),
            P("kv", "tp"),
            P("kv", "tp"),
            P(),
            P(),
            P(),
            P("tp", None),
            P(),
            P(None, ("kv", "tp")),
            P(None, ("kv", "tp")),
            P(("kv", "tp"), None),
        ),
        out_specs=P(("kv", "tp"), None),
        check_vma=False,
    )
```

```python
import functools
import math

import jax
import jax.numpy as jnp
from jax import lax
from jax.experimental import pallas as pl
from jax.experimental.pallas import tpu as pltpu
from jax.sharding import PartitionSpec as P

QUERY_HEADS = 40
KEY_VALUE_HEADS = 8
HEAD_WIDTH = 128
GROUP = QUERY_HEADS // KEY_VALUE_HEADS
LOWEST = -(2.0**100)
SCALE = 1.0 / math.sqrt(HEAD_WIDTH)
EPSILON = 1e-06
BF = jnp.bfloat16
F32 = jnp.float32
D = 5120
VM = pltpu.VMEM
SM = pltpu.SMEM


def call(kernel, out_shape, in_spaces, scratch=(), limit=12 << 20, **kw):
    outs = out_shape if isinstance(out_shape, (list, tuple)) else [out_shape]
    specs = [pl.BlockSpec(memory_space=VM) for _ in outs]
    return pl.pallas_call(
        kernel,
        out_shape=out_shape,
        in_specs=[pl.BlockSpec(memory_space=s) for s in in_spaces],
        out_specs=specs if isinstance(out_shape, (list, tuple)) else specs[0],
        scratch_shapes=list(scratch),
        compiler_params=pltpu.CompilerParams(vmem_limit_bytes=limit),
        **kw,
    )


def nt(a, b):
    return lax.dot_general(a, b, (((1,), (1,)), ((), ())), preferred_element_type=F32)


def mm(a, b):
    return lax.dot_general(a, b, (((1,), (0,)), ((), ())), preferred_element_type=F32)


def prepare_kernel(lengths, parents, kv, leaf, keys, values, keys_wide, values_out, onehot, starts):
    nodes = lengths.shape[0]
    slots = keys.shape[0]
    tokens = leaf.shape[1]
    running = jnp.int32(0)
    for n in range(nodes):
        starts[n] = running
        running = running + lengths[n]
    lane = lax.broadcasted_iota(jnp.int32, (1, 128), 1)
    zero = jnp.zeros((1, 128), jnp.int32)
    own_lo, own_hi, up_lo, up_hi = zero, zero, zero, zero
    for n in range(nodes):
        lo = starts[n]
        up = parents[n]
        here = lane == n
        own_lo = jnp.where(here, lo, own_lo)
        own_hi = jnp.where(here, lo + lengths[n], own_hi)
        up_lo = jnp.where(here, starts[up], up_lo)
        up_hi = jnp.where(here, starts[up] + lengths[up], up_hi)
    slot = kv[0] * slots + lax.broadcasted_iota(jnp.int32, (slots, 128), 0)
    seen = (
        (slot < lengths[0])
        | ((slot >= own_lo) & (slot < own_hi))
        | ((slot >= up_lo) & (slot < up_hi))
    )
    keys_wide[:, :HEAD_WIDTH] = keys[...]
    keys_wide[:, HEAD_WIDTH:] = jnp.where(seen, 0.0, LOWEST).astype(BF)
    values_out[...] = values[...]
    node = lax.broadcasted_iota(jnp.int32, (128, tokens), 0)
    onehot[...] = jnp.where(node == leaf[...], 1.0, 0.0).astype(F32).T.astype(BF)


def attend_kernel(q, keys_wide, values, onehot, out):
    tokens = q.shape[0]
    lane_t = lax.broadcasted_iota(jnp.int32, (tokens, 128), 1)
    stats = jnp.zeros((tokens, 128), F32)
    for g in range(GROUP):
        cols = pl.ds(g * HEAD_WIDTH, HEAD_WIDTH)
        q_wide = jnp.concatenate([q[:, cols], onehot[...]], axis=1)
        scores = nt(q_wide, keys_wide[...])
        top = jnp.max(scores, axis=1, keepdims=True).astype(BF).astype(F32)
        weights = jnp.exp((scores - top) * SCALE)
        mass = jnp.sum(weights, axis=1, keepdims=True)
        out[:, cols] = mm(weights.astype(BF), values[...]).astype(BF)
        high = mass.astype(BF).astype(F32)
        stats = jnp.where(lane_t == g, top, stats)
        stats = jnp.where(lane_t == GROUP + g, high, stats)
        stats = jnp.where(lane_t == 2 * GROUP + g, mass - high, stats)
    out[:, GROUP * HEAD_WIDTH :] = stats.astype(BF)


def project_kernel(tp, parts, weight_far, activations, own, other, weight, sem):
    copies = []
    for g in range(GROUP):
        piece = pl.ds(g * HEAD_WIDTH, HEAD_WIDTH)
        copies.append(pltpu.make_async_copy(weight_far.at[piece], weight.at[piece], sem.at[g]))
        copies[g].start()
    z, core = tp[0] >> 1, tp[0] & 1
    sources = parts.shape[0]
    width = GROUP * HEAD_WIDTH
    stats = [parts[s, :, width:].astype(F32) for s in range(sources)]
    top = stats[0]
    for s in stats[1:]:
        top = jnp.maximum(top, s)
    scales = [jnp.exp((s - top) * SCALE) for s in stats]
    heads = []
    for g in range(GROUP):
        total = jnp.zeros((16, HEAD_WIDTH), F32)
        mass = jnp.zeros((16, 1), F32)
        for s in range(sources):
            scale = scales[s][:, g : g + 1]
            part = parts[s, :, g * HEAD_WIDTH : (g + 1) * HEAD_WIDTH].astype(F32)
            total = total + part * scale
            low = stats[s][:, GROUP + g : GROUP + g + 1] + stats[s][:, 2 * GROUP + g : 2 * GROUP + g + 1]
            mass = mass + low * scale
        heads.append((total / mass).astype(BF))
    context = jnp.concatenate(heads, axis=1)
    row = lax.broadcasted_iota(jnp.int32, (16, 16), 0)
    col = lax.broadcasted_iota(jnp.int32, (16, 16), 1)
    half = jnp.where(row < 8, core, 1 - core)
    source = (row % 8) // 2 * 4 + half * 2 + row % 2
    pick = jnp.where(col == source, 1.0, 0.0).astype(BF)
    context = mm(pick, context).astype(BF)
    for copy in copies:
        copy.wait()
    result = mm(context, weight[...])
    row = lax.broadcasted_iota(jnp.int32, (8, 2), 0)
    col = lax.broadcasted_iota(jnp.int32, (8, 2), 1)
    place = jnp.where(row == z * 2 + col, 1.0, 0.0).astype(BF)
    own[...] = result[:8] + mm(place, activations[...])
    other[...] = result[8:].astype(BF)


def hidden_of(rows, gate, up):
    g = nt(rows, gate)
    u = nt(rows, up)
    return (g / (1.0 + jnp.exp(-g)) * u).astype(BF)


def ordered(hidden, kv, tp):
    n = hidden.shape[0]
    row = lax.broadcasted_iota(jnp.int32, (n, n), 0)
    col = lax.broadcasted_iota(jnp.int32, (n, n), 1)
    x, z, core = kv[0] >> 2, tp[0] >> 1, tp[0] & 1
    block = row // 32
    q = (row & 31) // 2
    places = jnp.where(block == 0, 0, jnp.where(block == 1, 2, jnp.where(block == 2, 1, 3)))
    along_z = q * 8 + ((z + places) & 3) * 2
    along_x = (((x + places) & 3) * 4 + q // 4) * 8 + (q & 3) * 2
    source = jnp.where(core == 0, along_z, along_x) + (row & 1)
    return mm(jnp.where(col == source, 1.0, 0.0).astype(BF), hidden).astype(BF)


def mlp_kernel(kv, tp, rows, gate, up, down, gate_far, up_far, down_far, own, *sent):
    near = ordered(hidden_of(rows[...], gate[...], up[...]), kv, tp)
    far = ordered(hidden_of(rows[...], gate_far[...], up_far[...]), kv, tp)
    result = mm(near, down[...]) + mm(far, down_far[...])
    own[...] = result[:32]
    for k, ref in enumerate(sent):
        ref[...] = result[32 * (k + 1) : 32 * (k + 2)].astype(BF)


def device(x, y, z, c):
    return (x * 4 + y) * 8 + z * 2 + c


def move_ring(value, k):
    pairs = [
        (device(x, y, z, c), device(x, y, (z + k) % 4, c) if c == 0 else device((x + k) % 4, y, z, c))
        for x in range(4)
        for y in range(4)
        for z in range(4)
        for c in range(2)
    ]
    return lax.ppermute(value, ("kv", "tp"), pairs)


PLANES = [[device(x, y, z, 0) for x in range(4) for y in range(4)] for z in range(4)] + [
    [device(x, y, z, 1) for y in range(4) for z in range(4)] for x in range(4)
]


def move_z(value, k):
    pairs = [(z * 2 + c, (z + k) % 4 * 2 + c) for z in range(4) for c in range(2)]
    return lax.ppermute(value, "tp", pairs)


def move_core(value):
    return lax.ppermute(value, "tp", [(i, i ^ 1) for i in range(8)])


def local(
    activations,
    queries,
    keys,
    values,
    parents,
    node_lengths,
    token_leaf,
    out_weight,
    norm_gain,
    gate_weight,
    up_weight,
    down_weight,
):
    kv = lax.axis_index("kv")[None]
    tp = lax.axis_index("tp")[None]
    gate_t, up_t = gate_weight.T, up_weight.T
    shape = jax.ShapeDtypeStruct
    far = [move_core(w) for w in (gate_t, up_t, down_weight)]
    queries, kv, tp = lax.optimization_barrier((queries, kv, tp))

    q = lax.all_to_all(jnp.broadcast_to(queries[None], (16, 16, 640)), "kv", 0, 0)
    keys_wide, values_in, onehot = call(
        prepare_kernel,
        [shape((keys.shape[0], 256), BF), shape(values.shape, BF), shape((256, 128), BF)],
        [SM, SM, SM, VM, VM, VM],
        [pltpu.SMEM((16,), jnp.int32)],
    )(node_lengths, parents, kv, token_leaf[None, :], keys, values)
    packed = call(attend_kernel, shape((256, 768), BF), [VM] * 4, limit=12 << 20)(
        q.reshape(256, 640), keys_wide, values_in, onehot
    )
    parts = lax.all_to_all(packed.reshape(16, 16, 768), "kv", 0, 0)
    own, other = call(
        project_kernel,
        [shape((8, D), F32), shape((8, D), BF)],
        [SM, VM, pl.ANY, VM],
        [pltpu.VMEM(out_weight.shape, BF), pltpu.SemaphoreType.DMA((GROUP,))],
        limit=48 << 20,
    )(tp, parts, out_weight, activations)
    attended = own + move_core(other).astype(F32)
    sent = attended.astype(BF)
    for part in [move_z(sent, k) for k in (1, 3, 2)]:
        attended = attended + part.astype(F32)
    residual = attended.astype(BF)
    widened = residual.astype(F32)
    normed = (
        widened
        * lax.rsqrt(jnp.mean(widened * widened, axis=1, keepdims=True) + EPSILON)
        * norm_gain
    ).astype(BF)

    rows = lax.all_to_all(jnp.broadcast_to(normed[None], (16, 8, D)), "kv", 0, 0).reshape(128, D)
    block = shape((32, D), BF)
    mixed, *sent = call(
        mlp_kernel, [shape((32, D), F32), block, block, block], [SM, SM] + [VM] * 7, limit=28 << 20
    )(kv, tp, rows, gate_t, up_t, down_weight, *far)
    for part in [move_ring(value, k) for value, k in zip(sent, (2, 1, 3))]:
        mixed = mixed + part.astype(F32)
    mixed = mixed.astype(BF).reshape(16, 2, D)
    keep = lax.dynamic_slice_in_dim(widened, (tp[0] >> 1) * 2, 2, 0)
    mixed, keep = lax.optimization_barrier((mixed, keep))
    mixed = lax.all_to_all(mixed, ("kv", "tp"), 0, 0, axis_index_groups=PLANES)
    return (keep + jnp.sum(mixed.astype(F32), axis=0)).astype(BF)


def solution(mesh):
    return jax.shard_map(
        local,
        mesh=mesh,
        in_specs=(
            P(("kv", "tp"), None),
            P("kv", "tp"),
            P("kv", "tp"),
            P("kv", "tp"),
            P(),
            P(),
            P(),
            P("tp", None),
            P(),
            P(None, ("kv", "tp")),
            P(None, ("kv", "tp")),
            P(("kv", "tp"), None),
        ),
        out_specs=P(("kv", "tp"), None),
        check_vma=False,
    )
```

```python
import functools
import math

import jax
import jax.numpy as jnp
from jax import lax
from jax.experimental import pallas as pl
from jax.experimental.pallas import tpu as pltpu
from jax.sharding import PartitionSpec as P

QUERY_HEADS = 40
KEY_VALUE_HEADS = 8
HEAD_WIDTH = 128
GROUP = QUERY_HEADS // KEY_VALUE_HEADS
LOWEST = -(2.0**100)
SCALE = 1.0 / math.sqrt(HEAD_WIDTH)
EPSILON = 1e-06
BF = jnp.bfloat16
F32 = jnp.float32
D = 5120
VM = pltpu.VMEM
SM = pltpu.SMEM


def call(kernel, out_shape, in_spaces, scratch=(), limit=12 << 20, **kw):
    outs = out_shape if isinstance(out_shape, (list, tuple)) else [out_shape]
    specs = [pl.BlockSpec(memory_space=VM) for _ in outs]
    return pl.pallas_call(
        kernel,
        out_shape=out_shape,
        in_specs=[pl.BlockSpec(memory_space=s) for s in in_spaces],
        out_specs=specs if isinstance(out_shape, (list, tuple)) else specs[0],
        scratch_shapes=list(scratch),
        compiler_params=pltpu.CompilerParams(vmem_limit_bytes=limit),
        **kw,
    )


def nt(a, b):
    return lax.dot_general(a, b, (((1,), (1,)), ((), ())), preferred_element_type=F32)


def mm(a, b):
    return lax.dot_general(a, b, (((1,), (0,)), ((), ())), preferred_element_type=F32)


def prepare_kernel(lengths, parents, kv, leaf, keys, values, keys_wide, values_out, onehot, starts):
    nodes = lengths.shape[0]
    slots = keys.shape[0]
    tokens = leaf.shape[1]
    running = jnp.int32(0)
    for n in range(nodes):
        starts[n] = running
        running = running + lengths[n]
    lane = lax.broadcasted_iota(jnp.int32, (1, 128), 1)
    zero = jnp.zeros((1, 128), jnp.int32)
    own_lo, own_hi, up_lo, up_hi = zero, zero, zero, zero
    for n in range(nodes):
        lo = starts[n]
        up = parents[n]
        here = lane == n
        own_lo = jnp.where(here, lo, own_lo)
        own_hi = jnp.where(here, lo + lengths[n], own_hi)
        up_lo = jnp.where(here, starts[up], up_lo)
        up_hi = jnp.where(here, starts[up] + lengths[up], up_hi)
    slot = kv[0] * slots + lax.broadcasted_iota(jnp.int32, (slots, 128), 0)
    seen = (
        (slot < lengths[0])
        | ((slot >= own_lo) & (slot < own_hi))
        | ((slot >= up_lo) & (slot < up_hi))
    )
    keys_wide[:, :HEAD_WIDTH] = keys[...]
    keys_wide[:, HEAD_WIDTH:] = jnp.where(seen, 0.0, LOWEST).astype(BF)
    values_out[...] = values[...]
    node = lax.broadcasted_iota(jnp.int32, (128, tokens), 0)
    onehot[...] = jnp.where(node == leaf[...], 1.0, 0.0).astype(F32).T.astype(BF)


def attend_kernel(q, keys_wide, values, onehot, weight, out):
    tokens = q.shape[0]
    lane_t = lax.broadcasted_iota(jnp.int32, (tokens, 128), 1)
    stats = jnp.zeros((tokens, 128), F32)
    for g in range(GROUP):
        cols = pl.ds(g * HEAD_WIDTH, HEAD_WIDTH)
        q_wide = jnp.concatenate([q[:, cols], onehot[...]], axis=1)
        scores = nt(q_wide, keys_wide[...])
        top = jnp.max(scores, axis=1, keepdims=True).astype(BF).astype(F32)
        weights = jnp.exp((scores - top) * SCALE)
        mass = jnp.sum(weights, axis=1, keepdims=True)
        out[:, cols] = mm(weights.astype(BF), values[...]).astype(BF)
        high = mass.astype(BF).astype(F32)
        stats = jnp.where(lane_t == g, top, stats)
        stats = jnp.where(lane_t == GROUP + g, high, stats)
        stats = jnp.where(lane_t == 2 * GROUP + g, mass - high, stats)
    out[:, GROUP * HEAD_WIDTH :] = stats.astype(BF)


def project_kernel(tp, parts, weight, activations, own, other):
    z, core = tp[0] >> 1, tp[0] & 1
    sources = parts.shape[0]
    width = GROUP * HEAD_WIDTH
    stats = [parts[s, :, width:].astype(F32) for s in range(sources)]
    top = stats[0]
    for s in stats[1:]:
        top = jnp.maximum(top, s)
    scales = [jnp.exp((s - top) * SCALE) for s in stats]
    heads = []
    for g in range(GROUP):
        total = jnp.zeros((16, HEAD_WIDTH), F32)
        mass = jnp.zeros((16, 1), F32)
        for s in range(sources):
            scale = scales[s][:, g : g + 1]
            part = parts[s, :, g * HEAD_WIDTH : (g + 1) * HEAD_WIDTH].astype(F32)
            total = total + part * scale
            low = stats[s][:, GROUP + g : GROUP + g + 1] + stats[s][:, 2 * GROUP + g : 2 * GROUP + g + 1]
            mass = mass + low * scale
        heads.append((total / mass).astype(BF))
    context = jnp.concatenate(heads, axis=1)
    row = lax.broadcasted_iota(jnp.int32, (16, 16), 0)
    col = lax.broadcasted_iota(jnp.int32, (16, 16), 1)
    half = jnp.where(row < 8, core, 1 - core)
    source = (row % 8) // 2 * 4 + half * 2 + row % 2
    pick = jnp.where(col == source, 1.0, 0.0).astype(BF)
    context = mm(pick, context).astype(BF)
    result = mm(context, weight[...])
    row = lax.broadcasted_iota(jnp.int32, (8, 2), 0)
    col = lax.broadcasted_iota(jnp.int32, (8, 2), 1)
    place = jnp.where(row == z * 2 + col, 1.0, 0.0).astype(BF)
    own[...] = result[:8] + mm(place, activations[...])
    other[...] = result[8:].astype(BF)


def hidden_of(rows, gate, up):
    g = nt(rows, gate)
    u = nt(rows, up)
    return (g / (1.0 + jnp.exp(-g)) * u).astype(BF)


def ordered(hidden, kv, tp):
    n = hidden.shape[0]
    row = lax.broadcasted_iota(jnp.int32, (n, n), 0)
    col = lax.broadcasted_iota(jnp.int32, (n, n), 1)
    x, z, core = kv[0] >> 2, tp[0] >> 1, tp[0] & 1
    block = row // 32
    q = (row & 31) // 2
    places = jnp.where(block == 0, 0, jnp.where(block == 1, 2, jnp.where(block == 2, 1, 3)))
    along_z = q * 8 + ((z + places) & 3) * 2
    along_x = (((x + places) & 3) * 4 + q // 4) * 8 + (q & 3) * 2
    source = jnp.where(core == 0, along_z, along_x) + (row & 1)
    return mm(jnp.where(col == source, 1.0, 0.0).astype(BF), hidden).astype(BF)


def mlp_kernel(kv, tp, rows, gate, up, down, gate_far, up_far, down_far, own, *sent):
    near = ordered(hidden_of(rows[...], gate[...], up[...]), kv, tp)
    far = ordered(hidden_of(rows[...], gate_far[...], up_far[...]), kv, tp)
    result = mm(near, down[...]) + mm(far, down_far[...])
    own[...] = result[:32]
    for k, ref in enumerate(sent):
        ref[...] = result[32 * (k + 1) : 32 * (k + 2)].astype(BF)


def finish_kernel(tp, residual, parts, out):
    row = lax.broadcasted_iota(jnp.int32, (2, 8), 0)
    col = lax.broadcasted_iota(jnp.int32, (2, 8), 1)
    pick = jnp.where(col == (tp[0] >> 1) * 2 + row, 1.0, 0.0).astype(BF)
    total = mm(pick, residual[...])
    for k in range(parts.shape[0]):
        total = total + parts[k].astype(F32)
    out[...] = total.astype(BF)


def device(x, y, z, c):
    return (x * 4 + y) * 8 + z * 2 + c


def move_ring(value, k):
    pairs = [
        (device(x, y, z, c), device(x, y, (z + k) % 4, c) if c == 0 else device((x + k) % 4, y, z, c))
        for x in range(4)
        for y in range(4)
        for z in range(4)
        for c in range(2)
    ]
    return lax.ppermute(value, ("kv", "tp"), pairs)


PLANES = [[device(x, y, z, 0) for x in range(4) for y in range(4)] for z in range(4)] + [
    [device(x, y, z, 1) for y in range(4) for z in range(4)] for x in range(4)
]


def move_z(value, k):
    pairs = [(z * 2 + c, (z + k) % 4 * 2 + c) for z in range(4) for c in range(2)]
    return lax.ppermute(value, "tp", pairs)


def move_core(value):
    return lax.ppermute(value, "tp", [(i, i ^ 1) for i in range(8)])


def local(
    activations,
    queries,
    keys,
    values,
    parents,
    node_lengths,
    token_leaf,
    out_weight,
    norm_gain,
    gate_weight,
    up_weight,
    down_weight,
):
    kv = lax.axis_index("kv")[None]
    tp = lax.axis_index("tp")[None]
    gate_t, up_t = gate_weight.T, up_weight.T
    shape = jax.ShapeDtypeStruct
    far = [move_core(w) for w in (gate_t, up_t, down_weight)]
    queries, kv, tp = lax.optimization_barrier((queries, kv, tp))

    q = lax.all_to_all(jnp.broadcast_to(queries[None], (16, 16, 640)), "kv", 0, 0)
    keys_wide, values_in, onehot = call(
        prepare_kernel,
        [shape((keys.shape[0], 256), BF), shape(values.shape, BF), shape((256, 128), BF)],
        [SM, SM, SM, VM, VM, VM],
        [pltpu.SMEM((16,), jnp.int32)],
    )(node_lengths, parents, kv, token_leaf[None, :], keys, values)
    packed = call(attend_kernel, shape((256, 768), BF), [VM] * 4 + [pl.ANY], limit=48 << 20)(
        q.reshape(256, 640), keys_wide, values_in, onehot, out_weight
    )
    parts = lax.all_to_all(packed.reshape(16, 16, 768), "kv", 0, 0)
    own, other = call(project_kernel, [shape((8, D), F32), shape((8, D), BF)], [SM, VM, VM, VM])(
        tp, parts, out_weight, activations
    )
    attended = own + move_core(other).astype(F32)
    sent = attended.astype(BF)
    for part in [move_z(sent, k) for k in (1, 3, 2)]:
        attended = attended + part.astype(F32)
    residual = attended.astype(BF)
    widened = residual.astype(F32)
    normed = (
        widened
        * lax.rsqrt(jnp.mean(widened * widened, axis=1, keepdims=True) + EPSILON)
        * norm_gain
    ).astype(BF)

    rows = lax.all_to_all(jnp.broadcast_to(normed[None], (16, 8, D)), "kv", 0, 0).reshape(128, D)
    block = shape((32, D), BF)
    mixed, *sent = call(
        mlp_kernel, [shape((32, D), F32), block, block, block], [SM, SM] + [VM] * 7, limit=28 << 20
    )(kv, tp, rows, gate_t, up_t, down_weight, *far)
    for part in [move_ring(value, k) for value, k in zip(sent, (2, 1, 3))]:
        mixed = mixed + part.astype(F32)
    mixed = mixed.astype(BF).reshape(16, 2, D)
    mixed = lax.all_to_all(mixed, ("kv", "tp"), 0, 0, axis_index_groups=PLANES)
    return call(finish_kernel, shape((2, D), BF), [SM, VM, VM])(tp, residual, mixed)


def solution(mesh):
    return jax.shard_map(
        local,
        mesh=mesh,
        in_specs=(
            P(("kv", "tp"), None),
            P("kv", "tp"),
            P("kv", "tp"),
            P("kv", "tp"),
            P(),
            P(),
            P(),
            P("tp", None),
            P(),
            P(None, ("kv", "tp")),
            P(None, ("kv", "tp")),
            P(("kv", "tp"), None),
        ),
        out_specs=P(("kv", "tp"), None),
        check_vma=False,
    )
```

```python
import functools
import math

import jax
import jax.numpy as jnp
from jax import lax
from jax.experimental import pallas as pl
from jax.experimental.pallas import tpu as pltpu
from jax.sharding import PartitionSpec as P

QUERY_HEADS = 40
KEY_VALUE_HEADS = 8
HEAD_WIDTH = 128
GROUP = QUERY_HEADS // KEY_VALUE_HEADS
LOWEST = -(2.0**100)
SCALE = 1.0 / math.sqrt(HEAD_WIDTH)
EPSILON = 1e-06
BF = jnp.bfloat16
F32 = jnp.float32
D = 5120
VM = pltpu.VMEM
SM = pltpu.SMEM


def call(kernel, out_shape, in_spaces, scratch=(), limit=12 << 20, **kw):
    outs = out_shape if isinstance(out_shape, (list, tuple)) else [out_shape]
    specs = [pl.BlockSpec(memory_space=VM) for _ in outs]
    return pl.pallas_call(
        kernel,
        out_shape=out_shape,
        in_specs=[pl.BlockSpec(memory_space=s) for s in in_spaces],
        out_specs=specs if isinstance(out_shape, (list, tuple)) else specs[0],
        scratch_shapes=list(scratch),
        compiler_params=pltpu.CompilerParams(vmem_limit_bytes=limit),
        **kw,
    )


def nt(a, b):
    return lax.dot_general(a, b, (((1,), (1,)), ((), ())), preferred_element_type=F32)


def mm(a, b):
    return lax.dot_general(a, b, (((1,), (0,)), ((), ())), preferred_element_type=F32)


def prepare_kernel(lengths, parents, kv, leaf, keys, values, keys_wide, values_out, onehot, starts):
    nodes = lengths.shape[0]
    slots = keys.shape[0]
    tokens = leaf.shape[1]
    running = jnp.int32(0)
    for n in range(nodes):
        starts[n] = running
        running = running + lengths[n]
    lane = lax.broadcasted_iota(jnp.int32, (1, 128), 1)
    zero = jnp.zeros((1, 128), jnp.int32)
    own_lo, own_hi, up_lo, up_hi = zero, zero, zero, zero
    for n in range(nodes):
        lo = starts[n]
        up = parents[n]
        here = lane == n
        own_lo = jnp.where(here, lo, own_lo)
        own_hi = jnp.where(here, lo + lengths[n], own_hi)
        up_lo = jnp.where(here, starts[up], up_lo)
        up_hi = jnp.where(here, starts[up] + lengths[up], up_hi)
    slot = kv[0] * slots + lax.broadcasted_iota(jnp.int32, (slots, 128), 0)
    seen = (
        (slot < lengths[0])
        | ((slot >= own_lo) & (slot < own_hi))
        | ((slot >= up_lo) & (slot < up_hi))
    )
    keys_wide[:, :HEAD_WIDTH] = keys[...]
    keys_wide[:, HEAD_WIDTH:] = jnp.where(seen, 0.0, LOWEST).astype(BF)
    values_out[...] = values[...]
    node = lax.broadcasted_iota(jnp.int32, (128, tokens), 0)
    onehot[...] = jnp.where(node == leaf[...], 1.0, 0.0).astype(F32).T.astype(BF)


def attend_kernel(q, keys_wide, values, onehot, weight, out):
    tokens = q.shape[0]
    lane_t = lax.broadcasted_iota(jnp.int32, (tokens, 128), 1)
    stats = jnp.zeros((tokens, 128), F32)
    for g in range(GROUP):
        cols = pl.ds(g * HEAD_WIDTH, HEAD_WIDTH)
        q_wide = jnp.concatenate([q[:, cols], onehot[...]], axis=1)
        scores = nt(q_wide, keys_wide[...])
        top = jnp.max(scores, axis=1, keepdims=True).astype(BF).astype(F32)
        weights = jnp.exp((scores - top) * SCALE)
        mass = jnp.sum(weights, axis=1, keepdims=True)
        out[:, cols] = mm(weights.astype(BF), values[...]).astype(BF)
        high = mass.astype(BF).astype(F32)
        stats = jnp.where(lane_t == g, top, stats)
        stats = jnp.where(lane_t == GROUP + g, high, stats)
        stats = jnp.where(lane_t == 2 * GROUP + g, mass - high, stats)
    out[:, GROUP * HEAD_WIDTH :] = stats.astype(BF)


def project_kernel(tp, parts, weight, activations, *refs):
    own, other = refs[-2:]
    z, core = tp[0] >> 1, tp[0] & 1
    sources = parts.shape[0]
    width = GROUP * HEAD_WIDTH
    stats = [parts[s, :, width:].astype(F32) for s in range(sources)]
    top = stats[0]
    for s in stats[1:]:
        top = jnp.maximum(top, s)
    scales = [jnp.exp((s - top) * SCALE) for s in stats]
    heads = []
    for g in range(GROUP):
        total = jnp.zeros((16, HEAD_WIDTH), F32)
        mass = jnp.zeros((16, 1), F32)
        for s in range(sources):
            scale = scales[s][:, g : g + 1]
            part = parts[s, :, g * HEAD_WIDTH : (g + 1) * HEAD_WIDTH].astype(F32)
            total = total + part * scale
            low = stats[s][:, GROUP + g : GROUP + g + 1] + stats[s][:, 2 * GROUP + g : 2 * GROUP + g + 1]
            mass = mass + low * scale
        heads.append((total / mass).astype(BF))
    context = jnp.concatenate(heads, axis=1)
    row = lax.broadcasted_iota(jnp.int32, (16, 16), 0)
    col = lax.broadcasted_iota(jnp.int32, (16, 16), 1)
    half = jnp.where(row < 8, core, 1 - core)
    source = (row % 8) // 2 * 4 + half * 2 + row % 2
    pick = jnp.where(col == source, 1.0, 0.0).astype(BF)
    context = mm(pick, context).astype(BF)
    result = mm(context, weight[...])
    row = lax.broadcasted_iota(jnp.int32, (8, 2), 0)
    col = lax.broadcasted_iota(jnp.int32, (8, 2), 1)
    place = jnp.where(row == z * 2 + col, 1.0, 0.0).astype(BF)
    own[...] = result[:8] + mm(place, activations[...])
    other[...] = result[8:].astype(BF)


def hidden_of(rows, gate, up):
    g = nt(rows, gate)
    u = nt(rows, up)
    return (g / (1.0 + jnp.exp(-g)) * u).astype(BF)


def ordered(hidden, kv, tp):
    n = hidden.shape[0]
    row = lax.broadcasted_iota(jnp.int32, (n, n), 0)
    col = lax.broadcasted_iota(jnp.int32, (n, n), 1)
    here = jnp.where((tp[0] & 1) == 0, kv[0] & 3, kv[0] >> 2)
    places = (here + 4 - (row & 31) // 8) & 3
    source = row // 32 * 32 + places * 8 + (row & 7)
    return mm(jnp.where(col == source, 1.0, 0.0).astype(BF), hidden).astype(BF)


def mlp_kernel(kv, tp, gate, up, down, gate_far, up_far, down_far, *refs):
    blocks = len(refs) // 2
    rows = jnp.concatenate([ref[...] for ref in refs[:blocks]], axis=0) if blocks > 1 else refs[0][...]
    near = ordered(hidden_of(rows, gate[...], up[...]), kv, tp)
    far = ordered(hidden_of(rows, gate_far[...], up_far[...]), kv, tp)
    result = mm(near, down[...]) + mm(far, down_far[...])
    for k, ref in enumerate(refs[blocks:]):
        ref[...] = result[32 * k : 32 * (k + 1)].astype(ref.dtype)


def stack_kernel(*refs):
    for k, ref in enumerate(refs[:-1]):
        refs[-1][8 * k : 8 * (k + 1)] = ref[...]


def finish_kernel(tp, residual, parts, out):
    row = lax.broadcasted_iota(jnp.int32, (2, 8), 0)
    col = lax.broadcasted_iota(jnp.int32, (2, 8), 1)
    pick = jnp.where(col == (tp[0] >> 1) * 2 + row, 1.0, 0.0).astype(BF)
    total = mm(pick, residual[...])
    for k in range(parts.shape[0]):
        total = total + parts[k].astype(F32)
    out[...] = total.astype(BF)


def device(x, y, z, c):
    return (x * 4 + y) * 8 + z * 2 + c


def move_along(value, k, first):
    pairs = [
        (device(x, y, z, c), device(x, (y + k) % 4, z, c) if (c == 0) == first else device((x + k) % 4, y, z, c))
        for x in range(4)
        for y in range(4)
        for z in range(4)
        for c in range(2)
    ]
    return lax.ppermute(value, ("kv", "tp"), pairs)


PLANES = [[device(x, y, z, 0) for y in range(4) for z in range(4)] for x in range(4)] + [
    [device(x, y, z, 1) for x in range(4) for z in range(4)] for y in range(4)
]


def move_z(value, k):
    pairs = [(z * 2 + c, (z + k) % 4 * 2 + c) for z in range(4) for c in range(2)]
    return lax.ppermute(value, "tp", pairs)


def move_core(value):
    return lax.ppermute(value, "tp", [(i, i ^ 1) for i in range(8)])


def local(
    activations,
    queries,
    keys,
    values,
    parents,
    node_lengths,
    token_leaf,
    out_weight,
    norm_gain,
    gate_weight,
    up_weight,
    down_weight,
):
    kv = lax.axis_index("kv")[None]
    tp = lax.axis_index("tp")[None]
    gate_t, up_t = gate_weight.T, up_weight.T
    shape = jax.ShapeDtypeStruct
    queries, kv, tp = lax.optimization_barrier((queries, kv, tp))

    q = lax.all_to_all(jnp.broadcast_to(queries[None], (16, 16, 640)), "kv", 0, 0)
    keys_wide, values_in, onehot = call(
        prepare_kernel,
        [shape((keys.shape[0], 256), BF), shape(values.shape, BF), shape((256, 128), BF)],
        [SM, SM, SM, VM, VM, VM],
        [pltpu.SMEM((16,), jnp.int32)],
    )(node_lengths, parents, kv, token_leaf[None, :], keys, values)
    q, keys_wide, values_in, onehot, *far = lax.optimization_barrier(
        (q, keys_wide, values_in, onehot, gate_t, up_t, down_weight)
    )
    far = [move_core(w) for w in far]
    packed = call(attend_kernel, shape((256, 768), BF), [VM] * 4 + [pl.ANY], limit=48 << 20)(
        q.reshape(256, 640), keys_wide, values_in, onehot, out_weight
    )
    parts = lax.all_to_all(packed.reshape(16, 16, 768), "kv", 0, 0)
    own, other = call(project_kernel, [shape((8, D), F32), shape((8, D), BF)], [SM, VM, VM, VM] + [pl.ANY] * 3)(
        tp, parts, out_weight, activations, *far
    )
    attended = own + move_core(other).astype(F32)
    sent = attended.astype(BF)
    for part in [move_z(sent, k) for k in (1, 3, 2)]:
        attended = attended + part.astype(F32)
    residual = attended.astype(BF)
    widened = residual.astype(F32)
    normed = (
        widened
        * lax.rsqrt(jnp.mean(widened * widened, axis=1, keepdims=True) + EPSILON)
        * norm_gain
    ).astype(BF)

    back = {k: move_along(normed, k, True) for k in (2, 1, 3)}
    rows = call(stack_kernel, shape((32, D), BF), [VM] * 4)(normed, back[1], back[2], back[3])
    weights = (kv, tp, gate_t, up_t, down_weight, *far)
    block, wide = shape((32, D), BF), shape((32, D), F32)
    back = {k: move_along(rows, k, False) for k in (1, 3, 2)}
    mixed = call(mlp_kernel, wide, [SM, SM] + [VM] * 7, limit=28 << 20)(*weights, rows)
    near = lax.optimization_barrier((back[1], back[3], mixed))
    mixed = near[2]
    ahead, behind = call(mlp_kernel, [block, block], [SM, SM] + [VM] * 8, limit=28 << 20)(*weights, near[0], near[1])
    opposite, ahead, behind = lax.optimization_barrier((back[2], ahead, behind))
    opposite = call(mlp_kernel, block, [SM, SM] + [VM] * 7, limit=28 << 20)(*weights, opposite)
    for part in [move_along(ahead, 3, False), move_along(behind, 1, False), move_along(opposite, 2, False)]:
        mixed = mixed + part.astype(F32)
    mixed = mixed.astype(BF).reshape(16, 2, D)
    mixed = lax.all_to_all(mixed, ("kv", "tp"), 0, 0, axis_index_groups=PLANES)
    return call(finish_kernel, shape((2, D), BF), [SM, VM, VM])(tp, residual, mixed)


def solution(mesh):
    return jax.shard_map(
        local,
        mesh=mesh,
        in_specs=(
            P(("kv", "tp"), None),
            P("kv", "tp"),
            P("kv", "tp"),
            P("kv", "tp"),
            P(),
            P(),
            P(),
            P("tp", None),
            P(),
            P(None, ("kv", "tp")),
            P(None, ("kv", "tp")),
            P(("kv", "tp"), None),
        ),
        out_specs=P(("kv", "tp"), None),
        check_vma=False,
    )
```

```python
import functools
import math

import jax
import jax.numpy as jnp
from jax import lax
from jax.experimental import pallas as pl
from jax.experimental.pallas import tpu as pltpu
from jax.sharding import PartitionSpec as P

QUERY_HEADS = 40
KEY_VALUE_HEADS = 8
HEAD_WIDTH = 128
GROUP = QUERY_HEADS // KEY_VALUE_HEADS
LOWEST = -(2.0**100)
SCALE = 1.0 / math.sqrt(HEAD_WIDTH)
EPSILON = 1e-06
BF = jnp.bfloat16
F32 = jnp.float32
D = 5120
VM = pltpu.VMEM
SM = pltpu.SMEM


def call(kernel, out_shape, in_spaces, scratch=(), limit=12 << 20, **kw):
    outs = out_shape if isinstance(out_shape, (list, tuple)) else [out_shape]
    specs = [pl.BlockSpec(memory_space=VM) for _ in outs]
    return pl.pallas_call(
        kernel,
        out_shape=out_shape,
        in_specs=[pl.BlockSpec(memory_space=s) for s in in_spaces],
        out_specs=specs if isinstance(out_shape, (list, tuple)) else specs[0],
        scratch_shapes=list(scratch),
        compiler_params=pltpu.CompilerParams(vmem_limit_bytes=limit),
        **kw,
    )


def nt(a, b):
    return lax.dot_general(a, b, (((1,), (1,)), ((), ())), preferred_element_type=F32)


def mm(a, b):
    return lax.dot_general(a, b, (((1,), (0,)), ((), ())), preferred_element_type=F32)


def prepare_kernel(lengths, parents, kv, leaf, keys, values, keys_wide, values_out, onehot, starts):
    nodes = lengths.shape[0]
    slots = keys.shape[0]
    tokens = leaf.shape[1]
    running = jnp.int32(0)
    for n in range(nodes):
        starts[n] = running
        running = running + lengths[n]
    lane = lax.broadcasted_iota(jnp.int32, (1, 128), 1)
    zero = jnp.zeros((1, 128), jnp.int32)
    own_lo, own_hi, up_lo, up_hi = zero, zero, zero, zero
    for n in range(nodes):
        lo = starts[n]
        up = parents[n]
        here = lane == n
        own_lo = jnp.where(here, lo, own_lo)
        own_hi = jnp.where(here, lo + lengths[n], own_hi)
        up_lo = jnp.where(here, starts[up], up_lo)
        up_hi = jnp.where(here, starts[up] + lengths[up], up_hi)
    slot = kv[0] * slots + lax.broadcasted_iota(jnp.int32, (slots, 128), 0)
    seen = (
        (slot < lengths[0])
        | ((slot >= own_lo) & (slot < own_hi))
        | ((slot >= up_lo) & (slot < up_hi))
    )
    keys_wide[:, :HEAD_WIDTH] = keys[...]
    keys_wide[:, HEAD_WIDTH:] = jnp.where(seen, 0.0, LOWEST).astype(BF)
    values_out[...] = values[...]
    node = lax.broadcasted_iota(jnp.int32, (128, tokens), 0)
    onehot[...] = jnp.where(node == leaf[...], 1.0, 0.0).astype(F32).T.astype(BF)


def attend_kernel(q, keys_wide, values, onehot, weight, out):
    tokens = q.shape[0]
    lane_t = lax.broadcasted_iota(jnp.int32, (tokens, 128), 1)
    stats = jnp.zeros((tokens, 128), F32)
    for g in range(GROUP):
        cols = pl.ds(g * HEAD_WIDTH, HEAD_WIDTH)
        q_wide = jnp.concatenate([q[:, cols], onehot[...]], axis=1)
        scores = nt(q_wide, keys_wide[...])
        top = jnp.max(scores, axis=1, keepdims=True).astype(BF).astype(F32)
        weights = jnp.exp((scores - top) * SCALE)
        mass = jnp.sum(weights, axis=1, keepdims=True)
        out[:, cols] = mm(weights.astype(BF), values[...]).astype(BF)
        high = mass.astype(BF).astype(F32)
        stats = jnp.where(lane_t == g, top, stats)
        stats = jnp.where(lane_t == GROUP + g, high, stats)
        stats = jnp.where(lane_t == 2 * GROUP + g, mass - high, stats)
    out[:, GROUP * HEAD_WIDTH :] = stats.astype(BF)


def project_kernel(tp, parts, weight, activations, own, other):
    z, core = tp[0] >> 1, tp[0] & 1
    sources = parts.shape[0]
    width = GROUP * HEAD_WIDTH
    stats = [parts[s, :, width:].astype(F32) for s in range(sources)]
    top = stats[0]
    for s in stats[1:]:
        top = jnp.maximum(top, s)
    scales = [jnp.exp((s - top) * SCALE) for s in stats]
    heads = []
    for g in range(GROUP):
        total = jnp.zeros((16, HEAD_WIDTH), F32)
        mass = jnp.zeros((16, 1), F32)
        for s in range(sources):
            scale = scales[s][:, g : g + 1]
            part = parts[s, :, g * HEAD_WIDTH : (g + 1) * HEAD_WIDTH].astype(F32)
            total = total + part * scale
            low = stats[s][:, GROUP + g : GROUP + g + 1] + stats[s][:, 2 * GROUP + g : 2 * GROUP + g + 1]
            mass = mass + low * scale
        heads.append((total / mass).astype(BF))
    context = jnp.concatenate(heads, axis=1)
    row = lax.broadcasted_iota(jnp.int32, (16, 16), 0)
    col = lax.broadcasted_iota(jnp.int32, (16, 16), 1)
    half = jnp.where(row < 8, core, 1 - core)
    source = (row % 8) // 2 * 4 + half * 2 + row % 2
    pick = jnp.where(col == source, 1.0, 0.0).astype(BF)
    context = mm(pick, context).astype(BF)
    result = mm(context, weight[...])
    row = lax.broadcasted_iota(jnp.int32, (8, 2), 0)
    col = lax.broadcasted_iota(jnp.int32, (8, 2), 1)
    place = jnp.where(row == z * 2 + col, 1.0, 0.0).astype(BF)
    own[...] = result[:8] + mm(place, activations[...])
    other[...] = result[8:].astype(BF)


def hidden_of(rows, gate, up):
    g = nt(rows, gate)
    u = nt(rows, up)
    return (g / (1.0 + jnp.exp(-g)) * u).astype(BF)


def ordered(hidden, kv, tp):
    n = hidden.shape[0]
    row = lax.broadcasted_iota(jnp.int32, (n, n), 0)
    col = lax.broadcasted_iota(jnp.int32, (n, n), 1)
    here = jnp.where((tp[0] & 1) == 0, kv[0] & 3, kv[0] >> 2)
    places = (here + 4 - (row & 31) // 8) & 3
    source = row // 32 * 32 + places * 8 + (row & 7)
    return mm(jnp.where(col == source, 1.0, 0.0).astype(BF), hidden).astype(BF)


def mlp_kernel(kv, tp, gate, up, down, gate_far, up_far, down_far, *refs):
    blocks = len(refs) // 2
    rows = jnp.concatenate([ref[...] for ref in refs[:blocks]], axis=0) if blocks > 1 else refs[0][...]
    near = ordered(hidden_of(rows, gate[...], up[...]), kv, tp)
    far = ordered(hidden_of(rows, gate_far[...], up_far[...]), kv, tp)
    result = mm(near, down[...]) + mm(far, down_far[...])
    for k, ref in enumerate(refs[blocks:]):
        ref[...] = result[32 * k : 32 * (k + 1)].astype(ref.dtype)


def stack_kernel(*refs):
    for k, ref in enumerate(refs[:-1]):
        refs[-1][8 * k : 8 * (k + 1)] = ref[...]


def finish_kernel(tp, residual, parts, out):
    row = lax.broadcasted_iota(jnp.int32, (2, 8), 0)
    col = lax.broadcasted_iota(jnp.int32, (2, 8), 1)
    pick = jnp.where(col == (tp[0] >> 1) * 2 + row, 1.0, 0.0).astype(BF)
    total = mm(pick, residual[...])
    for k in range(parts.shape[0]):
        total = total + parts[k].astype(F32)
    out[...] = total.astype(BF)


def device(x, y, z, c):
    return (x * 4 + y) * 8 + z * 2 + c


def move_along(value, k, first):
    pairs = [
        (device(x, y, z, c), device(x, (y + k) % 4, z, c) if (c == 0) == first else device((x + k) % 4, y, z, c))
        for x in range(4)
        for y in range(4)
        for z in range(4)
        for c in range(2)
    ]
    return lax.ppermute(value, ("kv", "tp"), pairs)


PLANES = [[device(x, y, z, 0) for y in range(4) for z in range(4)] for x in range(4)] + [
    [device(x, y, z, 1) for x in range(4) for z in range(4)] for y in range(4)
]


def move_z(value, k):
    pairs = [(z * 2 + c, (z + k) % 4 * 2 + c) for z in range(4) for c in range(2)]
    return lax.ppermute(value, "tp", pairs)


def move_core(value):
    return lax.ppermute(value, "tp", [(i, i ^ 1) for i in range(8)])


def local(
    activations,
    queries,
    keys,
    values,
    parents,
    node_lengths,
    token_leaf,
    out_weight,
    norm_gain,
    gate_weight,
    up_weight,
    down_weight,
):
    kv = lax.axis_index("kv")[None]
    tp = lax.axis_index("tp")[None]
    gate_t, up_t = gate_weight.T, up_weight.T
    shape = jax.ShapeDtypeStruct
    queries, kv, tp = lax.optimization_barrier((queries, kv, tp))

    q = lax.all_to_all(jnp.broadcast_to(queries[None], (16, 16, 640)), "kv", 0, 0)
    keys_wide, values_in, onehot = call(
        prepare_kernel,
        [shape((keys.shape[0], 256), BF), shape(values.shape, BF), shape((256, 128), BF)],
        [SM, SM, SM, VM, VM, VM],
        [pltpu.SMEM((16,), jnp.int32)],
    )(node_lengths, parents, kv, token_leaf[None, :], keys, values)
    packed = call(attend_kernel, shape((256, 768), BF), [VM] * 4 + [pl.ANY], limit=48 << 20)(
        q.reshape(256, 640), keys_wide, values_in, onehot, out_weight
    )
    parts = lax.all_to_all(packed.reshape(16, 16, 768), "kv", 0, 0)
    own, other = call(project_kernel, [shape((8, D), F32), shape((8, D), BF)], [SM, VM, VM, VM])(
        tp, parts, out_weight, activations
    )
    attended = own + move_core(other).astype(F32)
    sent, gate_far = lax.optimization_barrier((attended.astype(BF), gate_t))
    gate_far = move_core(gate_far)
    for part in [move_z(sent, k) for k in (1, 3, 2)]:
        attended = attended + part.astype(F32)
    residual = attended.astype(BF)
    widened = residual.astype(F32)
    normed = (
        widened
        * lax.rsqrt(jnp.mean(widened * widened, axis=1, keepdims=True) + EPSILON)
        * norm_gain
    ).astype(BF)

    normed, gate_far, up_far = lax.optimization_barrier((normed, gate_far, up_t))
    up_far = move_core(up_far)
    back = {k: move_along(normed, k, True) for k in (2, 1, 3)}
    rows = call(stack_kernel, shape((32, D), BF), [VM] * 4)(normed, back[1], back[2], back[3])
    rows, up_far, down_far = lax.optimization_barrier((rows, up_far, down_weight))
    weights = (kv, tp, gate_t, up_t, down_weight, gate_far, up_far, move_core(down_far))
    cost = pl.CostEstimate(flops=12 * 32 * gate_t.size, transcendentals=0, bytes_accessed=12 * gate_t.size)
    block, wide = shape((32, D), BF), shape((32, D), F32)
    back = {k: move_along(rows, k, False) for k in (1, 3, 2)}
    mixed, ahead, behind = call(mlp_kernel, [wide, block, block], [SM, SM] + [VM] * 9, limit=28 << 20)(
        *weights, rows, back[1], back[3]
    )
    opposite, ahead, behind = lax.optimization_barrier((back[2], ahead, behind))
    opposite = call(mlp_kernel, block, [SM, SM] + [VM] * 7, limit=28 << 20, cost_estimate=cost)(*weights, opposite)
    for part in [move_along(ahead, 3, False), move_along(behind, 1, False)]:
        mixed = mixed + part.astype(F32)
    mixed = lax.optimization_barrier(mixed) + move_along(opposite, 2, False).astype(F32)
    mixed = mixed.astype(BF).reshape(16, 2, D)
    mixed = lax.all_to_all(mixed, ("kv", "tp"), 0, 0, axis_index_groups=PLANES)
    return call(finish_kernel, shape((2, D), BF), [SM, VM, VM])(tp, residual, mixed)


def solution(mesh):
    return jax.shard_map(
        local,
        mesh=mesh,
        in_specs=(
            P(("kv", "tp"), None),
            P("kv", "tp"),
            P("kv", "tp"),
            P("kv", "tp"),
            P(),
            P(),
            P(),
            P("tp", None),
            P(),
            P(None, ("kv", "tp")),
            P(None, ("kv", "tp")),
            P(("kv", "tp"), None),
        ),
        out_specs=P(("kv", "tp"), None),
        check_vma=False,
    )
```

```python
import functools
import math

import jax
import jax.numpy as jnp
from jax import lax
from jax.experimental import pallas as pl
from jax.experimental.pallas import tpu as pltpu
from jax.sharding import PartitionSpec as P

QUERY_HEADS = 40
KEY_VALUE_HEADS = 8
HEAD_WIDTH = 128
GROUP = QUERY_HEADS // KEY_VALUE_HEADS
LOWEST = -(2.0**100)
SCALE = 1.0 / math.sqrt(HEAD_WIDTH)
EPSILON = 1e-06
BF = jnp.bfloat16
F32 = jnp.float32
D = 5120
VM = pltpu.VMEM
SM = pltpu.SMEM


def call(kernel, out_shape, in_spaces, scratch=(), limit=12 << 20, **kw):
    outs = out_shape if isinstance(out_shape, (list, tuple)) else [out_shape]
    specs = [pl.BlockSpec(memory_space=VM) for _ in outs]
    return pl.pallas_call(
        kernel,
        out_shape=out_shape,
        in_specs=[pl.BlockSpec(memory_space=s) for s in in_spaces],
        out_specs=specs if isinstance(out_shape, (list, tuple)) else specs[0],
        scratch_shapes=list(scratch),
        compiler_params=pltpu.CompilerParams(vmem_limit_bytes=limit),
        **kw,
    )


def nt(a, b):
    return lax.dot_general(a, b, (((1,), (1,)), ((), ())), preferred_element_type=F32)


def mm(a, b):
    return lax.dot_general(a, b, (((1,), (0,)), ((), ())), preferred_element_type=F32)


def repeat_kernel(rows, out, sem):
    copies = [pltpu.make_async_copy(rows, out.at[k], sem.at[k]) for k in range(out.shape[0])]
    for copy in copies:
        copy.start()
    for copy in copies:
        copy.wait()


def prepare_kernel(kv, tables, keys, values, keys_wide, values_out, onehot):
    slots = keys.shape[0]
    tokens = onehot.shape[0]
    row = lax.broadcasted_iota(jnp.int32, (128, 128), 0)
    col = lax.broadcasted_iota(jnp.int32, (128, 128), 1)
    leaf = tables[:, :tokens]
    lengths = tables[:, tokens : tokens + 128]
    parents = tables[:, tokens + 128 :]

    def upright(lanes):
        return jnp.sum(jnp.where(row == col, lanes, 0), axis=1, keepdims=True)

    own_lo = jnp.sum(jnp.where(row < col, upright(lengths), 0), axis=0, keepdims=True)
    own_hi = own_lo + lengths
    up_lo = jnp.sum(jnp.where(row == parents, upright(own_lo), 0), axis=0, keepdims=True)
    up_hi = jnp.sum(jnp.where(row == parents, upright(own_hi), 0), axis=0, keepdims=True)
    root = own_hi[:, :1]
    slot = kv[0] * slots + lax.broadcasted_iota(jnp.int32, (slots, 128), 0)
    seen = (
        (slot < root)
        | ((slot >= own_lo) & (slot < own_hi))
        | ((slot >= up_lo) & (slot < up_hi))
    )
    keys_wide[:, :HEAD_WIDTH] = keys[...]
    keys_wide[:, HEAD_WIDTH:] = jnp.where(seen, 0.0, LOWEST).astype(BF)
    values_out[...] = values[...]
    node = lax.broadcasted_iota(jnp.int32, (128, tokens), 0)
    onehot[...] = jnp.where(node == leaf, 1.0, 0.0).astype(F32).T.astype(BF)


def attend_kernel(q, keys_wide, values, onehot, weight, out):
    tokens = q.shape[0]
    lane_t = lax.broadcasted_iota(jnp.int32, (tokens, 128), 1)
    stats = jnp.zeros((tokens, 128), F32)
    for g in range(GROUP):
        cols = pl.ds(g * HEAD_WIDTH, HEAD_WIDTH)
        q_wide = jnp.concatenate([q[:, cols], onehot[...]], axis=1)
        scores = nt(q_wide, keys_wide[...])
        top = jnp.max(scores, axis=1, keepdims=True).astype(BF).astype(F32)
        weights = jnp.exp((scores - top) * SCALE)
        mass = jnp.sum(weights, axis=1, keepdims=True)
        out[:, cols] = mm(weights.astype(BF), values[...]).astype(BF)
        high = mass.astype(BF).astype(F32)
        stats = jnp.where(lane_t == g, top, stats)
        stats = jnp.where(lane_t == GROUP + g, high, stats)
        stats = jnp.where(lane_t == 2 * GROUP + g, mass - high, stats)
    out[:, GROUP * HEAD_WIDTH :] = stats.astype(BF)


def project_kernel(tp, parts, weight, activations, own, other):
    z, core = tp[0] >> 1, tp[0] & 1
    sources = parts.shape[0]
    width = GROUP * HEAD_WIDTH
    stats = [parts[s, :, width:].astype(F32) for s in range(sources)]
    top = stats[0]
    for s in stats[1:]:
        top = jnp.maximum(top, s)
    scales = [jnp.exp((s - top) * SCALE) for s in stats]
    heads = []
    for g in range(GROUP):
        total = jnp.zeros((16, HEAD_WIDTH), F32)
        mass = jnp.zeros((16, 1), F32)
        for s in range(sources):
            scale = scales[s][:, g : g + 1]
            part = parts[s, :, g * HEAD_WIDTH : (g + 1) * HEAD_WIDTH].astype(F32)
            total = total + part * scale
            low = stats[s][:, GROUP + g : GROUP + g + 1] + stats[s][:, 2 * GROUP + g : 2 * GROUP + g + 1]
            mass = mass + low * scale
        heads.append((total / mass).astype(BF))
    context = jnp.concatenate(heads, axis=1)
    row = lax.broadcasted_iota(jnp.int32, (16, 16), 0)
    col = lax.broadcasted_iota(jnp.int32, (16, 16), 1)
    half = jnp.where(row < 8, core, 1 - core)
    source = (row % 8) // 2 * 4 + half * 2 + row % 2
    pick = jnp.where(col == source, 1.0, 0.0).astype(BF)
    context = mm(pick, context).astype(BF)
    result = mm(context, weight[...])
    row = lax.broadcasted_iota(jnp.int32, (8, 2), 0)
    col = lax.broadcasted_iota(jnp.int32, (8, 2), 1)
    place = jnp.where(row == z * 2 + col, 1.0, 0.0).astype(BF)
    own[...] = result[:8] + mm(place, activations[...])
    other[...] = result[8:].astype(BF)


def hidden_of(rows, gate, up):
    g = nt(rows, gate)
    u = nt(rows, up)
    return (g / (1.0 + jnp.exp(-g)) * u).astype(BF)


def ordered(hidden, kv, tp):
    n = hidden.shape[0]
    row = lax.broadcasted_iota(jnp.int32, (n, n), 0)
    col = lax.broadcasted_iota(jnp.int32, (n, n), 1)
    x, z, core = kv[0] >> 2, tp[0] >> 1, tp[0] & 1
    block = row // 32
    q = (row & 31) // 2
    places = jnp.where(block == 0, 0, jnp.where(block == 1, 2, jnp.where(block == 2, 1, 3)))
    along_z = q * 8 + ((z + places) & 3) * 2
    along_x = (((x + places) & 3) * 4 + q // 4) * 8 + (q & 3) * 2
    source = jnp.where(core == 0, along_z, along_x) + (row & 1)
    return mm(jnp.where(col == source, 1.0, 0.0).astype(BF), hidden).astype(BF)


def mlp_kernel(kv, tp, rows, gate, up, down, gate_far, up_far, down_far, own, *sent):
    near = ordered(hidden_of(rows[...], gate[...], up[...]), kv, tp)
    far = ordered(hidden_of(rows[...], gate_far[...], up_far[...]), kv, tp)
    result = mm(near, down[...]) + mm(far, down_far[...])
    own[...] = result[:32]
    for k, ref in enumerate(sent):
        ref[...] = result[32 * (k + 1) : 32 * (k + 2)].astype(BF)


def finish_kernel(tp, residual, parts, out):
    row = lax.broadcasted_iota(jnp.int32, (2, 8), 0)
    col = lax.broadcasted_iota(jnp.int32, (2, 8), 1)
    pick = jnp.where(col == (tp[0] >> 1) * 2 + row, 1.0, 0.0).astype(BF)
    total = mm(pick, residual[...])
    for k in range(parts.shape[0]):
        total = total + parts[k].astype(F32)
    out[...] = total.astype(BF)


def device(x, y, z, c):
    return (x * 4 + y) * 8 + z * 2 + c


def move_ring(value, k):
    pairs = [
        (device(x, y, z, c), device(x, y, (z + k) % 4, c) if c == 0 else device((x + k) % 4, y, z, c))
        for x in range(4)
        for y in range(4)
        for z in range(4)
        for c in range(2)
    ]
    return lax.ppermute(value, ("kv", "tp"), pairs)


PLANES = [[device(x, y, z, 0) for x in range(4) for y in range(4)] for z in range(4)] + [
    [device(x, y, z, 1) for y in range(4) for z in range(4)] for x in range(4)
]


def move_z(value, k):
    pairs = [(z * 2 + c, (z + k) % 4 * 2 + c) for z in range(4) for c in range(2)]
    return lax.ppermute(value, "tp", pairs)


def move_core(value):
    return lax.ppermute(value, "tp", [(i, i ^ 1) for i in range(8)])


def local(
    activations,
    queries,
    keys,
    values,
    parents,
    node_lengths,
    token_leaf,
    out_weight,
    norm_gain,
    gate_weight,
    up_weight,
    down_weight,
):
    kv = lax.axis_index("kv")[None]
    tp = lax.axis_index("tp")[None]
    gate_t, up_t = gate_weight.T, up_weight.T
    shape = jax.ShapeDtypeStruct
    far = [move_core(w) for w in (gate_t, up_t, down_weight)]
    queries, kv, tp = lax.optimization_barrier((queries, kv, tp))

    padding = 128 - node_lengths.shape[0]
    tables = jnp.concatenate([token_leaf, jnp.pad(node_lengths, (0, padding)), jnp.pad(parents, (0, padding))])[None, :]
    repeated = pl.pallas_call(
        repeat_kernel,
        out_shape=shape((16, 16, 640), BF),
        in_specs=[pl.BlockSpec(memory_space=pl.ANY)],
        out_specs=pl.BlockSpec(memory_space=pl.ANY),
        scratch_shapes=[pltpu.SemaphoreType.DMA((16,))],
        compiler_params=pltpu.CompilerParams(vmem_limit_bytes=56 << 20),
    )(queries)
    q = lax.all_to_all(repeated, "kv", 0, 0)
    keys_wide, values_in, onehot = call(
        prepare_kernel,
        [shape((keys.shape[0], 256), BF), shape(values.shape, BF), shape((256, 128), BF)],
        [SM, VM, VM, VM],
    )(kv, tables, keys, values)
    packed = call(attend_kernel, shape((256, 768), BF), [VM] * 4 + [pl.ANY], limit=48 << 20)(
        q.reshape(256, 640), keys_wide, values_in, onehot, out_weight
    )
    parts = lax.all_to_all(packed.reshape(16, 16, 768), "kv", 0, 0)
    own, other = call(project_kernel, [shape((8, D), F32), shape((8, D), BF)], [SM, VM, VM, VM])(
        tp, parts, out_weight, activations
    )
    attended = own + move_core(other).astype(F32)
    sent = attended.astype(BF)
    for part in [move_z(sent, k) for k in (2, 1, 3)]:
        attended = attended + part.astype(F32)
    residual = attended.astype(BF)
    widened = residual.astype(F32)
    normed = (
        widened
        * lax.rsqrt(jnp.mean(widened * widened, axis=1, keepdims=True) + EPSILON)
        * norm_gain
    ).astype(BF)

    rows = lax.all_to_all(jnp.broadcast_to(normed[None], (16, 8, D)), "kv", 0, 0).reshape(128, D)
    block = shape((32, D), BF)
    mixed, *sent = call(
        mlp_kernel, [shape((32, D), F32), block, block, block], [SM, SM] + [VM] * 7, limit=28 << 20
    )(kv, tp, rows, gate_t, up_t, down_weight, *far)
    for part in [move_ring(value, k) for value, k in zip(sent, (2, 1, 3))]:
        mixed = mixed + part.astype(F32)
    mixed = mixed.astype(BF).reshape(16, 2, D)
    mixed = lax.all_to_all(mixed, ("kv", "tp"), 0, 0, axis_index_groups=PLANES)
    return call(finish_kernel, shape((2, D), BF), [SM, VM, VM])(tp, residual, mixed)


def solution(mesh):
    return jax.shard_map(
        local,
        mesh=mesh,
        in_specs=(
            P(("kv", "tp"), None),
            P("kv", "tp"),
            P("kv", "tp"),
            P("kv", "tp"),
            P(),
            P(),
            P(),
            P("tp", None),
            P(),
            P(None, ("kv", "tp")),
            P(None, ("kv", "tp")),
            P(("kv", "tp"), None),
        ),
        out_specs=P(("kv", "tp"), None),
        check_vma=False,
    )
```

```python
import functools
import math

import jax
import jax.numpy as jnp
from jax import lax
from jax.experimental import pallas as pl
from jax.experimental.pallas import tpu as pltpu
from jax.sharding import PartitionSpec as P

QUERY_HEADS = 40
KEY_VALUE_HEADS = 8
HEAD_WIDTH = 128
GROUP = QUERY_HEADS // KEY_VALUE_HEADS
LOWEST = -(2.0**100)
SCALE = 1.0 / math.sqrt(HEAD_WIDTH)
EPSILON = 1e-06
BF = jnp.bfloat16
F32 = jnp.float32
D = 5120
VM = pltpu.VMEM
SM = pltpu.SMEM


def call(kernel, out_shape, in_spaces, scratch=(), limit=12 << 20, **kw):
    outs = out_shape if isinstance(out_shape, (list, tuple)) else [out_shape]
    specs = [pl.BlockSpec(memory_space=VM) for _ in outs]
    return pl.pallas_call(
        kernel,
        out_shape=out_shape,
        in_specs=[pl.BlockSpec(memory_space=s) for s in in_spaces],
        out_specs=specs if isinstance(out_shape, (list, tuple)) else specs[0],
        scratch_shapes=list(scratch),
        compiler_params=pltpu.CompilerParams(vmem_limit_bytes=limit),
        **kw,
    )


def nt(a, b):
    return lax.dot_general(a, b, (((1,), (1,)), ((), ())), preferred_element_type=F32)


def mm(a, b):
    return lax.dot_general(a, b, (((1,), (0,)), ((), ())), preferred_element_type=F32)


def repeat_kernel(rows, out, sem):
    copies = [pltpu.make_async_copy(rows, out.at[k], sem.at[k]) for k in range(out.shape[0])]
    for copy in copies:
        copy.start()
    for copy in copies:
        copy.wait()


def prepare_kernel(kv, tables, keys, values, keys_wide, values_out, onehot):
    slots = keys.shape[0]
    tokens = onehot.shape[0]
    row = lax.broadcasted_iota(jnp.int32, (128, 128), 0)
    col = lax.broadcasted_iota(jnp.int32, (128, 128), 1)
    leaf = tables[:, :tokens]
    lengths = tables[:, tokens : tokens + 128]
    parents = tables[:, tokens + 128 :]

    def upright(lanes):
        return jnp.sum(jnp.where(row == col, lanes, 0), axis=1, keepdims=True)

    own_lo = jnp.sum(jnp.where(row < col, upright(lengths), 0), axis=0, keepdims=True)
    own_hi = own_lo + lengths
    up_lo = jnp.sum(jnp.where(row == parents, upright(own_lo), 0), axis=0, keepdims=True)
    up_hi = jnp.sum(jnp.where(row == parents, upright(own_hi), 0), axis=0, keepdims=True)
    root = own_hi[:, :1]
    slot = kv[0] * slots + lax.broadcasted_iota(jnp.int32, (slots, 128), 0)
    seen = (
        (slot < root)
        | ((slot >= own_lo) & (slot < own_hi))
        | ((slot >= up_lo) & (slot < up_hi))
    )
    keys_wide[:, :HEAD_WIDTH] = keys[...]
    keys_wide[:, HEAD_WIDTH:] = jnp.where(seen, 0.0, LOWEST).astype(BF)
    values_out[...] = values[...]
    node = lax.broadcasted_iota(jnp.int32, (128, tokens), 0)
    onehot[...] = jnp.where(node == leaf, 1.0, 0.0).astype(F32).T.astype(BF)


def attend_kernel(q, keys_wide, values, onehot, weight, out):
    tokens = q.shape[0]
    lane_t = lax.broadcasted_iota(jnp.int32, (tokens, 128), 1)
    stats = jnp.zeros((tokens, 128), F32)
    for g in range(GROUP):
        cols = pl.ds(g * HEAD_WIDTH, HEAD_WIDTH)
        q_wide = jnp.concatenate([q[:, cols], onehot[...]], axis=1)
        scores = nt(q_wide, keys_wide[...])
        top = jnp.max(scores, axis=1, keepdims=True).astype(BF).astype(F32)
        weights = jnp.exp((scores - top) * SCALE)
        mass = jnp.sum(weights, axis=1, keepdims=True)
        out[:, cols] = mm(weights.astype(BF), values[...]).astype(BF)
        high = mass.astype(BF).astype(F32)
        stats = jnp.where(lane_t == g, top, stats)
        stats = jnp.where(lane_t == GROUP + g, high, stats)
        stats = jnp.where(lane_t == 2 * GROUP + g, mass - high, stats)
    out[:, GROUP * HEAD_WIDTH :] = stats.astype(BF)


def project_kernel(tp, parts, weight, activations, own, other):
    z, core = tp[0] >> 1, tp[0] & 1
    sources = parts.shape[0]
    width = GROUP * HEAD_WIDTH
    stats = [parts[s, :, width:].astype(F32) for s in range(sources)]
    top = stats[0]
    for s in stats[1:]:
        top = jnp.maximum(top, s)
    scales = [jnp.exp((s - top) * SCALE) for s in stats]
    heads = []
    for g in range(GROUP):
        total = jnp.zeros((16, HEAD_WIDTH), F32)
        mass = jnp.zeros((16, 1), F32)
        for s in range(sources):
            scale = scales[s][:, g : g + 1]
            part = parts[s, :, g * HEAD_WIDTH : (g + 1) * HEAD_WIDTH].astype(F32)
            total = total + part * scale
            low = stats[s][:, GROUP + g : GROUP + g + 1] + stats[s][:, 2 * GROUP + g : 2 * GROUP + g + 1]
            mass = mass + low * scale
        heads.append((total / mass).astype(BF))
    context = jnp.concatenate(heads, axis=1)
    row = lax.broadcasted_iota(jnp.int32, (16, 16), 0)
    col = lax.broadcasted_iota(jnp.int32, (16, 16), 1)
    half = jnp.where(row < 8, core, 1 - core)
    source = (row % 8) // 2 * 4 + half * 2 + row % 2
    pick = jnp.where(col == source, 1.0, 0.0).astype(BF)
    context = mm(pick, context).astype(BF)
    result = mm(context, weight[...])
    row = lax.broadcasted_iota(jnp.int32, (8, 2), 0)
    col = lax.broadcasted_iota(jnp.int32, (8, 2), 1)
    place = jnp.where(row == z * 2 + col, 1.0, 0.0).astype(BF)
    own[...] = result[:8] + mm(place, activations[...])
    other[...] = result[8:].astype(BF)


def hidden_of(rows, gate, up):
    g = nt(rows, gate)
    u = nt(rows, up)
    return (g / (1.0 + jnp.exp(-g)) * u).astype(BF)


def ordered(hidden, kv, tp):
    n = hidden.shape[0]
    row = lax.broadcasted_iota(jnp.int32, (n, n), 0)
    col = lax.broadcasted_iota(jnp.int32, (n, n), 1)
    x, z, core = kv[0] >> 2, tp[0] >> 1, tp[0] & 1
    block = row // 32
    q = (row & 31) // 2
    places = jnp.where(block == 0, 0, jnp.where(block == 1, 2, jnp.where(block == 2, 1, 3)))
    along_z = q * 8 + ((z + places) & 3) * 2
    along_x = (((x + places) & 3) * 4 + q // 4) * 8 + (q & 3) * 2
    source = jnp.where(core == 0, along_z, along_x) + (row & 1)
    return mm(jnp.where(col == source, 1.0, 0.0).astype(BF), hidden).astype(BF)


def mlp_kernel(kv, tp, rows, gate, up, down, gate_far, up_far, down_far, own, *sent):
    near = ordered(hidden_of(rows[...], gate[...], up[...]), kv, tp)
    far = ordered(hidden_of(rows[...], gate_far[...], up_far[...]), kv, tp)
    result = mm(near, down[...]) + mm(far, down_far[...])
    own[...] = result[:32]
    for k, ref in enumerate(sent):
        ref[...] = result[32 * (k + 1) : 32 * (k + 2)].astype(BF)


def finish_kernel(tp, residual, parts, out):
    row = lax.broadcasted_iota(jnp.int32, (2, 8), 0)
    col = lax.broadcasted_iota(jnp.int32, (2, 8), 1)
    pick = jnp.where(col == (tp[0] >> 1) * 2 + row, 1.0, 0.0).astype(BF)
    total = mm(pick, residual[...])
    for k in range(parts.shape[0]):
        total = total + parts[k].astype(F32)
    out[...] = total.astype(BF)


def device(x, y, z, c):
    return (x * 4 + y) * 8 + z * 2 + c


def move_ring(value, k):
    pairs = [
        (device(x, y, z, c), device(x, y, (z + k) % 4, c) if c == 0 else device((x + k) % 4, y, z, c))
        for x in range(4)
        for y in range(4)
        for z in range(4)
        for c in range(2)
    ]
    return lax.ppermute(value, ("kv", "tp"), pairs)


PLANES = [[device(x, y, z, 0) for x in range(4) for y in range(4)] for z in range(4)] + [
    [device(x, y, z, 1) for y in range(4) for z in range(4)] for x in range(4)
]


def move_z(value, k):
    pairs = [(z * 2 + c, (z + k) % 4 * 2 + c) for z in range(4) for c in range(2)]
    return lax.ppermute(value, "tp", pairs)


def move_core(value):
    return lax.ppermute(value, "tp", [(i, i ^ 1) for i in range(8)])


def local(
    activations,
    queries,
    keys,
    values,
    parents,
    node_lengths,
    token_leaf,
    out_weight,
    norm_gain,
    gate_weight,
    up_weight,
    down_weight,
):
    kv = lax.axis_index("kv")[None]
    tp = lax.axis_index("tp")[None]
    gate_t, up_t = gate_weight.T, up_weight.T
    shape = jax.ShapeDtypeStruct
    far = [move_core(w) for w in (gate_t, up_t, down_weight)]
    queries, kv, tp = lax.optimization_barrier((queries, kv, tp))

    padding = 128 - node_lengths.shape[0]
    tables = jnp.concatenate([token_leaf, jnp.pad(node_lengths, (0, padding)), jnp.pad(parents, (0, padding))])[None, :]
    repeated = pl.pallas_call(
        repeat_kernel,
        out_shape=shape((16, 16, 640), BF),
        in_specs=[pl.BlockSpec(memory_space=VM)],
        out_specs=pl.BlockSpec(memory_space=pl.ANY),
        scratch_shapes=[pltpu.SemaphoreType.DMA((16,))],
        compiler_params=pltpu.CompilerParams(vmem_limit_bytes=56 << 20),
    )(queries)
    q = lax.all_to_all(repeated, "kv", 0, 0)
    keys_wide, values_in, onehot = call(
        prepare_kernel,
        [shape((keys.shape[0], 256), BF), shape(values.shape, BF), shape((256, 128), BF)],
        [SM, VM, VM, VM],
    )(kv, tables, keys, values)
    packed = call(attend_kernel, shape((256, 768), BF), [VM] * 4 + [pl.ANY], limit=48 << 20)(
        q.reshape(256, 640), keys_wide, values_in, onehot, out_weight
    )
    parts = lax.all_to_all(packed.reshape(16, 16, 768), "kv", 0, 0)
    own, other = call(project_kernel, [shape((8, D), F32), shape((8, D), BF)], [SM, VM, VM, VM])(
        tp, parts, out_weight, activations
    )
    attended = own + move_core(other).astype(F32)
    sent = attended.astype(BF)
    for part in [move_z(sent, k) for k in (2, 1, 3)]:
        attended = attended + part.astype(F32)
    residual = attended.astype(BF)
    widened = residual.astype(F32)
    normed = (
        widened
        * lax.rsqrt(jnp.mean(widened * widened, axis=1, keepdims=True) + EPSILON)
        * norm_gain
    ).astype(BF)

    rows = lax.all_to_all(jnp.broadcast_to(normed[None], (16, 8, D)), "kv", 0, 0).reshape(128, D)
    block = shape((32, D), BF)
    mixed, *sent = call(
        mlp_kernel, [shape((32, D), F32), block, block, block], [SM, SM] + [VM] * 7, limit=28 << 20
    )(kv, tp, rows, gate_t, up_t, down_weight, *far)
    for part in [move_ring(value, k) for value, k in zip(sent, (2, 1, 3))]:
        mixed = mixed + part.astype(F32)
    mixed = mixed.astype(BF).reshape(16, 2, D)
    mixed = lax.all_to_all(mixed, ("kv", "tp"), 0, 0, axis_index_groups=PLANES)
    return call(finish_kernel, shape((2, D), BF), [SM, VM, VM])(tp, residual, mixed)


def solution(mesh):
    return jax.shard_map(
        local,
        mesh=mesh,
        in_specs=(
            P(("kv", "tp"), None),
            P("kv", "tp"),
            P("kv", "tp"),
            P("kv", "tp"),
            P(),
            P(),
            P(),
            P("tp", None),
            P(),
            P(None, ("kv", "tp")),
            P(None, ("kv", "tp")),
            P(("kv", "tp"), None),
        ),
        out_specs=P(("kv", "tp"), None),
        check_vma=False,
    )
```

```python
import functools
import math

import jax
import jax.numpy as jnp
from jax import lax
from jax.experimental import pallas as pl
from jax.experimental.pallas import tpu as pltpu
from jax.sharding import PartitionSpec as P

QUERY_HEADS = 40
KEY_VALUE_HEADS = 8
HEAD_WIDTH = 128
GROUP = QUERY_HEADS // KEY_VALUE_HEADS
LOWEST = -(2.0**100)
SCALE = 1.0 / math.sqrt(HEAD_WIDTH)
EPSILON = 1e-06
BF = jnp.bfloat16
F32 = jnp.float32
D = 5120
VM = pltpu.VMEM
SM = pltpu.SMEM


def call(kernel, out_shape, in_spaces, scratch=(), limit=12 << 20, **kw):
    outs = out_shape if isinstance(out_shape, (list, tuple)) else [out_shape]
    specs = [pl.BlockSpec(memory_space=VM) for _ in outs]
    return pl.pallas_call(
        kernel,
        out_shape=out_shape,
        in_specs=[pl.BlockSpec(memory_space=s) for s in in_spaces],
        out_specs=specs if isinstance(out_shape, (list, tuple)) else specs[0],
        scratch_shapes=list(scratch),
        compiler_params=pltpu.CompilerParams(vmem_limit_bytes=limit),
        **kw,
    )


def nt(a, b):
    return lax.dot_general(a, b, (((1,), (1,)), ((), ())), preferred_element_type=F32)


def mm(a, b):
    return lax.dot_general(a, b, (((1,), (0,)), ((), ())), preferred_element_type=F32)


def prepare_kernel(kv, tables, keys, values, keys_wide, values_out, onehot):
    slots = keys.shape[0]
    tokens = onehot.shape[0]
    row = lax.broadcasted_iota(jnp.int32, (128, 128), 0)
    col = lax.broadcasted_iota(jnp.int32, (128, 128), 1)
    leaf = tables[:, :tokens]
    lengths = tables[:, tokens : tokens + 128]
    parents = tables[:, tokens + 128 :]

    def upright(lanes):
        return jnp.sum(jnp.where(row == col, lanes, 0), axis=1, keepdims=True)

    own_lo = jnp.sum(jnp.where(row < col, upright(lengths), 0), axis=0, keepdims=True)
    own_hi = own_lo + lengths
    up_lo = jnp.sum(jnp.where(row == parents, upright(own_lo), 0), axis=0, keepdims=True)
    up_hi = jnp.sum(jnp.where(row == parents, upright(own_hi), 0), axis=0, keepdims=True)
    root = own_hi[:, :1]
    slot = kv[0] * slots + lax.broadcasted_iota(jnp.int32, (slots, 128), 0)
    seen = (
        (slot < root)
        | ((slot >= own_lo) & (slot < own_hi))
        | ((slot >= up_lo) & (slot < up_hi))
    )
    keys_wide[:, :HEAD_WIDTH] = keys[...]
    keys_wide[:, HEAD_WIDTH:] = jnp.where(seen, 0.0, LOWEST).astype(BF)
    values_out[...] = values[...]
    node = lax.broadcasted_iota(jnp.int32, (128, tokens), 0)
    onehot[...] = jnp.where(node == leaf, 1.0, 0.0).astype(F32).T.astype(BF)


def attend_kernel(q, keys_wide, values, onehot, weight, out):
    tokens = q.shape[0]
    lane_t = lax.broadcasted_iota(jnp.int32, (tokens, 128), 1)
    stats = jnp.zeros((tokens, 128), F32)
    for g in range(GROUP):
        cols = pl.ds(g * HEAD_WIDTH, HEAD_WIDTH)
        q_wide = jnp.concatenate([q[:, cols], onehot[...]], axis=1)
        scores = nt(q_wide, keys_wide[...])
        top = jnp.max(scores, axis=1, keepdims=True).astype(BF).astype(F32)
        weights = jnp.exp((scores - top) * SCALE)
        mass = jnp.sum(weights, axis=1, keepdims=True)
        out[:, cols] = mm(weights.astype(BF), values[...]).astype(BF)
        high = mass.astype(BF).astype(F32)
        stats = jnp.where(lane_t == g, top, stats)
        stats = jnp.where(lane_t == GROUP + g, high, stats)
        stats = jnp.where(lane_t == 2 * GROUP + g, mass - high, stats)
    out[:, GROUP * HEAD_WIDTH :] = stats.astype(BF)


def project_kernel(tp, parts, weight, activations, own, other):
    z, core = tp[0] >> 1, tp[0] & 1
    sources = parts.shape[0]
    width = GROUP * HEAD_WIDTH
    stats = [parts[s, :, width:].astype(F32) for s in range(sources)]
    top = stats[0]
    for s in stats[1:]:
        top = jnp.maximum(top, s)
    scales = [jnp.exp((s - top) * SCALE) for s in stats]
    heads = []
    for g in range(GROUP):
        total = jnp.zeros((16, HEAD_WIDTH), F32)
        mass = jnp.zeros((16, 1), F32)
        for s in range(sources):
            scale = scales[s][:, g : g + 1]
            part = parts[s, :, g * HEAD_WIDTH : (g + 1) * HEAD_WIDTH].astype(F32)
            total = total + part * scale
            low = stats[s][:, GROUP + g : GROUP + g + 1] + stats[s][:, 2 * GROUP + g : 2 * GROUP + g + 1]
            mass = mass + low * scale
        heads.append((total / mass).astype(BF))
    context = jnp.concatenate(heads, axis=1)
    row = lax.broadcasted_iota(jnp.int32, (16, 16), 0)
    col = lax.broadcasted_iota(jnp.int32, (16, 16), 1)
    half = jnp.where(row < 8, core, 1 - core)
    source = (row % 8) // 2 * 4 + half * 2 + row % 2
    pick = jnp.where(col == source, 1.0, 0.0).astype(BF)
    context = mm(pick, context).astype(BF)
    result = mm(context, weight[...])
    row = lax.broadcasted_iota(jnp.int32, (8, 2), 0)
    col = lax.broadcasted_iota(jnp.int32, (8, 2), 1)
    place = jnp.where(row == z * 2 + col, 1.0, 0.0).astype(BF)
    own[...] = result[:8] + mm(place, activations[...])
    other[...] = result[8:].astype(BF)


def normalize_kernel(gain, own, swapped, *refs):
    residual, repeated = refs[-2:]
    total = own[...] + swapped[...].astype(F32)
    for part in refs[:-2]:
        total = total + part[...].astype(F32)
    rounded = total.astype(BF)
    residual[...] = rounded
    wide = rounded.astype(F32)
    scale = lax.rsqrt(jnp.mean(wide * wide, axis=1, keepdims=True) + EPSILON)
    normed = (wide * scale * gain[...]).astype(BF)
    for k in range(repeated.shape[0]):
        repeated[k] = normed


def hidden_of(rows, gate, up):
    g = nt(rows, gate)
    u = nt(rows, up)
    return (g / (1.0 + jnp.exp(-g)) * u).astype(BF)


def ordered(hidden, kv, tp):
    n = hidden.shape[0]
    row = lax.broadcasted_iota(jnp.int32, (n, n), 0)
    col = lax.broadcasted_iota(jnp.int32, (n, n), 1)
    x, z, core = kv[0] >> 2, tp[0] >> 1, tp[0] & 1
    block = row // 32
    q = (row & 31) // 2
    places = jnp.where(block == 0, 0, jnp.where(block == 1, 2, jnp.where(block == 2, 1, 3)))
    along_z = q * 8 + ((z + places) & 3) * 2
    along_x = (((x + places) & 3) * 4 + q // 4) * 8 + (q & 3) * 2
    source = jnp.where(core == 0, along_z, along_x) + (row & 1)
    return mm(jnp.where(col == source, 1.0, 0.0).astype(BF), hidden).astype(BF)


def mlp_kernel(kv, tp, rows, gate, up, down, gate_far, up_far, down_far, own, *sent):
    near = ordered(hidden_of(rows[...], gate[...], up[...]), kv, tp)
    far = ordered(hidden_of(rows[...], gate_far[...], up_far[...]), kv, tp)
    result = mm(near, down[...]) + mm(far, down_far[...])
    own[...] = result[:32]
    for k, ref in enumerate(sent):
        ref[...] = result[32 * (k + 1) : 32 * (k + 2)].astype(BF)


def finish_kernel(tp, residual, parts, out):
    row = lax.broadcasted_iota(jnp.int32, (2, 8), 0)
    col = lax.broadcasted_iota(jnp.int32, (2, 8), 1)
    pick = jnp.where(col == (tp[0] >> 1) * 2 + row, 1.0, 0.0).astype(BF)
    total = mm(pick, residual[...])
    for k in range(parts.shape[0]):
        total = total + parts[k].astype(F32)
    out[...] = total.astype(BF)


def device(x, y, z, c):
    return (x * 4 + y) * 8 + z * 2 + c


def move_ring(value, k):
    pairs = [
        (device(x, y, z, c), device(x, y, (z + k) % 4, c) if c == 0 else device((x + k) % 4, y, z, c))
        for x in range(4)
        for y in range(4)
        for z in range(4)
        for c in range(2)
    ]
    return lax.ppermute(value, ("kv", "tp"), pairs)


PLANES = [[device(x, y, z, 0) for x in range(4) for y in range(4)] for z in range(4)] + [
    [device(x, y, z, 1) for y in range(4) for z in range(4)] for x in range(4)
]


def move_z(value, k):
    pairs = [(z * 2 + c, (z + k) % 4 * 2 + c) for z in range(4) for c in range(2)]
    return lax.ppermute(value, "tp", pairs)


def move_core(value):
    return lax.ppermute(value, "tp", [(i, i ^ 1) for i in range(8)])


def local(
    activations,
    queries,
    keys,
    values,
    parents,
    node_lengths,
    token_leaf,
    out_weight,
    norm_gain,
    gate_weight,
    up_weight,
    down_weight,
):
    kv = lax.axis_index("kv")[None]
    tp = lax.axis_index("tp")[None]
    gate_t, up_t = gate_weight.T, up_weight.T
    shape = jax.ShapeDtypeStruct
    queries, kv, tp = lax.optimization_barrier((queries, kv, tp))

    padding = 128 - node_lengths.shape[0]
    tables = jnp.concatenate([token_leaf, jnp.pad(node_lengths, (0, padding)), jnp.pad(parents, (0, padding))])[None, :]
    q = lax.all_to_all(jnp.broadcast_to(queries[None], (16, 16, 640)), "kv", 0, 0)
    keys_wide, values_in, onehot = call(
        prepare_kernel,
        [shape((keys.shape[0], 256), BF), shape(values.shape, BF), shape((256, 128), BF)],
        [SM, VM, VM, VM],
    )(kv, tables, keys, values)
    packed = call(attend_kernel, shape((256, 768), BF), [VM] * 4 + [pl.ANY], limit=48 << 20)(
        q.reshape(256, 640), keys_wide, values_in, onehot, out_weight
    )
    parts = lax.all_to_all(packed.reshape(16, 16, 768), "kv", 0, 0)
    own, other = call(project_kernel, [shape((8, D), F32), shape((8, D), BF)], [SM, VM, VM, VM])(
        tp, parts, out_weight, activations
    )
    swapped = move_core(other)
    sent = (own + swapped.astype(F32)).astype(BF)
    around = [move_z(sent, k) for k in (2, 1, 3)]
    residual, repeated = call(normalize_kernel, [shape((8, D), BF), shape((16, 8, D), BF)], [VM] * 6)(
        norm_gain[None, :], own, swapped, *around
    )
    repeated, *far = lax.optimization_barrier((repeated, gate_t, up_t, down_weight))
    far = [move_core(w) for w in far]
    rows = lax.all_to_all(repeated, "kv", 0, 0).reshape(128, D)
    block = shape((32, D), BF)
    mixed, *sent = call(
        mlp_kernel, [shape((32, D), F32), block, block, block], [SM, SM] + [VM] * 7, limit=28 << 20
    )(kv, tp, rows, gate_t, up_t, down_weight, *far)
    for part in [move_ring(value, k) for value, k in zip(sent, (2, 1, 3))]:
        mixed = mixed + part.astype(F32)
    mixed = mixed.astype(BF).reshape(16, 2, D)
    mixed = lax.all_to_all(mixed, ("kv", "tp"), 0, 0, axis_index_groups=PLANES)
    return call(finish_kernel, shape((2, D), BF), [SM, VM, VM])(tp, residual, mixed)


def solution(mesh):
    return jax.shard_map(
        local,
        mesh=mesh,
        in_specs=(
            P(("kv", "tp"), None),
            P("kv", "tp"),
            P("kv", "tp"),
            P("kv", "tp"),
            P(),
            P(),
            P(),
            P("tp", None),
            P(),
            P(None, ("kv", "tp")),
            P(None, ("kv", "tp")),
            P(("kv", "tp"), None),
        ),
        out_specs=P(("kv", "tp"), None),
        check_vma=False,
    )
```

```python
import functools
import math

import jax
import jax.numpy as jnp
from jax import lax
from jax.experimental import pallas as pl
from jax.experimental.pallas import tpu as pltpu
from jax.sharding import PartitionSpec as P

QUERY_HEADS = 40
KEY_VALUE_HEADS = 8
HEAD_WIDTH = 128
GROUP = QUERY_HEADS // KEY_VALUE_HEADS
LOWEST = -(2.0**100)
SCALE = 1.0 / math.sqrt(HEAD_WIDTH)
EPSILON = 1e-06
BF = jnp.bfloat16
F32 = jnp.float32
D = 5120
VM = pltpu.VMEM
SM = pltpu.SMEM


def call(kernel, out_shape, in_spaces, scratch=(), limit=12 << 20, **kw):
    outs = out_shape if isinstance(out_shape, (list, tuple)) else [out_shape]
    specs = [pl.BlockSpec(memory_space=VM) for _ in outs]
    return pl.pallas_call(
        kernel,
        out_shape=out_shape,
        in_specs=[pl.BlockSpec(memory_space=s) for s in in_spaces],
        out_specs=specs if isinstance(out_shape, (list, tuple)) else specs[0],
        scratch_shapes=list(scratch),
        compiler_params=pltpu.CompilerParams(vmem_limit_bytes=limit),
        **kw,
    )


def nt(a, b):
    return lax.dot_general(a, b, (((1,), (1,)), ((), ())), preferred_element_type=F32)


def mm(a, b):
    return lax.dot_general(a, b, (((1,), (0,)), ((), ())), preferred_element_type=F32)


def prepare_kernel(kv, tables, keys, values, keys_wide, values_out, onehot):
    slots = keys.shape[0]
    tokens = onehot.shape[0]
    row = lax.broadcasted_iota(jnp.int32, (128, 128), 0)
    col = lax.broadcasted_iota(jnp.int32, (128, 128), 1)
    leaf = tables[:, :tokens]
    lengths = tables[:, tokens : tokens + 128]
    parents = tables[:, tokens + 128 :]

    def upright(lanes):
        return jnp.sum(jnp.where(row == col, lanes, 0), axis=1, keepdims=True)

    own_lo = jnp.sum(jnp.where(row < col, upright(lengths), 0), axis=0, keepdims=True)
    own_hi = own_lo + lengths
    up_lo = jnp.sum(jnp.where(row == parents, upright(own_lo), 0), axis=0, keepdims=True)
    up_hi = jnp.sum(jnp.where(row == parents, upright(own_hi), 0), axis=0, keepdims=True)
    root = own_hi[:, :1]
    slot = kv[0] * slots + lax.broadcasted_iota(jnp.int32, (slots, 128), 0)
    seen = (
        (slot < root)
        | ((slot >= own_lo) & (slot < own_hi))
        | ((slot >= up_lo) & (slot < up_hi))
    )
    keys_wide[:, :HEAD_WIDTH] = keys[...]
    keys_wide[:, HEAD_WIDTH:] = jnp.where(seen, 0.0, LOWEST).astype(BF)
    values_out[...] = values[...]
    node = lax.broadcasted_iota(jnp.int32, (128, tokens), 0)
    onehot[...] = jnp.where(node == leaf, 1.0, 0.0).astype(F32).T.astype(BF)


def attend_kernel(q, keys_wide, values, onehot, weight, out):
    tokens = q.shape[0]
    lane_t = lax.broadcasted_iota(jnp.int32, (tokens, 128), 1)
    stats = jnp.zeros((tokens, 128), F32)
    for g in range(GROUP):
        cols = pl.ds(g * HEAD_WIDTH, HEAD_WIDTH)
        q_wide = jnp.concatenate([q[:, cols], onehot[...]], axis=1)
        scores = nt(q_wide, keys_wide[...])
        top = jnp.max(scores, axis=1, keepdims=True).astype(BF).astype(F32)
        weights = jnp.exp((scores - top) * SCALE)
        mass = jnp.sum(weights, axis=1, keepdims=True)
        out[:, cols] = mm(weights.astype(BF), values[...]).astype(BF)
        high = mass.astype(BF).astype(F32)
        stats = jnp.where(lane_t == g, top, stats)
        stats = jnp.where(lane_t == GROUP + g, high, stats)
        stats = jnp.where(lane_t == 2 * GROUP + g, mass - high, stats)
    out[:, GROUP * HEAD_WIDTH :] = stats.astype(BF)


def project_kernel(tp, parts, weight, activations, own, other):
    z, core = tp[0] >> 1, tp[0] & 1
    sources = parts.shape[0]
    width = GROUP * HEAD_WIDTH
    stats = [parts[s, :, width:].astype(F32) for s in range(sources)]
    top = stats[0]
    for s in stats[1:]:
        top = jnp.maximum(top, s)
    scales = [jnp.exp((s - top) * SCALE) for s in stats]
    heads = []
    for g in range(GROUP):
        total = jnp.zeros((16, HEAD_WIDTH), F32)
        mass = jnp.zeros((16, 1), F32)
        for s in range(sources):
            scale = scales[s][:, g : g + 1]
            part = parts[s, :, g * HEAD_WIDTH : (g + 1) * HEAD_WIDTH].astype(F32)
            total = total + part * scale
            low = stats[s][:, GROUP + g : GROUP + g + 1] + stats[s][:, 2 * GROUP + g : 2 * GROUP + g + 1]
            mass = mass + low * scale
        heads.append((total / mass).astype(BF))
    context = jnp.concatenate(heads, axis=1)
    row = lax.broadcasted_iota(jnp.int32, (16, 16), 0)
    col = lax.broadcasted_iota(jnp.int32, (16, 16), 1)
    half = jnp.where(row < 8, core, 1 - core)
    source = (row % 8) // 2 * 4 + half * 2 + row % 2
    pick = jnp.where(col == source, 1.0, 0.0).astype(BF)
    context = mm(pick, context).astype(BF)
    result = mm(context, weight[...])
    row = lax.broadcasted_iota(jnp.int32, (8, 2), 0)
    col = lax.broadcasted_iota(jnp.int32, (8, 2), 1)
    place = jnp.where(row == z * 2 + col, 1.0, 0.0).astype(BF)
    own[...] = result[:8] + mm(place, activations[...])
    other[...] = result[8:].astype(BF)


def normalize_kernel(gain, own, swapped, *refs):
    residual, repeated = refs[-2:]
    total = own[...] + swapped[...].astype(F32)
    for part in refs[:-2]:
        total = total + part[...].astype(F32)
    rounded = total.astype(BF)
    residual[...] = rounded
    wide = rounded.astype(F32)
    scale = lax.rsqrt(jnp.mean(wide * wide, axis=1, keepdims=True) + EPSILON)
    normed = (wide * scale * gain[...]).astype(BF)
    for k in range(repeated.shape[0]):
        repeated[k] = normed


def hidden_of(rows, gate, up):
    g = nt(rows, gate)
    u = nt(rows, up)
    return (g / (1.0 + jnp.exp(-g)) * u).astype(BF)


def ordered(hidden, kv, tp):
    n = hidden.shape[0]
    row = lax.broadcasted_iota(jnp.int32, (n, n), 0)
    col = lax.broadcasted_iota(jnp.int32, (n, n), 1)
    x, z, core = kv[0] >> 2, tp[0] >> 1, tp[0] & 1
    block = row // 32
    q = (row & 31) // 2
    places = jnp.where(block == 0, 0, jnp.where(block == 1, 2, jnp.where(block == 2, 1, 3)))
    along_z = q * 8 + ((z + places) & 3) * 2
    along_x = (((x + places) & 3) * 4 + q // 4) * 8 + (q & 3) * 2
    source = jnp.where(core == 0, along_z, along_x) + (row & 1)
    return mm(jnp.where(col == source, 1.0, 0.0).astype(BF), hidden).astype(BF)


def mlp_kernel(kv, tp, rows, gate, up, down, gate_far, up_far, down_far, own, *sent):
    near = ordered(hidden_of(rows[...], gate[...], up[...]), kv, tp)
    far = ordered(hidden_of(rows[...], gate_far[...], up_far[...]), kv, tp)
    result = mm(near, down[...]) + mm(far, down_far[...])
    own[...] = result[:32]
    for k, ref in enumerate(sent):
        ref[...] = result[32 * (k + 1) : 32 * (k + 2)].astype(BF)


def finish_kernel(tp, residual, parts, out):
    row = lax.broadcasted_iota(jnp.int32, (2, 8), 0)
    col = lax.broadcasted_iota(jnp.int32, (2, 8), 1)
    pick = jnp.where(col == (tp[0] >> 1) * 2 + row, 1.0, 0.0).astype(BF)
    total = mm(pick, residual[...])
    for k in range(parts.shape[0]):
        total = total + parts[k].astype(F32)
    out[...] = total.astype(BF)


def device(x, y, z, c):
    return (x * 4 + y) * 8 + z * 2 + c


def move_ring(value, k):
    pairs = [
        (device(x, y, z, c), device(x, y, (z + k) % 4, c) if c == 0 else device((x + k) % 4, y, z, c))
        for x in range(4)
        for y in range(4)
        for z in range(4)
        for c in range(2)
    ]
    return lax.ppermute(value, ("kv", "tp"), pairs)


PLANES = [[device(x, y, z, 0) for x in range(4) for y in range(4)] for z in range(4)] + [
    [device(x, y, z, 1) for y in range(4) for z in range(4)] for x in range(4)
]


def move_z(value, k):
    pairs = [(z * 2 + c, (z + k) % 4 * 2 + c) for z in range(4) for c in range(2)]
    return lax.ppermute(value, "tp", pairs)


def move_core(value):
    return lax.ppermute(value, "tp", [(i, i ^ 1) for i in range(8)])


def local(
    activations,
    queries,
    keys,
    values,
    parents,
    node_lengths,
    token_leaf,
    out_weight,
    norm_gain,
    gate_weight,
    up_weight,
    down_weight,
):
    kv = lax.axis_index("kv")[None]
    tp = lax.axis_index("tp")[None]
    gate_t, up_t = gate_weight.T, up_weight.T
    shape = jax.ShapeDtypeStruct
    queries, kv, tp = lax.optimization_barrier((queries, kv, tp))

    padding = 128 - node_lengths.shape[0]
    tables = jnp.concatenate([token_leaf, jnp.pad(node_lengths, (0, padding)), jnp.pad(parents, (0, padding))])[None, :]
    q = lax.all_to_all(jnp.broadcast_to(queries[None], (16, 16, 640)), "kv", 0, 0)
    keys_wide, values_in, onehot = call(
        prepare_kernel,
        [shape((keys.shape[0], 256), BF), shape(values.shape, BF), shape((256, 128), BF)],
        [SM, VM, VM, VM],
    )(kv, tables, keys, values)
    packed = call(attend_kernel, shape((256, 768), BF), [VM] * 4 + [pl.ANY], limit=48 << 20)(
        q.reshape(256, 640), keys_wide, values_in, onehot, out_weight
    )
    parts = lax.all_to_all(packed.reshape(16, 16, 768), "kv", 0, 0)
    own, other = call(project_kernel, [shape((8, D), F32), shape((8, D), BF)], [SM, VM, VM, VM])(
        tp, parts, out_weight, activations
    )
    far = [move_core(w) for w in (gate_t, up_t)]
    swapped = move_core(other)
    sent = (own + swapped.astype(F32)).astype(BF)
    around = [move_z(sent, k) for k in (2, 1, 3)]
    residual, repeated = call(normalize_kernel, [shape((8, D), BF), shape((16, 8, D), BF)], [VM] * 6)(
        norm_gain[None, :], own, swapped, *around
    )
    repeated, down_far = lax.optimization_barrier((repeated, down_weight))
    far.append(move_core(down_far))
    rows = lax.all_to_all(repeated, "kv", 0, 0).reshape(128, D)
    block = shape((32, D), BF)
    mixed, *sent = call(
        mlp_kernel, [shape((32, D), F32), block, block, block], [SM, SM] + [VM] * 7, limit=28 << 20
    )(kv, tp, rows, gate_t, up_t, down_weight, *far)
    for part in [move_ring(value, k) for value, k in zip(sent, (2, 1, 3))]:
        mixed = mixed + part.astype(F32)
    mixed = mixed.astype(BF).reshape(16, 2, D)
    mixed = lax.all_to_all(mixed, ("kv", "tp"), 0, 0, axis_index_groups=PLANES)
    return call(finish_kernel, shape((2, D), BF), [SM, VM, VM])(tp, residual, mixed)


def solution(mesh):
    return jax.shard_map(
        local,
        mesh=mesh,
        in_specs=(
            P(("kv", "tp"), None),
            P("kv", "tp"),
            P("kv", "tp"),
            P("kv", "tp"),
            P(),
            P(),
            P(),
            P("tp", None),
            P(),
            P(None, ("kv", "tp")),
            P(None, ("kv", "tp")),
            P(("kv", "tp"), None),
        ),
        out_specs=P(("kv", "tp"), None),
        check_vma=False,
    )
```

```python
import functools
import math

import jax
import jax.numpy as jnp
from jax import lax
from jax.experimental import pallas as pl
from jax.experimental.pallas import tpu as pltpu
from jax.sharding import PartitionSpec as P

QUERY_HEADS = 40
KEY_VALUE_HEADS = 8
HEAD_WIDTH = 128
GROUP = QUERY_HEADS // KEY_VALUE_HEADS
LOWEST = -(2.0**100)
SCALE = 1.0 / math.sqrt(HEAD_WIDTH)
EPSILON = 1e-06
BF = jnp.bfloat16
F32 = jnp.float32
D = 5120
VM = pltpu.VMEM
SM = pltpu.SMEM


def call(kernel, out_shape, in_spaces, scratch=(), limit=12 << 20, **kw):
    outs = out_shape if isinstance(out_shape, (list, tuple)) else [out_shape]
    specs = [pl.BlockSpec(memory_space=VM) for _ in outs]
    return pl.pallas_call(
        kernel,
        out_shape=out_shape,
        in_specs=[pl.BlockSpec(memory_space=s) for s in in_spaces],
        out_specs=specs if isinstance(out_shape, (list, tuple)) else specs[0],
        scratch_shapes=list(scratch),
        compiler_params=pltpu.CompilerParams(vmem_limit_bytes=limit),
        **kw,
    )


def nt(a, b):
    return lax.dot_general(a, b, (((1,), (1,)), ((), ())), preferred_element_type=F32)


def mm(a, b):
    return lax.dot_general(a, b, (((1,), (0,)), ((), ())), preferred_element_type=F32)


def prepare_kernel(kv, tables, keys, values, keys_wide, values_out, onehot):
    slots = keys.shape[0]
    tokens = onehot.shape[0]
    row = lax.broadcasted_iota(jnp.int32, (128, 128), 0)
    col = lax.broadcasted_iota(jnp.int32, (128, 128), 1)
    leaf = tables[:, :tokens]
    lengths = tables[:, tokens : tokens + 128]
    parents = tables[:, tokens + 128 :]

    def upright(lanes):
        return jnp.sum(jnp.where(row == col, lanes, 0), axis=1, keepdims=True)

    own_lo = jnp.sum(jnp.where(row < col, upright(lengths), 0), axis=0, keepdims=True)
    own_hi = own_lo + lengths
    up_lo = jnp.sum(jnp.where(row == parents, upright(own_lo), 0), axis=0, keepdims=True)
    up_hi = jnp.sum(jnp.where(row == parents, upright(own_hi), 0), axis=0, keepdims=True)
    root = own_hi[:, :1]
    slot = kv[0] * slots + lax.broadcasted_iota(jnp.int32, (slots, 128), 0)
    seen = (
        (slot < root)
        | ((slot >= own_lo) & (slot < own_hi))
        | ((slot >= up_lo) & (slot < up_hi))
    )
    keys_wide[:, :HEAD_WIDTH] = keys[...]
    keys_wide[:, HEAD_WIDTH:] = jnp.where(seen, 0.0, LOWEST).astype(BF)
    values_out[...] = values[...]
    node = lax.broadcasted_iota(jnp.int32, (128, tokens), 0)
    onehot[...] = jnp.where(node == leaf, 1.0, 0.0).astype(F32).T.astype(BF)


def attend_kernel(q, keys_wide, values, onehot, weight, out):
    tokens = q.shape[0]
    lane_t = lax.broadcasted_iota(jnp.int32, (tokens, 128), 1)
    stats = jnp.zeros((tokens, 128), F32)
    for g in range(GROUP):
        cols = pl.ds(g * HEAD_WIDTH, HEAD_WIDTH)
        q_wide = jnp.concatenate([q[:, cols], onehot[...]], axis=1)
        scores = nt(q_wide, keys_wide[...])
        top = jnp.max(scores, axis=1, keepdims=True).astype(BF).astype(F32)
        weights = jnp.exp((scores - top) * SCALE)
        mass = jnp.sum(weights, axis=1, keepdims=True)
        out[:, cols] = mm(weights.astype(BF), values[...]).astype(BF)
        high = mass.astype(BF).astype(F32)
        stats = jnp.where(lane_t == g, top, stats)
        stats = jnp.where(lane_t == GROUP + g, high, stats)
        stats = jnp.where(lane_t == 2 * GROUP + g, mass - high, stats)
    out[:, GROUP * HEAD_WIDTH :] = stats.astype(BF)


def project_kernel(tp, parts, weight, activations, own, other):
    z, core = tp[0] >> 1, tp[0] & 1
    sources = parts.shape[0]
    width = GROUP * HEAD_WIDTH
    stats = [parts[s, :, width:].astype(F32) for s in range(sources)]
    top = stats[0]
    for s in stats[1:]:
        top = jnp.maximum(top, s)
    scales = [jnp.exp((s - top) * SCALE) for s in stats]
    heads = []
    for g in range(GROUP):
        total = jnp.zeros((16, HEAD_WIDTH), F32)
        mass = jnp.zeros((16, 1), F32)
        for s in range(sources):
            scale = scales[s][:, g : g + 1]
            part = parts[s, :, g * HEAD_WIDTH : (g + 1) * HEAD_WIDTH].astype(F32)
            total = total + part * scale
            low = stats[s][:, GROUP + g : GROUP + g + 1] + stats[s][:, 2 * GROUP + g : 2 * GROUP + g + 1]
            mass = mass + low * scale
        heads.append((total / mass).astype(BF))
    context = jnp.concatenate(heads, axis=1)
    row = lax.broadcasted_iota(jnp.int32, (16, 16), 0)
    col = lax.broadcasted_iota(jnp.int32, (16, 16), 1)
    half = jnp.where(row < 8, core, 1 - core)
    source = (row % 8) // 2 * 4 + half * 2 + row % 2
    pick = jnp.where(col == source, 1.0, 0.0).astype(BF)
    context = mm(pick, context).astype(BF)
    result = mm(context, weight[...])
    row = lax.broadcasted_iota(jnp.int32, (8, 2), 0)
    col = lax.broadcasted_iota(jnp.int32, (8, 2), 1)
    place = jnp.where(row == z * 2 + col, 1.0, 0.0).astype(BF)
    own[...] = result[:8] + mm(place, activations[...])
    other[...] = result[8:].astype(BF)


def hidden_of(rows, gate, up):
    g = nt(rows, gate)
    u = nt(rows, up)
    return (g / (1.0 + jnp.exp(-g)) * u).astype(BF)


def ordered(hidden, kv, tp):
    n = hidden.shape[0]
    row = lax.broadcasted_iota(jnp.int32, (n, n), 0)
    col = lax.broadcasted_iota(jnp.int32, (n, n), 1)
    x, z, core = kv[0] >> 2, tp[0] >> 1, tp[0] & 1
    block = row // 32
    q = (row & 31) // 2
    places = jnp.where(block == 0, 0, jnp.where(block == 1, 2, jnp.where(block == 2, 1, 3)))
    along_z = q * 8 + ((z + places) & 3) * 2
    along_x = (((x + places) & 3) * 4 + q // 4) * 8 + (q & 3) * 2
    source = jnp.where(core == 0, along_z, along_x) + (row & 1)
    return mm(jnp.where(col == source, 1.0, 0.0).astype(BF), hidden).astype(BF)


def mlp_kernel(kv, tp, rows, gate, up, down, gate_far, up_far, down_far, own, *sent):
    near = ordered(hidden_of(rows[...], gate[...], up[...]), kv, tp)
    far = ordered(hidden_of(rows[...], gate_far[...], up_far[...]), kv, tp)
    result = mm(near, down[...]) + mm(far, down_far[...])
    own[...] = result[:32]
    for k, ref in enumerate(sent):
        ref[...] = result[32 * (k + 1) : 32 * (k + 2)].astype(BF)


def finish_kernel(tp, residual, parts, out):
    row = lax.broadcasted_iota(jnp.int32, (2, 8), 0)
    col = lax.broadcasted_iota(jnp.int32, (2, 8), 1)
    pick = jnp.where(col == (tp[0] >> 1) * 2 + row, 1.0, 0.0).astype(BF)
    total = mm(pick, residual[...])
    for k in range(parts.shape[0]):
        total = total + parts[k].astype(F32)
    out[...] = total.astype(BF)


def device(x, y, z, c):
    return (x * 4 + y) * 8 + z * 2 + c


def move_ring(value, k):
    pairs = [
        (device(x, y, z, c), device(x, y, (z + k) % 4, c) if c == 0 else device((x + k) % 4, y, z, c))
        for x in range(4)
        for y in range(4)
        for z in range(4)
        for c in range(2)
    ]
    return lax.ppermute(value, ("kv", "tp"), pairs)


PLANES = [[device(x, y, z, 0) for x in range(4) for y in range(4)] for z in range(4)] + [
    [device(x, y, z, 1) for y in range(4) for z in range(4)] for x in range(4)
]


def move_z(value, k):
    pairs = [(z * 2 + c, (z + k) % 4 * 2 + c) for z in range(4) for c in range(2)]
    return lax.ppermute(value, "tp", pairs)


def move_core(value):
    return lax.ppermute(value, "tp", [(i, i ^ 1) for i in range(8)])


def local(
    activations,
    queries,
    keys,
    values,
    parents,
    node_lengths,
    token_leaf,
    out_weight,
    norm_gain,
    gate_weight,
    up_weight,
    down_weight,
):
    kv = lax.axis_index("kv")[None]
    tp = lax.axis_index("tp")[None]
    gate_t, up_t = gate_weight.T, up_weight.T
    shape = jax.ShapeDtypeStruct
    far = [move_core(w) for w in (gate_t, up_t, down_weight)]
    queries, kv, tp = lax.optimization_barrier((queries, kv, tp))

    padding = 128 - node_lengths.shape[0]
    tables = jnp.concatenate([token_leaf, jnp.pad(node_lengths, (0, padding)), jnp.pad(parents, (0, padding))])[None, :]
    q = lax.all_to_all(jnp.broadcast_to(queries[None], (16, 16, 640)), "kv", 0, 0)
    keys_wide, values_in, onehot = call(
        prepare_kernel,
        [shape((keys.shape[0], 256), BF), shape(values.shape, BF), shape((256, 128), BF)],
        [SM, VM, VM, VM],
    )(kv, tables, keys, values)
    packed = call(attend_kernel, shape((256, 768), BF), [VM] * 4 + [pl.ANY], limit=48 << 20)(
        q.reshape(256, 640), keys_wide, values_in, onehot, out_weight
    )
    parts = lax.all_to_all(packed.reshape(16, 16, 768), "kv", 0, 0)
    own, other = call(project_kernel, [shape((8, D), F32), shape((8, D), BF)], [SM, VM, VM, VM])(
        tp, parts, out_weight, activations
    )
    attended = own + move_core(other).astype(F32)
    sent = attended.astype(BF)
    for part in [move_z(sent, k) for k in (1, 3, 2)]:
        attended = attended + part.astype(F32)
    residual = attended.astype(BF)
    widened = residual.astype(F32)
    normed = (
        widened
        * lax.rsqrt(jnp.mean(widened * widened, axis=1, keepdims=True) + EPSILON)
        * norm_gain
    ).astype(BF)

    rows = lax.all_to_all(jnp.broadcast_to(normed[None], (16, 8, D)), "kv", 0, 0).reshape(128, D)
    block = shape((32, D), BF)
    mixed, *sent = call(
        mlp_kernel, [shape((32, D), F32), block, block, block], [SM, SM] + [VM] * 7, limit=28 << 20
    )(kv, tp, rows, gate_t, up_t, down_weight, *far)
    for part in [move_ring(value, k) for value, k in zip(sent, (2, 1, 3))]:
        mixed = mixed + part.astype(F32)
    mixed = mixed.astype(BF).reshape(16, 2, D)
    mixed = lax.all_to_all(mixed, ("kv", "tp"), 0, 0, axis_index_groups=PLANES)
    return call(finish_kernel, shape((2, D), BF), [SM, VM, VM])(tp, residual, mixed)


def solution(mesh):
    return jax.shard_map(
        local,
        mesh=mesh,
        in_specs=(
            P(("kv", "tp"), None),
            P("kv", "tp"),
            P("kv", "tp"),
            P("kv", "tp"),
            P(),
            P(),
            P(),
            P("tp", None),
            P(),
            P(None, ("kv", "tp")),
            P(None, ("kv", "tp")),
            P(("kv", "tp"), None),
        ),
        out_specs=P(("kv", "tp"), None),
        check_vma=False,
    )
```

```python
import functools
import math

import jax
import jax.numpy as jnp
from jax import lax
from jax.experimental import pallas as pl
from jax.experimental.pallas import tpu as pltpu
from jax.sharding import PartitionSpec as P

QUERY_HEADS = 40
KEY_VALUE_HEADS = 8
HEAD_WIDTH = 128
GROUP = QUERY_HEADS // KEY_VALUE_HEADS
LOWEST = -(2.0**100)
SCALE = 1.0 / math.sqrt(HEAD_WIDTH)
EPSILON = 1e-06
BF = jnp.bfloat16
F32 = jnp.float32
D = 5120
VM = pltpu.VMEM
SM = pltpu.SMEM


def call(kernel, out_shape, in_spaces, scratch=(), limit=12 << 20, **kw):
    outs = out_shape if isinstance(out_shape, (list, tuple)) else [out_shape]
    specs = [pl.BlockSpec(memory_space=VM) for _ in outs]
    return pl.pallas_call(
        kernel,
        out_shape=out_shape,
        in_specs=[pl.BlockSpec(memory_space=s) for s in in_spaces],
        out_specs=specs if isinstance(out_shape, (list, tuple)) else specs[0],
        scratch_shapes=list(scratch),
        compiler_params=pltpu.CompilerParams(vmem_limit_bytes=limit),
        **kw,
    )


def nt(a, b):
    return lax.dot_general(a, b, (((1,), (1,)), ((), ())), preferred_element_type=F32)


def mm(a, b):
    return lax.dot_general(a, b, (((1,), (0,)), ((), ())), preferred_element_type=F32)


def prepare_kernel(kv, tables, keys, values, keys_wide, values_out, onehot):
    slots = keys.shape[0]
    tokens = onehot.shape[0]
    row = lax.broadcasted_iota(jnp.int32, (128, 128), 0)
    col = lax.broadcasted_iota(jnp.int32, (128, 128), 1)
    leaf = tables[:, :tokens]
    lengths = tables[:, tokens : tokens + 128]
    parents = tables[:, tokens + 128 :]

    def upright(lanes):
        return jnp.sum(jnp.where(row == col, lanes, 0), axis=1, keepdims=True)

    own_lo = jnp.sum(jnp.where(row < col, upright(lengths), 0), axis=0, keepdims=True)
    own_hi = own_lo + lengths
    up_lo = jnp.sum(jnp.where(row == parents, upright(own_lo), 0), axis=0, keepdims=True)
    up_hi = jnp.sum(jnp.where(row == parents, upright(own_hi), 0), axis=0, keepdims=True)
    root = own_hi[:, :1]
    slot = kv[0] * slots + lax.broadcasted_iota(jnp.int32, (slots, 128), 0)
    seen = (
        (slot < root)
        | ((slot >= own_lo) & (slot < own_hi))
        | ((slot >= up_lo) & (slot < up_hi))
    )
    keys_wide[:, :HEAD_WIDTH] = keys[...]
    keys_wide[:, HEAD_WIDTH:] = jnp.where(seen, 0.0, LOWEST).astype(BF)
    values_out[...] = values[...]
    node = lax.broadcasted_iota(jnp.int32, (128, tokens), 0)
    onehot[...] = jnp.where(node == leaf, 1.0, 0.0).astype(F32).T.astype(BF)


def attend_kernel(q, keys_wide, values, onehot, weight, out):
    tokens = q.shape[0]
    lane_t = lax.broadcasted_iota(jnp.int32, (tokens, 128), 1)
    stats = jnp.zeros((tokens, 128), F32)
    for g in range(GROUP):
        cols = pl.ds(g * HEAD_WIDTH, HEAD_WIDTH)
        q_wide = jnp.concatenate([q[:, cols], onehot[...]], axis=1)
        scores = nt(q_wide, keys_wide[...])
        top = jnp.max(scores, axis=1, keepdims=True).astype(BF).astype(F32)
        weights = jnp.exp((scores - top) * SCALE)
        mass = jnp.sum(weights, axis=1, keepdims=True)
        out[:, cols] = mm(weights.astype(BF), values[...]).astype(BF)
        high = mass.astype(BF).astype(F32)
        stats = jnp.where(lane_t == g, top, stats)
        stats = jnp.where(lane_t == GROUP + g, high, stats)
        stats = jnp.where(lane_t == 2 * GROUP + g, mass - high, stats)
    out[:, GROUP * HEAD_WIDTH :] = stats.astype(BF)


def project_kernel(tp, parts, weight, activations, own, other):
    z, core = tp[0] >> 1, tp[0] & 1
    sources = parts.shape[0]
    width = GROUP * HEAD_WIDTH
    stats = [parts[s, :, width:].astype(F32) for s in range(sources)]
    top = stats[0]
    for s in stats[1:]:
        top = jnp.maximum(top, s)
    scales = [jnp.exp((s - top) * SCALE) for s in stats]
    heads = []
    for g in range(GROUP):
        total = jnp.zeros((16, HEAD_WIDTH), F32)
        mass = jnp.zeros((16, 1), F32)
        for s in range(sources):
            scale = scales[s][:, g : g + 1]
            part = parts[s, :, g * HEAD_WIDTH : (g + 1) * HEAD_WIDTH].astype(F32)
            total = total + part * scale
            low = stats[s][:, GROUP + g : GROUP + g + 1] + stats[s][:, 2 * GROUP + g : 2 * GROUP + g + 1]
            mass = mass + low * scale
        heads.append((total / mass).astype(BF))
    context = jnp.concatenate(heads, axis=1)
    row = lax.broadcasted_iota(jnp.int32, (16, 16), 0)
    col = lax.broadcasted_iota(jnp.int32, (16, 16), 1)
    half = jnp.where(row < 8, core, 1 - core)
    source = (row % 8) // 2 * 4 + half * 2 + row % 2
    pick = jnp.where(col == source, 1.0, 0.0).astype(BF)
    context = mm(pick, context).astype(BF)
    result = mm(context, weight[...])
    row = lax.broadcasted_iota(jnp.int32, (8, 2), 0)
    col = lax.broadcasted_iota(jnp.int32, (8, 2), 1)
    place = jnp.where(row == z * 2 + col, 1.0, 0.0).astype(BF)
    own[...] = result[:8] + mm(place, activations[...])
    other[...] = result[8:].astype(BF)


def hidden_of(rows, gate, up):
    g = nt(rows, gate)
    u = nt(rows, up)
    return (g / (1.0 + jnp.exp(-g)) * u).astype(BF)


def ordered(hidden, kv, tp):
    n = hidden.shape[0]
    row = lax.broadcasted_iota(jnp.int32, (n, n), 0)
    col = lax.broadcasted_iota(jnp.int32, (n, n), 1)
    x, z, core = kv[0] >> 2, tp[0] >> 1, tp[0] & 1
    block = row // 32
    q = (row & 31) // 2
    places = jnp.where(block == 0, 0, jnp.where(block == 1, 2, jnp.where(block == 2, 1, 3)))
    along_z = q * 8 + ((z + places) & 3) * 2
    along_x = (((x + places) & 3) * 4 + q // 4) * 8 + (q & 3) * 2
    source = jnp.where(core == 0, along_z, along_x) + (row & 1)
    return mm(jnp.where(col == source, 1.0, 0.0).astype(BF), hidden).astype(BF)


def mlp_kernel(kv, tp, rows, gate, up, down, gate_far, up_far, down_far, own, *sent):
    near = ordered(hidden_of(rows[...], gate[...], up[...]), kv, tp)
    far = ordered(hidden_of(rows[...], gate_far[...], up_far[...]), kv, tp)
    result = mm(near, down[...]) + mm(far, down_far[...])
    own[...] = result[:32]
    for k, ref in enumerate(sent):
        ref[...] = result[32 * (k + 1) : 32 * (k + 2)].astype(BF)


def finish_kernel(tp, residual, parts, out):
    row = lax.broadcasted_iota(jnp.int32, (2, 8), 0)
    col = lax.broadcasted_iota(jnp.int32, (2, 8), 1)
    pick = jnp.where(col == (tp[0] >> 1) * 2 + row, 1.0, 0.0).astype(BF)
    total = mm(pick, residual[...])
    for k in range(parts.shape[0]):
        total = total + parts[k].astype(F32)
    out[...] = total.astype(BF)


def device(x, y, z, c):
    return (x * 4 + y) * 8 + z * 2 + c


def move_ring(value, k):
    pairs = [
        (device(x, y, z, c), device(x, y, (z + k) % 4, c) if c == 0 else device((x + k) % 4, y, z, c))
        for x in range(4)
        for y in range(4)
        for z in range(4)
        for c in range(2)
    ]
    return lax.ppermute(value, ("kv", "tp"), pairs)


PLANES = [[device(x, y, z, 0) for x in range(4) for y in range(4)] for z in range(4)] + [
    [device(x, y, z, 1) for y in range(4) for z in range(4)] for x in range(4)
]


def move_z(value, k):
    pairs = [(z * 2 + c, (z + k) % 4 * 2 + c) for z in range(4) for c in range(2)]
    return lax.ppermute(value, "tp", pairs)


def move_core(value):
    return lax.ppermute(value, "tp", [(i, i ^ 1) for i in range(8)])


def local(
    activations,
    queries,
    keys,
    values,
    parents,
    node_lengths,
    token_leaf,
    out_weight,
    norm_gain,
    gate_weight,
    up_weight,
    down_weight,
):
    kv = lax.axis_index("kv")[None]
    tp = lax.axis_index("tp")[None]
    gate_t, up_t = gate_weight.T, up_weight.T
    shape = jax.ShapeDtypeStruct
    far = [move_core(w) for w in (gate_t, up_t, down_weight)]
    queries, kv, tp = lax.optimization_barrier((queries, kv, tp))

    padding = 128 - node_lengths.shape[0]
    tables = jnp.concatenate([token_leaf, jnp.pad(node_lengths, (0, padding)), jnp.pad(parents, (0, padding))])[None, :]
    q = lax.all_to_all(jnp.broadcast_to(queries[None], (16, 16, 640)), "kv", 0, 0)
    keys_wide, values_in, onehot = call(
        prepare_kernel,
        [shape((keys.shape[0], 256), BF), shape(values.shape, BF), shape((256, 128), BF)],
        [SM, VM, VM, VM],
    )(kv, tables, keys, values)
    packed = call(attend_kernel, shape((256, 768), BF), [VM] * 4 + [pl.ANY], limit=48 << 20)(
        q.reshape(256, 640), keys_wide, values_in, onehot, out_weight
    )
    parts = lax.all_to_all(packed.reshape(16, 16, 768), "kv", 0, 0)
    own, other = call(project_kernel, [shape((8, D), F32), shape((8, D), BF)], [SM, VM, VM, VM])(
        tp, parts, out_weight, activations
    )
    attended = own + move_core(other).astype(F32)
    sent = attended.astype(BF)
    for part in [move_z(sent, k) for k in (1, 3, 2)]:
        attended = attended + part.astype(F32)
    residual = attended.astype(BF)
    widened = residual.astype(F32)
    normed = (
        widened
        * lax.rsqrt(jnp.mean(widened * widened, axis=1, keepdims=True) + EPSILON)
        * norm_gain
    ).astype(BF)

    rows = lax.all_to_all(jnp.broadcast_to(normed[None], (16, 8, D)), "kv", 0, 0).reshape(128, D)
    block = shape((32, D), BF)
    mixed, *sent = call(
        mlp_kernel, [shape((32, D), F32), block, block, block], [SM, SM] + [VM] * 7, limit=28 << 20
    )(kv, tp, rows, gate_t, up_t, down_weight, *far)
    for part in [move_ring(value, k) for value, k in ((sent[0], 2), (sent[2], 3), (sent[1], 1))]:
        mixed = mixed + part.astype(F32)
    mixed = mixed.astype(BF).reshape(16, 2, D)
    mixed = lax.all_to_all(mixed, ("kv", "tp"), 0, 0, axis_index_groups=PLANES)
    return call(finish_kernel, shape((2, D), BF), [SM, VM, VM])(tp, residual, mixed)


def solution(mesh):
    return jax.shard_map(
        local,
        mesh=mesh,
        in_specs=(
            P(("kv", "tp"), None),
            P("kv", "tp"),
            P("kv", "tp"),
            P("kv", "tp"),
            P(),
            P(),
            P(),
            P("tp", None),
            P(),
            P(None, ("kv", "tp")),
            P(None, ("kv", "tp")),
            P(("kv", "tp"), None),
        ),
        out_specs=P(("kv", "tp"), None),
        check_vma=False,
    )
```
